256 devices in a mesh: heads: 8 (over z), tokens: 32 (over x, y, core).
Axes of the slice: x: 4, y: 4, z: 8, core: 2. Of those that a mesh axis runs over, the one named last changes fastest.
Arguments:
- hidden_in: bfloat16 [8192, 5120], P('tokens', 'heads'), may hold values from -4 to 4
- queries: bfloat16 [8192, 5120], P('tokens', 'heads'), may hold values from -7 to 7
- keyvals: bfloat16 [8192, 2, 1024], P('tokens', None, 'heads'), may hold values from -6 to 6
- out_weight: bfloat16 [5120, 5120], P('heads', 'tokens'), may hold values from -0.01953125 to 0.01953125
- kv_gain: bfloat16 [5120], P('heads'), may hold values from 0.099609375 to 1.8984375
- kv_weight: bfloat16 [5120, 2, 1024], P(None, None, 'heads'), may hold values from -0.25 to 0.25
- cache: bfloat16 [131072, 2, 1024], P('tokens', None, 'heads'), may hold values from -12 to 12
- page_home: int32 [512], replicated, may hold values from 0 to 8191, as said below
- cache_len: int32 [1], replicated, may hold values from 16384 to 65536
- beam_state: bfloat16 [256, 5120], P(None, 'tokens'), may hold values from -4 to 4
- parents: int32 [256], replicated, may hold values from 0 to 255
- beam_gain: bfloat16 [2, 5120], P(None, 'tokens'), may hold values from 0.099609375 to 1.8984375
- query_weight: bfloat16 [2, 5120, 5120], P(None, 'tokens', 'heads'), may hold values from -1 to 1
- beam_out_weight: bfloat16 [2, 5120, 5120], P(None, 'heads', 'tokens'), may hold values from -0.078125 to 0.078125
Outputs:
- stretch_hidden: bfloat16 [8192, 5120], P('tokens', 'heads')
- new_cache: bfloat16 [131072, 2, 1024], P('tokens', None, 'heads')
- beams_out: bfloat16 [256, 5120], P(None, 'tokens')
The draws below stay inside these ranges and needn't reach their ends.
Inputs may be any that keep to these rules, and one draw needn't show every extreme that they name: Prefill page p overwrites a page held by index (p + c) mod 32 of tokens, i.e. page_home[p] // 256 equals it, for one c of each draw; all entries differ.
All inputs are finite; a program needn't handle non-finite values.
Results may differ from the reference program's by a relative error of at most 0.023.
Values may be sent and summed in bfloat16 or wider, within the bound.
A program may use at most 128 MiB of HBM per device.

```python
import jax
import jax.numpy as jnp
from jax import lax

D = 5120
HEADS = 40
KV = 8
DH = 128
WINDOW = 1024
PAGE = 16
LAYERS = 2
TOK_DEV = 256
CACHE_DEV = 4096
BEAMS = 256
STRETCH = 8192
CACHE = 131072
NEW_PAGES = 512
N_TOKENS = 32


def rising_rows(key, rows_total):
    first_key = jax.random.fold_in(key, 0)
    position = jnp.arange(D, dtype=jnp.float32) / D - 1.0
    column_scale = jnp.exp(position * jnp.log(30.0))
    base = jnp.clip(jax.random.normal(first_key, (rows_total, D), jnp.float32), -4.0, 4.0)
    return (base * column_scale[None, :]).astype(jnp.bfloat16)


def draw_hidden_in(key, part):
    return rising_rows(jax.random.fold_in(key, 3), STRETCH)


def draw_beam_state(key, part):
    rows = rising_rows(jax.random.fold_in(key, 5), BEAMS)
    return rows


def draw_query_weight(key, part):
    weight_key = jax.random.fold_in(key, 31)
    values = jnp.clip(jax.random.normal(weight_key, (LAYERS, D, HEADS * DH), jnp.float32), -6.0, 6.0) * D ** (-0.5)
    return values.astype(jnp.bfloat16)


def attention_inputs(key):
    base_key = jax.random.fold_in(key, 11)
    query_key, key_key, value_key = jax.random.split(base_key, 3)
    group_size = HEADS // KV
    query_vals = jnp.clip(1.5 * jax.random.normal(query_key, (STRETCH, KV, group_size, DH), jnp.float32), -6.0, 6.0)
    key_vals = jnp.clip(1.5 * jax.random.normal(key_key, (STRETCH, KV, DH), jnp.float32), -6.0, 6.0)
    value_vals = jnp.clip(jax.random.normal(value_key, (STRETCH, KV, DH), jnp.float32), -5.0, 5.0)
    query_out = query_vals.reshape(STRETCH, HEADS * DH).astype(jnp.bfloat16)
    kv_out = jnp.stack([key_vals.reshape(STRETCH, KV * DH), value_vals.reshape(STRETCH, KV * DH)], axis=1).astype(jnp.bfloat16)
    return (query_out, kv_out)


def draw_queries(key, part):
    return attention_inputs(key)[0]


def draw_keyvals(key, part):
    return attention_inputs(key)[1]


def draw_cache(key, part):
    key_key, value_key = jax.random.split(jax.random.fold_in(key, 17), 2)
    key_vals = jnp.clip(3.0 * jax.random.normal(key_key, (CACHE, KV * DH), jnp.float32), -12.0, 12.0)
    value_vals = jnp.clip(jax.random.normal(value_key, (CACHE, KV * DH), jnp.float32), -5.0, 5.0)
    return jnp.stack([key_vals, value_vals], axis=1).astype(jnp.bfloat16)


def draw_page_home(key, part):
    shift_key, slot_key = jax.random.split(jax.random.fold_in(key, 23))
    pages_here = CACHE_DEV // PAGE
    offset = jax.random.randint(shift_key, (), 0, N_TOKENS)
    every_page = jnp.arange(NEW_PAGES, dtype=jnp.int32)
    target = (every_page + offset) % N_TOKENS
    arrival = every_page // N_TOKENS
    orders = jax.vmap(lambda one_key: jax.random.permutation(one_key, pages_here))(jax.random.split(slot_key, N_TOKENS))
    return (target * pages_here + orders[target, arrival]).astype(jnp.int32)


def place_ends(drawn, own_key, low, largest):
    longest = drawn.shape.index(max(drawn.shape))
    spots = []
    for shift in (0, 1):
        where = [jax.random.randint(jax.random.fold_in(own_key, axis), (), 0, length) for axis, length in enumerate(drawn.shape)]
        where[longest] = (where[longest] + shift) % drawn.shape[longest]
        spots.append(tuple(where))
    return drawn.at[spots[0]].set(low).at[spots[1]].set(largest)


def shard_levels(key, dims, cuts, least, largest):
    level = 1.0
    for axis_at, parts in cuts:
        draws = jax.random.uniform(jax.random.fold_in(jax.random.fold_in(key, 6), axis_at), (parts,), jnp.float32, least / len(cuts), largest / len(cuts))
        level = level * jnp.repeat(jnp.exp(draws), dims[axis_at] // parts).reshape((-1,) + (1,) * (len(dims) - 1 - axis_at))
    return level


def scatter_about(key, shape, deviation, bound, pieces=(), held_as=jnp.bfloat16):
    level = shard_levels(key, shape, pieces, -0.22, 0.18) if pieces else 1.0
    drawn = jax.random.normal(key, shape, jnp.float32) * deviation * level
    return jnp.minimum(jnp.maximum(drawn, -bound), bound).astype(held_as)


def setup_inputs(seed: int = 0) -> dict:
    keys = jax.random.split(jax.random.key(seed), 15)
    return {
        "hidden_in": draw_hidden_in(jax.random.fold_in(keys[14], 71), 0),
        "queries": draw_queries(jax.random.fold_in(keys[14], 71), 0),
        "keyvals": draw_keyvals(jax.random.fold_in(keys[14], 71), 0),
        "out_weight": scatter_about(keys[3], (HEADS * DH, D), (16 * HEADS * DH) ** -0.5, 0.01953125, ((0, 8), (1, 32))),
        "kv_gain": jnp.clip(1.0 + 0.18 * jax.random.normal(keys[4], (D,), jnp.float32), 0.099609375, 1.8984375).astype(jnp.bfloat16),
        "kv_weight": scatter_about(keys[5], (D, 2, KV * DH), (D // 9) ** -0.5, 0.25, ((2, 8),)),
        "cache": draw_cache(jax.random.fold_in(keys[14], 71), 0),
        "page_home": draw_page_home(jax.random.fold_in(keys[14], 71), 0),
        "cache_len": jax.random.randint(keys[8], (1,), CACHE // 8, CACHE // 2 + 1).astype(jnp.int32),
        "beam_state": draw_beam_state(jax.random.fold_in(keys[14], 71), 0),
        "parents": place_ends(jax.random.randint(keys[10], (BEAMS,), 0, BEAMS), jax.random.fold_in(keys[10], 1), 0, BEAMS - 1).astype(jnp.int32),
        "beam_gain": jnp.clip(1.0 + 0.18 * jax.random.normal(keys[11], (LAYERS, D), jnp.float32), 0.099609375, 1.8984375).astype(jnp.bfloat16),
        "query_weight": draw_query_weight(jax.random.fold_in(keys[14], 71), 0),
        "beam_out_weight": scatter_about(keys[13], (LAYERS, HEADS * DH, D), (HEADS * DH) ** -0.5, 0.078125, ((1, 8), (2, 32))),
    }


epsilon = 1e-06

def row_norm(values, gain):
    values_f = values.astype(jnp.float32)
    squares = lax.optimization_barrier(jnp.mean(values_f * values_f, axis=1, keepdims=True))
    return (values_f * lax.rsqrt(squares + epsilon) * gain.astype(jnp.float32)[None, :]).astype(jnp.bfloat16)

def reference(hidden_in, queries, keyvals, out_weight, kv_gain, kv_weight, cache, page_home, cache_len, beam_state, parents, beam_gain, query_weight, beam_out_weight):
    group_size = HEADS // KV
    score_scale = DH ** (-0.5)
    padded = jnp.concatenate([jnp.zeros((WINDOW, 2, KV * DH), jnp.bfloat16), keyvals], axis=0)

    def window_block(block_index):
        start_row = (block_index * TOK_DEV).astype(jnp.int32)
        query_block = lax.dynamic_slice_in_dim(queries, start_row, TOK_DEV, 0).reshape(TOK_DEV, KV, group_size, DH)
        key_rows = lax.dynamic_slice_in_dim(padded, start_row, TOK_DEV + WINDOW, 0)
        key_block = key_rows[:, 0].reshape(-1, KV, DH)
        value_block = key_rows[:, 1].reshape(-1, KV, DH)
        scores = jnp.einsum('tkgd,skd->kgts', query_block.astype(jnp.float32), key_block.astype(jnp.float32)) * score_scale
        query_pos = start_row + jnp.arange(TOK_DEV, dtype=jnp.int32)
        key_pos = start_row - WINDOW + jnp.arange(TOK_DEV + WINDOW, dtype=jnp.int32)
        allowed = (key_pos[None, :] <= query_pos[:, None]) & (key_pos[None, :] > query_pos[:, None] - WINDOW) & (key_pos[None, :] >= 0)
        scores = jnp.where(allowed, scores, -1e+30)
        highest = lax.optimization_barrier(jnp.max(scores, axis=-1, keepdims=True))
        expo = jnp.exp(scores - highest)
        weights = (expo / lax.optimization_barrier(jnp.sum(expo, axis=-1, keepdims=True))).astype(jnp.bfloat16)
        mixed = jnp.einsum('kgts,skd->tkgd', weights.astype(jnp.float32), value_block.astype(jnp.float32))
        return mixed.astype(jnp.bfloat16).reshape(TOK_DEV, HEADS * DH)
    attended = lax.map(window_block, jnp.arange(N_TOKENS, dtype=jnp.int32)).reshape(STRETCH, HEADS * DH)
    projected = jnp.dot(attended, out_weight, preferred_element_type=jnp.float32)
    stretch_hidden = (hidden_in.astype(jnp.float32) + projected).astype(jnp.bfloat16)
    kv_normed = row_norm(stretch_hidden, kv_gain)
    fresh = jnp.dot(kv_normed, kv_weight.reshape(D, 2 * KV * DH), preferred_element_type=jnp.float32).astype(jnp.bfloat16)
    page_count = CACHE // PAGE
    pages_new = fresh.reshape(NEW_PAGES, PAGE, 2, KV * DH)
    cache_pages = cache.reshape(page_count, PAGE, 2, KV * DH).at[page_home].set(pages_new)
    new_cache = cache_pages.reshape(CACHE, 2, KV * DH)
    written_page = jnp.zeros((page_count,), jnp.bool_).at[page_home].set(True)
    live_rows = (jnp.arange(CACHE, dtype=jnp.int32) < cache_len[0]) | jnp.repeat(written_page, PAGE)
    keys_all = new_cache[:, 0].reshape(CACHE, KV, DH).transpose(1, 0, 2)
    values_all = new_cache[:, 1].reshape(CACHE, KV, DH).transpose(1, 0, 2)
    state = jnp.take(beam_state, parents, axis=0)
    for layer_index in range(LAYERS):
        normed = row_norm(state, beam_gain[layer_index])
        query_rows = jnp.dot(normed, query_weight[layer_index], preferred_element_type=jnp.float32).astype(jnp.bfloat16)
        query_heads = query_rows.reshape(BEAMS, HEADS, DH).transpose(1, 0, 2)

        def head_attend(head_index):
            kv_index = head_index // group_size
            query_one = lax.dynamic_index_in_dim(query_heads, head_index, 0, keepdims=False)
            key_one = lax.dynamic_index_in_dim(keys_all, kv_index, 0, keepdims=False)
            value_one = lax.dynamic_index_in_dim(values_all, kv_index, 0, keepdims=False)
            scores = jnp.dot(query_one, key_one.T, preferred_element_type=jnp.float32) * score_scale
            scores = jnp.where(live_rows[None, :], scores, -1e+30)
            highest = lax.optimization_barrier(jnp.max(scores, axis=-1, keepdims=True))
            expo = jnp.exp(scores - highest)
            total = lax.optimization_barrier(jnp.sum(expo, axis=-1, keepdims=True))
            summed = jnp.dot(expo.astype(jnp.bfloat16), value_one, preferred_element_type=jnp.float32)
            return (summed / total).astype(jnp.bfloat16)
        cross_out = lax.map(head_attend, jnp.arange(HEADS, dtype=jnp.int32)).transpose(1, 0, 2).reshape(BEAMS, HEADS * DH)
        branch = jnp.dot(cross_out, beam_out_weight[layer_index], preferred_element_type=jnp.float32)
        state = (state.astype(jnp.float32) + branch).astype(jnp.bfloat16)
    return (stretch_hidden, new_cache, state)
```

```python
import functools
import math

import jax
import jax.numpy as jnp
from jax import lax
from jax.experimental import pallas as pl
from jax.experimental.pallas import tpu as pltpu
from jax.sharding import PartitionSpec as P

D = 5120
DH = 128
WINDOW = 1024
PAGE = 16
LAYERS = 2
EPSILON = 1e-06
SCALE = DH ** (-0.5)
SCALE2 = SCALE * math.log2(math.e)
MESH = pl.DeviceIdType.MESH
VMEM_SPEC = pl.BlockSpec(memory_space=pltpu.VMEM)


def scatter_start(send, recv, sems, axis, count, me):
    def one(step, carry):
        peer = lax.rem(me + step, count)
        pltpu.make_async_remote_copy(
            src_ref=send.at[peer],
            dst_ref=recv.at[me],
            send_sem=sems.at[0],
            recv_sem=sems.at[1],
            device_id={axis: peer},
            device_id_type=MESH,
        ).start()
        return carry

    lax.fori_loop(1, count, one, 0)


def gather_start(held, sems, axis, count, me):
    def one(step, carry):
        peer = lax.rem(me + step, count)
        pltpu.make_async_remote_copy(
            src_ref=held.at[me],
            dst_ref=held.at[me],
            send_sem=sems.at[0],
            recv_sem=sems.at[1],
            device_id={axis: peer},
            device_id_type=MESH,
        ).start()
        return carry

    lax.fori_loop(1, count, one, 0)


def finish(held, sems, axis, count, me):
    everything = held.at[pl.ds(0, count - 1)]
    pltpu.make_async_remote_copy(
        src_ref=everything,
        dst_ref=everything,
        send_sem=sems.at[0],
        recv_sem=sems.at[1],
        device_id={axis: lax.rem(me + 1, count)},
        device_id_type=MESH,
    ).wait()


def greet(axis, count, me):
    barrier = pltpu.get_barrier_semaphore()

    def one(step, carry):
        pl.semaphore_signal(
            barrier, inc=1, device_id={axis: lax.rem(me + step, count)}, device_id_type=MESH
        )
        return carry

    lax.fori_loop(1, count, one, 0)


def beam_kernel(do_out, do_query, do_pages, n_tok, n_head, *refs):
    refs = list(refs)
    take = lambda k: [refs.pop(0) for _ in range(k)]
    if do_out:
        o_ref, lse_ref, wo_ref = take(3)
    (state_ref,) = take(1)
    if do_query:
        gain_ref, wq_ref = take(2)
    if do_pages:
        (outbox_ref,) = take(1)
    if do_out:
        (state_out_ref,) = take(1)
    if do_query:
        (q_out_ref,) = take(1)
    if do_pages:
        (inbox_out_ref,) = take(1)
    if do_out:
        o_recv, lse_recv, o_held, b_send, b_recv, s_held = take(6)
    if do_query:
        q_send, q_recv, q_held = take(3)
    if do_pages:
        (inbox,) = take(1)
    (sems,) = take(1)

    me_t = lax.axis_index("tokens")
    me_h = lax.axis_index("heads")
    tok = ("tokens", n_tok, me_t)
    head = ("heads", n_head, me_h)
    greet(*tok)
    peers = n_tok - 1
    if do_out:
        greet(*head)
        peers += n_head - 1
    pl.semaphore_wait(pltpu.get_barrier_semaphore(), peers)

    if do_out:
        scatter_start(o_ref, o_recv, sems.at[0], *tok)
        scatter_start(lse_ref, lse_recv, sems.at[1], *tok)
    if do_pages:
        scatter_start(outbox_ref, inbox, sems.at[2], *tok)
        inbox[me_t] = outbox_ref[me_t]
    if do_out:
        o_recv[me_t] = o_ref[me_t]
        lse_recv[me_t] = lse_ref[me_t]
        finish(lse_recv, sems.at[1], *tok)
        lse = lse_recv[...]
        weight = jnp.exp2(lse - jnp.max(lse, axis=0, keepdims=True))
        share = weight / jnp.sum(weight, axis=0, keepdims=True)
        finish(o_recv, sems.at[0], *tok)
        for g in range(o_ref.shape[2] // DH):
            cols = slice(g * DH, (g + 1) * DH)
            mixed = jnp.sum(o_recv[:, :, cols].astype(jnp.float32) * share[:, :, g : g + 1], axis=0)
            o_held[me_t, :, cols] = mixed.astype(jnp.bfloat16)
        gather_start(o_held, sems.at[3], *tok)
        finish(o_held, sems.at[3], *tok)
        width = o_ref.shape[2]
        whole = o_held[...].astype(jnp.float32).reshape(-1, width).astype(jnp.bfloat16)
        branch = jnp.dot(whole, wo_ref[...], preferred_element_type=jnp.float32)
        b_send[...] = branch.reshape(b_send.shape).astype(jnp.bfloat16)
        scatter_start(b_send, b_recv, sems.at[4], *head)
        b_recv[me_h] = b_send[me_h]
        finish(b_recv, sems.at[4], *head)
        total = jnp.sum(b_recv[...].astype(jnp.float32), axis=0)
        s_held[me_h] = (state_ref[me_h].astype(jnp.float32) + total).astype(jnp.bfloat16)
        gather_start(s_held, sems.at[5], *head)
        finish(s_held, sems.at[5], *head)
        state_out_ref[...] = s_held[...]
        state = s_held[...]
    else:
        state = state_ref[...]
    if do_query:
        state = state.astype(jnp.float32).reshape(-1, state.shape[2])
        squares = jnp.sum(state * state, axis=1, keepdims=True)
        scaled = (state * gain_ref[...].astype(jnp.float32)).astype(jnp.bfloat16)
        part = jnp.dot(scaled, wq_ref[...], preferred_element_type=jnp.float32)
        width = part.shape[1]
        rows = part.shape[0] // n_tok
        q_send[:, :, :width] = part.reshape(n_tok, rows, width).astype(jnp.bfloat16)
        q_send[:, :, width:] = (
            jnp.broadcast_to(squares, (part.shape[0], DH))
            .reshape(n_tok, rows, DH)
            .astype(jnp.bfloat16)
        )
        scatter_start(q_send, q_recv, sems.at[6], *tok)
        q_recv[me_t] = q_send[me_t]
        finish(q_recv, sems.at[6], *tok)
        total = jnp.sum(q_recv[...].astype(jnp.float32), axis=0)
        factor = lax.rsqrt(total[:, width : width + 1] / D + EPSILON)
        q_held[me_t] = (total[:, :width] * factor).astype(jnp.bfloat16)
        gather_start(q_held, sems.at[7], *tok)
        finish(q_held, sems.at[7], *tok)
        q_out_ref[...] = q_held[...].astype(jnp.float32).reshape(-1, width).astype(jnp.bfloat16)
    if do_pages:
        finish(inbox, sems.at[2], *tok)
        inbox_out_ref[...] = inbox[...]


def beam_step(n_tok, n_head, collective_id, state, out=None, query=None, pages=None):
    do_out, do_query, do_pages = (out is not None, query is not None, pages is not None)
    beams, cols = state.shape
    state3 = state.reshape(n_head, beams // n_head, cols)
    bf16 = jnp.bfloat16
    args, out_shape, scratch = [], [], []
    if do_out:
        o, lse, wo = out
        width = o.shape[1]
        args += [o.reshape(n_tok, -1, width), lse.reshape(n_tok, -1, DH), wo]
        out_shape += [jax.ShapeDtypeStruct(state3.shape, bf16)]
        rows = beams // n_tok
        scratch += [
            pltpu.VMEM((n_tok, rows, width), bf16),
            pltpu.VMEM((n_tok, rows, DH), jnp.float32),
            pltpu.VMEM((n_tok, rows, width), bf16),
            pltpu.VMEM(state3.shape, bf16),
            pltpu.VMEM(state3.shape, bf16),
            pltpu.VMEM(state3.shape, bf16),
        ]
    args += [state3]
    if do_query:
        gain, wq = query
        args += [gain, wq]
        width = wq.shape[1]
        out_shape += [jax.ShapeDtypeStruct((beams, width), bf16)]
        rows = beams // n_tok
        scratch += [
            pltpu.VMEM((n_tok, rows, width + DH), bf16),
            pltpu.VMEM((n_tok, rows, width + DH), bf16),
            pltpu.VMEM((n_tok, rows, width), bf16),
        ]
    if do_pages:
        args += [pages]
        out_shape += [jax.ShapeDtypeStruct(pages.shape, bf16)]
        scratch += [pltpu.VMEM(pages.shape, bf16)]
    scratch += [pltpu.SemaphoreType.DMA((8, 2))]
    res = pl.pallas_call(
        functools.partial(beam_kernel, do_out, do_query, do_pages, n_tok, n_head),
        out_shape=out_shape,
        in_specs=[VMEM_SPEC] * len(args),
        out_specs=[VMEM_SPEC] * len(out_shape),
        scratch_shapes=scratch,
        compiler_params=pltpu.CompilerParams(
            collective_id=collective_id, has_side_effects=True, vmem_limit_bytes=32 << 20
        ),
        name=f"beam_step_{collective_id}",
    )(*args)
    res = list(res)
    if do_out:
        res[0] = res[0].reshape(beams, cols)
    return res


def attend_kernel(blocks, block, has_fresh, has_carry, last, *refs):
    refs = list(refs)
    q_ref = refs.pop(0)
    if blocks:
        k_ref, v_ref, bias_ref = [refs.pop(0) for _ in range(3)]
    if has_fresh:
        kf_ref, vf_ref = [refs.pop(0) for _ in range(2)]
    if has_carry:
        acc_in_ref, top_in_ref = [refs.pop(0) for _ in range(2)]
    if last:
        o_ref, lse_ref, acc, top = refs
    else:
        acc, top = refs
    g = pl.program_id(0)
    q = q_ref[...]
    rows = q.shape[0]
    if has_carry:
        acc[...] = acc_in_ref[...]
        top[...] = top_in_ref[...]
    else:
        acc[...] = jnp.zeros(acc.shape, jnp.float32)
        top[...] = jnp.full(top.shape, -1e30, jnp.float32)

    def step(keys, values, bias):
        s = lax.dot_general(
            q, keys, (((1,), (1,)), ((), ())), preferred_element_type=jnp.float32
        )
        if bias is not None:
            s = s + bias
        before = top[...]
        here = jnp.maximum(before, jnp.max(s, axis=1, keepdims=True))
        p = jnp.exp2((s - here[:, :1]) * SCALE2).astype(jnp.bfloat16)
        shrink = jnp.exp2((before - here) * SCALE2)
        top[...] = here
        pv = jnp.dot(p, values, preferred_element_type=jnp.float32)
        acc[...] = acc[...] * jnp.concatenate([shrink, shrink], axis=1) + pv

    if blocks:

        def body(b, carry):
            at = pl.ds(pl.multiple_of(b * block, block), block)
            step(k_ref[at, :], v_ref[at, :], bias_ref[:, at])
            return carry

        lax.fori_loop(0, blocks, body, 0)
    if has_fresh:
        step(kf_ref[...], vf_ref[...], None)
    if last:
        amount = acc[:, DH:]
        o_ref[...] = (acc[:, :DH] / amount).astype(jnp.bfloat16)
        lane = lax.broadcasted_iota(jnp.int32, (rows, DH), 1)
        value = top[...] * SCALE2 + jnp.log2(amount)
        kept = jnp.where(g == 0, jnp.zeros_like(value), lse_ref[...])
        lse_ref[...] = jnp.where(lane == g, value, kept)


def attend(q, old=None, fresh=None, carry=None, block=1024):
    beams, width = q.shape
    groups = width // DH
    args, specs = [q], [pl.BlockSpec((beams, DH), lambda g: (0, g))]
    whole = lambda a: pl.BlockSpec(a.shape, lambda g: (0,) * a.ndim)
    blocks = 0
    for extra in (old, fresh):
        if extra is not None:
            args += list(extra)
            specs += [whole(a) for a in extra]
    if old is not None:
        blocks = old[0].shape[0] // block
    last = fresh is not None
    acc_spec = pl.BlockSpec((beams, 2 * DH), lambda g: (0, g))
    top_spec = pl.BlockSpec((beams, DH), lambda g: (0, g))
    if carry is not None:
        args += list(carry)
        specs += [acc_spec, top_spec]
    if last:
        out_shape = [
            jax.ShapeDtypeStruct((beams, width), jnp.bfloat16),
            jax.ShapeDtypeStruct((beams, DH), jnp.float32),
        ]
        out_specs = [
            pl.BlockSpec((beams, DH), lambda g: (0, g)),
            pl.BlockSpec((beams, DH), lambda g: (0, 0)),
        ]
        scratch = [
            pltpu.VMEM((beams, 2 * DH), jnp.float32),
            pltpu.VMEM((beams, DH), jnp.float32),
        ]
    else:
        out_shape = [
            jax.ShapeDtypeStruct((beams, 2 * width), jnp.float32),
            jax.ShapeDtypeStruct((beams, width), jnp.float32),
        ]
        out_specs = [acc_spec, top_spec]
        scratch = []
    rows = sum(a[0].shape[0] for a in (old, fresh) if a is not None)
    return pl.pallas_call(
        functools.partial(
            attend_kernel, blocks, block, fresh is not None, carry is not None, last
        ),
        grid=(groups,),
        out_shape=out_shape,
        in_specs=specs,
        out_specs=out_specs,
        scratch_shapes=scratch,
        compiler_params=pltpu.CompilerParams(vmem_limit_bytes=40 << 20),
        cost_estimate=pl.CostEstimate(
            flops=4 * beams * width * rows,
            bytes_accessed=rows * 3 * DH * 2,
            transcendentals=beams * groups * rows,
        ),
        name=f"attend_{blocks}_{int(last)}",
    )(*args)


def place_kernel(page_rows, slots, row_ref, cache_ref, inbox_ref, out_ref, sem):
    def copy(slot):
        return pltpu.make_async_copy(
            inbox_ref.at[slot], out_ref.at[pl.ds(row_ref[slot] * page_rows, page_rows)], sem
        )

    def start(slot, carry):
        @pl.when(row_ref[slot] >= 0)
        def _():
            copy(slot).start()

        return carry

    def wait(slot, carry):
        @pl.when(row_ref[slot] >= 0)
        def _():
            copy(slot).wait()

        return carry

    lax.fori_loop(0, slots, start, 0)
    lax.fori_loop(0, slots, wait, 0)


def place_pages(rows, cache, inbox):
    return pl.pallas_call(
        functools.partial(place_kernel, PAGE, inbox.shape[0]),
        out_shape=jax.ShapeDtypeStruct(cache.shape, cache.dtype),
        in_specs=[
            pl.BlockSpec(memory_space=pltpu.SMEM),
            pl.BlockSpec(memory_space=pl.ANY),
            pl.BlockSpec(memory_space=pl.ANY),
        ],
        out_specs=pl.BlockSpec(memory_space=pl.ANY),
        scratch_shapes=[pltpu.SemaphoreType.DMA],
        input_output_aliases={1: 0},
        name="place_pages",
    )(rows, cache, inbox)


def shards(
    hidden_in,
    queries,
    keyvals,
    out_weight,
    kv_gain,
    kv_weight,
    cache,
    page_home,
    cache_len,
    beam_state,
    parents,
    beam_gain,
    query_weight,
    beam_out_weight,
):
    n_tok = lax.axis_size("tokens")
    n_head = lax.axis_size("heads")
    tok_rows = hidden_in.shape[0]
    head_local = queries.shape[1] // DH
    me = lax.axis_index("tokens")
    reach_back = -(-WINDOW // tok_rows)

    state = jnp.take(beam_state, parents, axis=0)
    (q,) = beam_step(n_tok, n_head, 1, state, query=(beam_gain[0:1], query_weight[0]))

    cache_rows = cache.shape[0]
    pages_here = cache_rows // PAGE
    local_page = jnp.where(page_home // pages_here == me, page_home % pages_here, -1)
    page_ids = jnp.arange(pages_here, dtype=jnp.int32)
    written = jnp.any(page_ids[:, None] == local_page[None, :], axis=1)
    row_ids = me * cache_rows + jnp.arange(cache_rows, dtype=jnp.int32)
    kept = (row_ids < cache_len[0]) & ~jnp.repeat(written, PAGE)
    bias = jnp.where(kept, 0.0, -1e30).astype(jnp.float32)[None, :]
    old_keys = cache[:, 0]
    old_values = jnp.concatenate([cache[:, 1], jnp.ones_like(old_keys)], axis=1)
    old = (old_keys, old_values, bias)
    carry = attend(q, old=old)

    blocks = [keyvals]
    for back in range(1, reach_back + 1):
        pairs = [(s, s + back) for s in range(n_tok - back)]
        blocks.insert(0, lax.ppermute(keyvals, "tokens", pairs))
    window_rows = jnp.concatenate(blocks, axis=0)
    query_block = queries.reshape(tok_rows, head_local, DH)
    scores = (
        jnp.einsum(
            "tgd,sd->gts", query_block, window_rows[:, 0], preferred_element_type=jnp.float32
        )
        * SCALE
    )
    query_pos = me * tok_rows + jnp.arange(tok_rows, dtype=jnp.int32)
    key_pos = (me - reach_back) * tok_rows + jnp.arange(window_rows.shape[0], dtype=jnp.int32)
    allowed = (
        (key_pos[None, :] <= query_pos[:, None])
        & (key_pos[None, :] > query_pos[:, None] - WINDOW)
        & (key_pos[None, :] >= 0)
    )
    scores = jnp.where(allowed, scores, -1e30)
    expo = jnp.exp(scores - jnp.max(scores, axis=-1, keepdims=True))
    weights = (expo / jnp.sum(expo, axis=-1, keepdims=True)).astype(jnp.bfloat16)
    attended = jnp.einsum(
        "gts,sd->tgd", weights, window_rows[:, 1], preferred_element_type=jnp.float32
    )
    attended = attended.astype(jnp.bfloat16).reshape(tok_rows, head_local * DH)

    partial_out = jnp.dot(
        attended,
        lax.all_gather(out_weight, "tokens", axis=1, tiled=True),
        preferred_element_type=jnp.float32,
    ).astype(jnp.bfloat16)
    head_total = lax.psum_scatter(partial_out, "heads", scatter_dimension=1, tiled=True)
    stretch_hidden = (
        hidden_in.astype(jnp.float32) + head_total.astype(jnp.float32)
    ).astype(jnp.bfloat16)
    both = jnp.concatenate([stretch_hidden, jnp.tile(kv_gain[None, :], (16, 1))], axis=0)
    both = lax.all_gather(both, "heads", axis=1, tiled=True)
    hidden_f = both[:tok_rows].astype(jnp.float32)
    gain_f = both[tok_rows].astype(jnp.float32)
    factor = lax.rsqrt(jnp.mean(hidden_f * hidden_f, axis=1) + EPSILON)
    full_rows = (hidden_f * factor[:, None] * gain_f).astype(jnp.bfloat16)
    fresh = jnp.dot(
        full_rows, kv_weight.reshape(kv_weight.shape[0], -1), preferred_element_type=jnp.float32
    ).astype(jnp.bfloat16)

    own_pages = tok_rows // PAGE
    pages = fresh.reshape(own_pages, PAGE, -1)
    shift = page_home[0] // pages_here
    empty = jnp.zeros((n_tok - own_pages, *pages.shape[1:]), pages.dtype)
    ring = jnp.concatenate([pages, empty, pages, empty], axis=0)
    begin = (2 * n_tok * own_pages - shift - own_pages * me) % n_tok
    outbox = lax.dynamic_slice_in_dim(ring, begin, n_tok, 0)
    source = jnp.arange(n_tok, dtype=jnp.int32)
    which = (me - shift - own_pages * source + 2 * n_tok * own_pages) % n_tok
    landing = jnp.where(
        which < own_pages,
        jnp.take(page_home, jnp.minimum(own_pages * source + which, page_home.shape[0] - 1))
        % pages_here,
        -1,
    )

    fresh_keys = fresh[:, :DH]
    fresh_values = jnp.concatenate([fresh[:, DH:], jnp.ones_like(fresh_keys)], axis=1)
    new = (fresh_keys, fresh_values)
    o, lse = attend(q, fresh=new, carry=carry)
    state, q, inbox = beam_step(
        n_tok,
        n_head,
        2,
        state,
        out=(o, lse, beam_out_weight[0]),
        query=(beam_gain[1:2], query_weight[1]),
        pages=outbox,
    )
    new_cache = place_pages(landing, cache, inbox.reshape(n_tok, PAGE, *cache.shape[1:]))
    o, lse = attend(q, old=old, fresh=new)
    (state,) = beam_step(n_tok, n_head, 3, state, out=(o, lse, beam_out_weight[1]))
    return (stretch_hidden, new_cache, state)


def solution(mesh):
    tokens = "tokens"
    placed = (
        P(tokens, "heads"),
        P(tokens, "heads"),
        P(tokens, None, "heads"),
        P("heads", tokens),
        P("heads"),
        P(None, None, "heads"),
        P(tokens, None, "heads"),
        P(),
        P(),
        P(None, tokens),
        P(),
        P(None, tokens),
        P(None, tokens, "heads"),
        P(None, "heads", tokens),
    )
    return jax.shard_map(
        shards,
        mesh=mesh,
        in_specs=placed,
        out_specs=(P(tokens, "heads"), P(tokens, None, "heads"), P(None, tokens)),
        check_vma=False,
    )
```

```python
import functools
import math

import jax
import jax.numpy as jnp
from jax import lax
from jax.experimental import pallas as pl
from jax.experimental.pallas import tpu as pltpu
from jax.sharding import PartitionSpec as P

D = 5120
DH = 128
WINDOW = 1024
PAGE = 16
LAYERS = 2
EPSILON = 1e-06
SCALE = DH ** (-0.5)
SCALE2 = SCALE * math.log2(math.e)
MESH = pl.DeviceIdType.MESH
VMEM_SPEC = pl.BlockSpec(memory_space=pltpu.VMEM)


def scatter_start(send, recv, sems, axis, count, me):
    def one(step, carry):
        peer = lax.rem(me + step, count)
        pltpu.make_async_remote_copy(
            src_ref=send.at[peer],
            dst_ref=recv.at[me],
            send_sem=sems.at[0],
            recv_sem=sems.at[1],
            device_id={axis: peer},
            device_id_type=MESH,
        ).start()
        return carry

    lax.fori_loop(1, count, one, 0)


def gather_start(held, sems, axis, count, me):
    def one(step, carry):
        peer = lax.rem(me + step, count)
        pltpu.make_async_remote_copy(
            src_ref=held.at[me],
            dst_ref=held.at[me],
            send_sem=sems.at[0],
            recv_sem=sems.at[1],
            device_id={axis: peer},
            device_id_type=MESH,
        ).start()
        return carry

    lax.fori_loop(1, count, one, 0)


def finish(held, sems, axis, count, me):
    everything = held.at[pl.ds(0, count - 1)]
    pltpu.make_async_remote_copy(
        src_ref=everything,
        dst_ref=everything,
        send_sem=sems.at[0],
        recv_sem=sems.at[1],
        device_id={axis: lax.rem(me + 1, count)},
        device_id_type=MESH,
    ).wait()


def greet(axis, count, me):
    barrier = pltpu.get_barrier_semaphore()

    def one(step, carry):
        pl.semaphore_signal(
            barrier, inc=1, device_id={axis: lax.rem(me + step, count)}, device_id_type=MESH
        )
        return carry

    lax.fori_loop(1, count, one, 0)


def beam_kernel(do_out, do_query, do_pages, n_tok, n_head, *refs):
    refs = list(refs)
    take = lambda k: [refs.pop(0) for _ in range(k)]
    if do_out:
        o_ref, lse_ref, wo_ref = take(3)
    (state_ref,) = take(1)
    if do_query:
        gain_ref, wq_ref = take(2)
    if do_pages:
        (outbox_ref,) = take(1)
    if do_out:
        (state_out_ref,) = take(1)
    if do_query:
        (q_out_ref,) = take(1)
    if do_pages:
        (inbox_out_ref,) = take(1)
    if do_out:
        o_recv, lse_recv, o_held, b_send, b_recv, s_held = take(6)
    if do_query:
        q_send, q_recv, q_held = take(3)
    if do_pages:
        (inbox,) = take(1)
    (sems,) = take(1)

    me_t = lax.axis_index("tokens")
    me_h = lax.axis_index("heads")
    tok = ("tokens", n_tok, me_t)
    head = ("heads", n_head, me_h)
    greet(*tok)
    peers = n_tok - 1
    if do_out:
        greet(*head)
        peers += n_head - 1
    pl.semaphore_wait(pltpu.get_barrier_semaphore(), peers)

    if do_out:
        scatter_start(o_ref, o_recv, sems.at[0], *tok)
        scatter_start(lse_ref, lse_recv, sems.at[1], *tok)
    if do_pages:
        scatter_start(outbox_ref, inbox, sems.at[2], *tok)
        inbox[me_t] = outbox_ref[me_t]
    if do_out:
        o_recv[me_t] = o_ref[me_t]
        lse_recv[me_t] = lse_ref[me_t]
        finish(lse_recv, sems.at[1], *tok)
        lse = lse_recv[...]
        weight = jnp.exp2(lse - jnp.max(lse, axis=0, keepdims=True))
        share = weight / jnp.sum(weight, axis=0, keepdims=True)
        finish(o_recv, sems.at[0], *tok)
        for g in range(o_ref.shape[2] // DH):
            cols = slice(g * DH, (g + 1) * DH)
            mixed = jnp.sum(o_recv[:, :, cols].astype(jnp.float32) * share[:, :, g : g + 1], axis=0)
            o_held[me_t, :, cols] = mixed.astype(jnp.bfloat16)
        gather_start(o_held, sems.at[3], *tok)
        finish(o_held, sems.at[3], *tok)
        width = o_ref.shape[2]
        whole = o_held[...].astype(jnp.float32).reshape(-1, width).astype(jnp.bfloat16)
        branch = jnp.dot(whole, wo_ref[...], preferred_element_type=jnp.float32)
        b_send[...] = branch.reshape(b_send.shape).astype(jnp.bfloat16)
        scatter_start(b_send, b_recv, sems.at[4], *head)
        b_recv[me_h] = b_send[me_h]
        finish(b_recv, sems.at[4], *head)
        total = jnp.sum(b_recv[...].astype(jnp.float32), axis=0)
        s_held[me_h] = (state_ref[me_h].astype(jnp.float32) + total).astype(jnp.bfloat16)
        gather_start(s_held, sems.at[5], *head)
        finish(s_held, sems.at[5], *head)
        state_out_ref[...] = s_held[...]
        state = s_held[...]
    else:
        state = state_ref[...]
    if do_query:
        state = state.astype(jnp.float32).reshape(-1, state.shape[2])
        squares = jnp.sum(state * state, axis=1, keepdims=True)
        scaled = (state * gain_ref[...].astype(jnp.float32)).astype(jnp.bfloat16)
        part = jnp.dot(scaled, wq_ref[...], preferred_element_type=jnp.float32)
        width = part.shape[1]
        rows = part.shape[0] // n_tok
        q_send[:, :, :width] = part.reshape(n_tok, rows, width).astype(jnp.bfloat16)
        q_send[:, :, width:] = (
            jnp.broadcast_to(squares, (part.shape[0], DH))
            .reshape(n_tok, rows, DH)
            .astype(jnp.bfloat16)
        )
        scatter_start(q_send, q_recv, sems.at[6], *tok)
        q_recv[me_t] = q_send[me_t]
        finish(q_recv, sems.at[6], *tok)
        total = jnp.sum(q_recv[...].astype(jnp.float32), axis=0)
        factor = lax.rsqrt(total[:, width : width + 1] / D + EPSILON)
        q_held[me_t] = (total[:, :width] * factor).astype(jnp.bfloat16)
        gather_start(q_held, sems.at[7], *tok)
        finish(q_held, sems.at[7], *tok)
        q_out_ref[...] = q_held[...].astype(jnp.float32).reshape(-1, width).astype(jnp.bfloat16)
    if do_pages:
        finish(inbox, sems.at[2], *tok)
        inbox_out_ref[...] = inbox[...]


def beam_step(n_tok, n_head, collective_id, state, out=None, query=None, pages=None):
    do_out, do_query, do_pages = (out is not None, query is not None, pages is not None)
    beams, cols = state.shape
    state3 = state.reshape(n_head, beams // n_head, cols)
    bf16 = jnp.bfloat16
    args, out_shape, scratch = [], [], []
    if do_out:
        o, lse, wo = out
        width = o.shape[1]
        args += [o.reshape(n_tok, -1, width), lse.reshape(n_tok, -1, DH), wo]
        out_shape += [jax.ShapeDtypeStruct(state3.shape, bf16)]
        rows = beams // n_tok
        scratch += [
            pltpu.VMEM((n_tok, rows, width), bf16),
            pltpu.VMEM((n_tok, rows, DH), jnp.float32),
            pltpu.VMEM((n_tok, rows, width), bf16),
            pltpu.VMEM(state3.shape, bf16),
            pltpu.VMEM(state3.shape, bf16),
            pltpu.VMEM(state3.shape, bf16),
        ]
    args += [state3]
    if do_query:
        gain, wq = query
        args += [gain, wq]
        width = wq.shape[1]
        out_shape += [jax.ShapeDtypeStruct((beams, width), bf16)]
        rows = beams // n_tok
        scratch += [
            pltpu.VMEM((n_tok, rows, width + DH), bf16),
            pltpu.VMEM((n_tok, rows, width + DH), bf16),
            pltpu.VMEM((n_tok, rows, width), bf16),
        ]
    if do_pages:
        args += [pages]
        out_shape += [jax.ShapeDtypeStruct(pages.shape, bf16)]
        scratch += [pltpu.VMEM(pages.shape, bf16)]
    scratch += [pltpu.SemaphoreType.DMA((8, 2))]
    res = pl.pallas_call(
        functools.partial(beam_kernel, do_out, do_query, do_pages, n_tok, n_head),
        out_shape=out_shape,
        in_specs=[VMEM_SPEC] * len(args),
        out_specs=[VMEM_SPEC] * len(out_shape),
        scratch_shapes=scratch,
        compiler_params=pltpu.CompilerParams(
            collective_id=collective_id, has_side_effects=True, vmem_limit_bytes=32 << 20
        ),
        name=f"beam_step_{collective_id}",
    )(*args)
    res = list(res)
    if do_out:
        res[0] = res[0].reshape(beams, cols)
    return res


def attend_kernel(blocks, block, has_fresh, has_carry, last, *refs):
    refs = list(refs)
    q_ref = refs.pop(0)
    if blocks:
        k_ref, v_ref, bias_ref = [refs.pop(0) for _ in range(3)]
    if has_fresh:
        kf_ref, vf_ref = [refs.pop(0) for _ in range(2)]
    if has_carry:
        acc_in_ref, top_in_ref = [refs.pop(0) for _ in range(2)]
    q = q_ref[...]
    rows = q.shape[0]
    if has_carry:
        acc, top = acc_in_ref[...], top_in_ref[:, :1]
    else:
        acc = jnp.zeros((rows, 2 * DH), jnp.float32)
        top = jnp.full((rows, 1), -1e30, jnp.float32)

    def step(acc, top, keys, values, bias):
        s = lax.dot_general(
            q, keys, (((1,), (1,)), ((), ())), preferred_element_type=jnp.float32
        )
        if bias is not None:
            s = s + bias
        here = jnp.maximum(top, jnp.max(s, axis=1, keepdims=True))
        p = jnp.exp2((s - here) * SCALE2).astype(jnp.bfloat16)
        shrink = jnp.exp2((top - here) * SCALE2)
        return acc * shrink + jnp.dot(p, values, preferred_element_type=jnp.float32), here

    for b in range(blocks):
        at = slice(b * block, (b + 1) * block)
        acc, top = step(acc, top, k_ref[at, :], v_ref[at, :], bias_ref[:, at])
    if has_fresh:
        acc, top = step(acc, top, kf_ref[...], vf_ref[...], None)
    if last:
        o_ref, lse_ref = refs
        g = pl.program_id(0)
        amount = acc[:, DH:]
        o_ref[...] = (acc[:, :DH] / amount).astype(jnp.bfloat16)
        lane = lax.broadcasted_iota(jnp.int32, (rows, DH), 1)
        value = top * SCALE2 + jnp.log2(amount)
        kept = jnp.where(g == 0, jnp.zeros_like(value), lse_ref[...])
        lse_ref[...] = jnp.where(lane == g, value, kept)
    else:
        acc_ref, top_ref = refs
        acc_ref[...] = acc
        top_ref[...] = jnp.broadcast_to(top, (rows, DH))


def attend(q, old=None, fresh=None, carry=None, block=512):
    beams, width = q.shape
    groups = width // DH
    args, specs = [q], [pl.BlockSpec((beams, DH), lambda g: (0, g))]
    whole = lambda a: pl.BlockSpec(a.shape, lambda g: (0,) * a.ndim)
    blocks = 0
    for extra in (old, fresh):
        if extra is not None:
            args += list(extra)
            specs += [whole(a) for a in extra]
    if old is not None:
        blocks = old[0].shape[0] // block
    last = fresh is not None
    acc_spec = pl.BlockSpec((beams, 2 * DH), lambda g: (0, g))
    top_spec = pl.BlockSpec((beams, DH), lambda g: (0, g))
    if carry is not None:
        args += list(carry)
        specs += [acc_spec, top_spec]
    if last:
        out_shape = [
            jax.ShapeDtypeStruct((beams, width), jnp.bfloat16),
            jax.ShapeDtypeStruct((beams, DH), jnp.float32),
        ]
        out_specs = [
            pl.BlockSpec((beams, DH), lambda g: (0, g)),
            pl.BlockSpec((beams, DH), lambda g: (0, 0)),
        ]
    else:
        out_shape = [
            jax.ShapeDtypeStruct((beams, 2 * width), jnp.float32),
            jax.ShapeDtypeStruct((beams, width), jnp.float32),
        ]
        out_specs = [acc_spec, top_spec]
    rows = sum(a[0].shape[0] for a in (old, fresh) if a is not None)
    return pl.pallas_call(
        functools.partial(
            attend_kernel, blocks, block, fresh is not None, carry is not None, last
        ),
        grid=(groups,),
        out_shape=out_shape,
        in_specs=specs,
        out_specs=out_specs,
        compiler_params=pltpu.CompilerParams(vmem_limit_bytes=40 << 20),
        cost_estimate=pl.CostEstimate(
            flops=4 * beams * width * rows,
            bytes_accessed=rows * 3 * DH * 2,
            transcendentals=beams * groups * rows,
        ),
        name=f"attend_{blocks}_{int(last)}",
    )(*args)


def fresh_kernel(
    n_head,
    subs,
    subs2,
    att_ref,
    wt_hbm,
    hid_ref,
    gain_ref,
    kvr_ref,
    hid_out_ref,
    fresh_ref,
    wt,
    part,
    s_buf,
    r_buf,
    part2,
    s_buf2,
    r_buf2,
    squares,
    w_sems,
    s_sems,
    r_sems,
    s_sems2,
    r_sems2,
    sq_sems,
):
    me = lax.axis_index("heads")
    tokens, width = hid_ref.shape
    half = tokens // 2
    middle = n_head // 2
    rows_sub = half // subs
    rows_sub2 = tokens // subs2
    wrap = lambda value: lax.rem(value + 2 * n_head, n_head)
    lanes = [(sub, way) for sub in range(subs) for way in (0, 1)]
    sign = (1, -1)
    at_rows = lambda sub, way: slice(way * half + sub * rows_sub, way * half + (sub + 1) * rows_sub)

    def load(c):
        rows = pl.ds(pl.multiple_of(c * width, width), width)
        return pltpu.make_async_copy(wt_hbm.at[rows], wt.at[c], w_sems.at[c])

    lax.fori_loop(0, n_head, lambda c, k: (load(c).start(), k)[1], 0)
    greet("heads", n_head, me)
    pl.semaphore_wait(pltpu.get_barrier_semaphore(), n_head - 1)

    def product(c):
        load(c).wait()
        part[c] = lax.dot_general(
            att_ref[...], wt[c], (((1,), (1,)), ((), ())), preferred_element_type=jnp.float32
        )

    def sum_copy(step, sub, way):
        return pltpu.make_async_remote_copy(
            src_ref=s_buf.at[step, way, sub],
            dst_ref=r_buf.at[step, way, sub],
            send_sem=s_sems.at[step, way, sub],
            recv_sem=r_sems.at[step, way, sub],
            device_id={"heads": wrap(me + sign[way])},
            device_id_type=MESH,
        )

    product(wrap(me - 1))
    product(wrap(me + 1))

    def reduce_step(step, carry):
        for sub, way in lanes:
            c = wrap(me - sign[way] * (1 + step))
            own = part[c, at_rows(sub, way), :]

            @pl.when(step == 0)
            def _():
                s_buf[step, way, sub] = own.astype(jnp.bfloat16)

            @pl.when(step > 0)
            def _():
                sum_copy(step - 1, sub, way).wait_recv()
                s_buf[step, way, sub] = (
                    own + r_buf[step - 1, way, sub].astype(jnp.float32)
                ).astype(jnp.bfloat16)

            sum_copy(step, sub, way).start()

        @pl.when(step < middle - 1)
        def _():
            product(wrap(me - 2 - step))
            product(lax.select(step == middle - 2, me, wrap(me + 2 + step)))

        return carry

    lax.fori_loop(0, n_head - 1, reduce_step, 0)

    last = n_head - 2
    for sub, way in lanes:
        rows = at_rows(sub, way)
        sum_copy(last, sub, way).wait_recv()
        total = part[me, rows, :] + r_buf[last, way, sub].astype(jnp.float32)
        hid_out_ref[rows, :] = (hid_ref[rows, :].astype(jnp.float32) + total).astype(jnp.bfloat16)

    hidden = hid_out_ref[...].astype(jnp.float32)
    scaled = (hidden * gain_ref[...].astype(jnp.float32)).astype(jnp.bfloat16)

    def product2(c):
        part2[c] = jnp.dot(scaled, kvr_ref[c], preferred_element_type=jnp.float32)

    count = (middle, n_head - 1 - middle)

    def chunk(step, way):
        return wrap(me + middle - step) if way == 0 else wrap(me - count[1] + step)

    def share_copy(step, sub, way):
        return pltpu.make_async_remote_copy(
            src_ref=s_buf2.at[step, way, sub],
            dst_ref=r_buf2.at[step, way, sub],
            send_sem=s_sems2.at[step, way, sub],
            recv_sem=r_sems2.at[step, way, sub],
            device_id={"heads": wrap(me + sign[way])},
            device_id_type=MESH,
        )

    product2(chunk(0, 0))
    product2(chunk(0, 1))
    for step in range(middle):
        for sub in range(subs2):
            rows = slice(sub * rows_sub2, (sub + 1) * rows_sub2)
            for way in (0, 1):
                if step >= count[way]:
                    continue
                value = part2[chunk(step, way), rows, :]
                if step:
                    share_copy(step - 1, sub, way).wait_recv()
                    value = value + r_buf2[step - 1, way, sub].astype(jnp.float32)
                s_buf2[step, way, sub] = value.astype(jnp.bfloat16)
                share_copy(step, sub, way).start()
        if step == 0:
            flat = (hidden * hidden).astype(jnp.bfloat16)
            ones = jnp.ones((8, width), jnp.bfloat16)
            squares[me] = lax.dot_general(
                ones, flat, (((1,), (1,)), ((), ())), preferred_element_type=jnp.float32
            )
            gather_start(squares, sq_sems, "heads", n_head, me)
        for way in (0, 1):
            if step + 1 < count[way]:
                product2(chunk(step + 1, way))
        if step == middle - 1:
            product2(me)
    finish(squares, sq_sems, "heads", n_head, me)
    mean = jnp.transpose(jnp.sum(squares[...], axis=0))[:, :1] / D
    factor = lax.rsqrt(mean + EPSILON)
    for sub in range(subs2):
        rows = slice(sub * rows_sub2, (sub + 1) * rows_sub2)
        total = part2[me, rows, :]
        for way in (0, 1):
            share_copy(count[way] - 1, sub, way).wait_recv()
            total = total + r_buf2[count[way] - 1, way, sub].astype(jnp.float32)
        fresh_ref[rows, :] = (total * factor[rows]).astype(jnp.bfloat16)

    def drain(step, carry):
        for sub, way in lanes:
            sum_copy(step, sub, way).wait_send()
        return carry

    lax.fori_loop(0, n_head - 1, drain, 0)
    for way in (0, 1):
        for step in range(count[way]):
            for sub in range(subs2):
                share_copy(step, sub, way).wait_send()


def fresh_rows(n_head, attended, weight_t, hidden, gain, kvr, subs=2, subs2=2):
    tokens, width = hidden.shape
    bf16, f32 = jnp.bfloat16, jnp.float32
    out_cols = kvr.shape[2]
    pieces = (2, subs, tokens // 2 // subs, width)
    pieces2 = (2, subs2, tokens // subs2, out_cols)
    return pl.pallas_call(
        functools.partial(fresh_kernel, n_head, subs, subs2),
        out_shape=[
            jax.ShapeDtypeStruct(hidden.shape, bf16),
            jax.ShapeDtypeStruct((tokens, out_cols), bf16),
        ],
        in_specs=[VMEM_SPEC, pl.BlockSpec(memory_space=pl.ANY)] + [VMEM_SPEC] * 3,
        out_specs=[VMEM_SPEC] * 2,
        scratch_shapes=[
            pltpu.VMEM((n_head, width, width), bf16),
            pltpu.VMEM((n_head, tokens, width), f32),
            pltpu.VMEM((n_head - 1, *pieces), bf16),
            pltpu.VMEM((n_head - 1, *pieces), bf16),
            pltpu.VMEM((n_head, tokens, out_cols), f32),
            pltpu.VMEM((n_head // 2, *pieces2), bf16),
            pltpu.VMEM((n_head // 2, *pieces2), bf16),
            pltpu.VMEM((n_head, 8, tokens), f32),
            pltpu.SemaphoreType.DMA((n_head,)),
            pltpu.SemaphoreType.DMA((n_head - 1, 2, subs)),
            pltpu.SemaphoreType.DMA((n_head - 1, 2, subs)),
            pltpu.SemaphoreType.DMA((n_head // 2, 2, subs2)),
            pltpu.SemaphoreType.DMA((n_head // 2, 2, subs2)),
            pltpu.SemaphoreType.DMA((2,)),
        ],
        compiler_params=pltpu.CompilerParams(
            collective_id=4, has_side_effects=True, vmem_limit_bytes=48 << 20
        ),
        name="fresh_rows",
    )(attended, weight_t, hidden, gain[None, :], kvr)


def entry_kernel(
    n_tok,
    n_head,
    side,
    state_ref,
    gain_ref,
    wq_ref,
    own_w,
    own_kv,
    kvw,
    q_out_ref,
    whole_w,
    win,
    kvr,
    q_send,
    q_recv,
    q_held,
    q_sems,
    w_sems,
    pair_sems,
    win_sems,
    kv_sems,
    kv_pair_sems,
    local_sems,
):
    me = lax.axis_index("tokens")
    me_h = lax.axis_index("heads")
    core = lax.rem(me, 2)
    y = lax.rem(me // 2, side)
    x = me // (2 * side)
    wide = n_tok // (2 * side)
    partner = me + 1 - 2 * core
    at = lambda i, j: (
        lax.rem(x + i + 2 * wide, wide) * side + lax.rem(y + j + 2 * side, side)
    ) * 2 + core
    greet("tokens", n_tok, me)
    greet("heads", n_head, me_h)
    pl.semaphore_wait(pltpu.get_barrier_semaphore(), n_tok + n_head - 2)

    state = state_ref[...].astype(jnp.float32)
    squares = jnp.sum(state * state, axis=1, keepdims=True)
    scaled = (state * gain_ref[...].astype(jnp.float32)).astype(jnp.bfloat16)
    part = jnp.dot(scaled, wq_ref[...], preferred_element_type=jnp.float32)
    width = part.shape[1]
    rows = part.shape[0] // n_tok
    q_send[:, :, :width] = part.reshape(n_tok, rows, width).astype(jnp.bfloat16)
    q_send[:, :, width:] = (
        jnp.broadcast_to(squares, (part.shape[0], DH)).reshape(n_tok, rows, DH).astype(jnp.bfloat16)
    )
    scatter_start(q_send, q_recv, q_sems.at[0], "tokens", n_tok, me)
    q_recv[me] = q_send[me]

    def remote(src, dst, sems, target, axis="tokens"):
        return pltpu.make_async_remote_copy(
            src_ref=src,
            dst_ref=dst,
            send_sem=sems.at[0],
            recv_sem=sems.at[1],
            device_id={axis: target},
            device_id_type=MESH,
        )

    back = lambda b: lax.rem(me - b + n_tok, n_tok)
    ahead = lambda b: lax.rem(me + b, n_tok)
    win_two = remote(own_kv, win.at[2], win_sems.at[0], ahead(2))
    win_four = remote(own_kv, win.at[4], win_sems.at[1], ahead(4))
    win_two.start()
    win_four.start()

    depth = own_w.shape[0]
    piece = depth // 4
    block = lambda half, i, j: at(i, j) if half == 0 else at(j, i)

    def rows_of(half, part_at=None):
        if part_at is None:
            return pl.ds(half * 2 * piece, 2 * piece)
        return pl.ds((half * 2 + part_at) * piece, piece)

    slots = {}
    for half in (0, 1):
        for name in ("a+", "a-", "f+", "f-"):
            slots[half, name] = len(slots)
        for i in (0, -1, 1, 2):
            for name in ("a+", "a-", "f+", "f-"):
                slots[half, i, name] = len(slots)

    def first(half, name):
        way = 1 if name[1] == "+" else -1
        target = block(half, way, 0)
        if name[0] == "a":
            where = rows_of(half)
            return remote(
                own_w.at[where], whole_w.at[me, where], w_sems.at[slots[half, name]], target
            )
        ref = whole_w.at[block(half, -way, 0), rows_of(half, 0 if way == 1 else 1)]
        return remote(ref, ref, w_sems.at[slots[half, name]], target)

    def first_in(half, name):
        way = 1 if name[1] == "+" else -1
        if name[0] == "a":
            ref = whole_w.at[block(half, -way, 0), rows_of(half)]
        else:
            ref = whole_w.at[block(half, -2 * way, 0), rows_of(half, 0 if way == 1 else 1)]
        return remote(ref, ref, w_sems.at[slots[half, name]], block(half, way, 0))

    def second(half, i, name):
        way = 1 if name[1] == "+" else -1
        target = block(half, 0, way)
        if name[0] == "a":
            where = rows_of(half)
            dst = whole_w.at[block(half, i, 0), where]
            src = own_w.at[where] if i == 0 else dst
        else:
            src = dst = whole_w.at[block(half, i, -way), rows_of(half, 0 if way == 1 else 1)]
        return remote(src, dst, w_sems.at[slots[half, i, name]], target)

    def second_in(half, i, name):
        way = 1 if name[1] == "+" else -1
        if name[0] == "a":
            ref = whole_w.at[block(half, i, -way), rows_of(half)]
        else:
            ref = whole_w.at[block(half, i, -2 * way), rows_of(half, 0 if way == 1 else 1)]
        return remote(ref, ref, w_sems.at[slots[half, i, name]], block(half, 0, way))

    def share(half, i, j):
        where = rows_of(half)
        dst = whole_w.at[block(half, i, j), where]
        src = own_w.at[where] if (i, j) == (0, 0) else dst
        remote(src, dst, pair_sems, partner).start()

    halves = (0, 1)
    for half in halves:
        for name in ("a+", "a-"):
            first(half, name).start()
    for half in halves:
        for name in ("a+", "a-"):
            second(half, 0, name).start()
    for half in halves:
        share(half, 0, 0)

    kv_rows = kvw.shape[1] // 2
    kv_half = pl.ds(pl.multiple_of(core * kv_rows, kv_rows), kv_rows)

    def kv_out(k):
        target = lax.rem(me_h + k, n_head)
        return remote(
            kvw.at[target, kv_half], kvr.at[me_h, kv_half], kv_sems.at[k - 1], target, "heads"
        )

    def kv_in(k):
        ref = kvr.at[lax.rem(me_h - k + n_head, n_head), kv_half]
        return remote(ref, ref, kv_sems.at[k - 1], lax.rem(me_h + k, n_head), "heads")

    order = sorted(range(1, n_head), key=lambda k: min(k, n_head - k))
    for k in order:
        kv_out(k).start()

    own_copies = [
        pltpu.make_async_copy(own_w, whole_w.at[me], local_sems.at[0]),
        pltpu.make_async_copy(own_kv, win.at[0], local_sems.at[1]),
        pltpu.make_async_copy(kvw.at[me_h], kvr.at[me_h], local_sems.at[2]),
    ]
    for copy in own_copies:
        copy.start()

    finish(q_recv, q_sems.at[0], "tokens", n_tok, me)
    total = jnp.sum(q_recv[...].astype(jnp.float32), axis=0)
    factor = lax.rsqrt(total[:, width : width + 1] / D + EPSILON)
    q_held[me] = (total[:, :width] * factor).astype(jnp.bfloat16)
    gather_start(q_held, q_sems.at[1], "tokens", n_tok, me)

    own_copies[1].wait()
    win_in = lambda b, k: remote(win.at[b], win.at[b], win_sems.at[k], partner)

    def relay(src, dst, k):
        return remote(win.at[src], win.at[dst], win_sems.at[k], partner)

    for name in ("a+", "a-"):
        way = 1 if name[1] == "+" else -1
        for half in halves:
            first_in(half, name).wait_recv()
            first(half, "f" + name[1]).start()
            for other in ("a+", "a-"):
                second(half, -way, other).start()
            share(half, -way, 0)
    win_in(2, 0).wait_recv()
    relay(2 * core, 1, 2).start()
    for name in ("a+", "a-"):
        way = 1 if name[1] == "+" else -1
        for half in halves:
            second_in(half, 0, name).wait_recv()
            second(half, 0, "f" + name[1]).start()
            share(half, 0, -way)
    for half in halves:
        first_in(half, "f+").wait_recv()
        first_in(half, "f-").wait_recv()
        for other in ("a+", "a-"):
            second(half, 2, other).start()
        share(half, 2, 0)
    win_in(4, 1).wait_recv()
    relay(2 + 2 * core, 3, 3).start()
    for i in (-1, 1):
        for name in ("a+", "a-"):
            way = 1 if name[1] == "+" else -1
            for half in halves:
                second_in(half, i, name).wait_recv()
                second(half, i, "f" + name[1]).start()
                share(half, i, -way)
    finish(q_held, q_sems.at[1], "tokens", n_tok, me)
    q_out_ref[...] = q_held[...].astype(jnp.float32).reshape(-1, width).astype(jnp.bfloat16)

    def kv_share(k):
        ref = kvr.at[lax.rem(me_h - k + n_head, n_head), kv_half]
        return remote(ref, ref, kv_pair_sems.at[k - 1], partner)

    def kv_share_in(k):
        other = pl.ds(pl.multiple_of((1 - core) * kv_rows, kv_rows), kv_rows)
        ref = kvr.at[lax.rem(me_h - k + n_head, n_head), other]
        return remote(ref, ref, kv_pair_sems.at[k - 1], partner)

    for k in order[: n_head // 2]:
        kv_in(k).wait_recv()
        kv_share(k).start()
    for half in halves:
        second_in(half, 0, "f+").wait_recv()
        second_in(half, 0, "f-").wait_recv()
        share(half, 0, 2)
    for name in ("a+", "a-"):
        way = 1 if name[1] == "+" else -1
        for half in halves:
            second_in(half, 2, name).wait_recv()
            second(half, 2, "f" + name[1]).start()
            share(half, 2, -way)
    for i in (-1, 1, 2):
        for half in halves:
            second_in(half, i, "f+").wait_recv()
            second_in(half, i, "f-").wait_recv()
            share(half, i, 2)
    for k in order[n_head // 2 :]:
        kv_in(k).wait_recv()
        kv_share(k).start()

    win_in(1, 2).wait_recv()
    win_in(3, 3).wait_recv()
    relay(2 * core, 1, 2).wait_send()
    relay(2 + 2 * core, 3, 3).wait_send()
    win_two.wait_send()
    win_four.wait_send()
    for half in halves:
        for name in ("a+", "a-", "f+", "f-"):
            first(half, name).wait_send()
            for i in (0, -1, 1, 2):
                second(half, i, name).wait_send()
    for k in order:
        kv_out(k).wait_send()
        kv_share(k).wait_send()
        kv_share_in(k).wait_recv()
    half_of_all = whole_w.at[pl.ds(0, n_tok // 2)]
    remote(half_of_all, half_of_all, pair_sems, partner).wait()
    own_copies[0].wait()
    own_copies[2].wait()


def entry(n_tok, n_head, state, gain, wq, own_w, own_kv, kvw, side=4):
    bf16 = jnp.bfloat16
    beams = state.shape[0]
    width = wq.shape[1]
    rows = beams // n_tok
    any_spec = pl.BlockSpec(memory_space=pl.ANY)
    reach = WINDOW // own_kv.shape[1] + 1
    return pl.pallas_call(
        functools.partial(entry_kernel, n_tok, n_head, side),
        out_shape=[
            jax.ShapeDtypeStruct((beams, width), bf16),
            jax.ShapeDtypeStruct((n_tok, *own_w.shape), bf16),
            jax.ShapeDtypeStruct((reach, *own_kv.shape), bf16),
            jax.ShapeDtypeStruct(kvw.shape, bf16),
        ],
        in_specs=[VMEM_SPEC] * 3 + [any_spec] * 3,
        out_specs=[VMEM_SPEC] + [any_spec] * 3,
        scratch_shapes=[
            pltpu.VMEM((n_tok, rows, width + DH), bf16),
            pltpu.VMEM((n_tok, rows, width + DH), bf16),
            pltpu.VMEM((n_tok, rows, width), bf16),
            pltpu.SemaphoreType.DMA((2, 2)),
            pltpu.SemaphoreType.DMA((40, 2)),
            pltpu.SemaphoreType.DMA((2,)),
            pltpu.SemaphoreType.DMA((4, 2)),
            pltpu.SemaphoreType.DMA((n_head - 1, 2)),
            pltpu.SemaphoreType.DMA((n_head - 1, 2)),
            pltpu.SemaphoreType.DMA((3,)),
        ],
        compiler_params=pltpu.CompilerParams(
            collective_id=1, has_side_effects=True, vmem_limit_bytes=16 << 20
        ),
        name="entry",
    )(state, gain, wq, own_w, own_kv, kvw)


def window_kernel(reach, q_ref, win_ref, bias_ref, o_ref):
    q = q_ref[...]
    rows = q.shape[0]
    acc = jnp.zeros((rows, 2 * DH), jnp.float32)
    top = jnp.full((rows, 1), -1e30, jnp.float32)
    row = lax.broadcasted_iota(jnp.int32, (rows, rows), 0)
    col = lax.broadcasted_iota(jnp.int32, (rows, rows), 1)
    ones = jnp.ones((rows, DH), jnp.bfloat16)
    for b in range(reach):
        s = lax.dot_general(
            q, win_ref[b, 0], (((1,), (1,)), ((), ())), preferred_element_type=jnp.float32
        )
        if b == 0:
            s = jnp.where(col <= row, s, -1e30)
        else:
            s = s + bias_ref[:, b * rows : (b + 1) * rows]
        if b == reach - 1:
            s = jnp.where(col > row, s, -1e30)
        here = jnp.maximum(top, jnp.max(s, axis=1, keepdims=True))
        p = jnp.exp2((s - here) * SCALE2).astype(jnp.bfloat16)
        shrink = jnp.exp2((top - here) * SCALE2)
        values = jnp.concatenate([win_ref[b, 1], ones], axis=1)
        acc = acc * shrink + jnp.dot(p, values, preferred_element_type=jnp.float32)
        top = here
    o_ref[...] = (acc[:, :DH] / acc[:, DH:]).astype(jnp.bfloat16)


def window_attend(q, win, bias):
    rows, width = q.shape
    head = pl.BlockSpec((rows, DH), lambda g: (0, g))
    whole = lambda a: pl.BlockSpec(a.shape, lambda g: (0,) * a.ndim)
    return pl.pallas_call(
        functools.partial(window_kernel, win.shape[0]),
        grid=(width // DH,),
        out_shape=jax.ShapeDtypeStruct(q.shape, jnp.bfloat16),
        in_specs=[head, whole(win), whole(bias)],
        out_specs=head,
        compiler_params=pltpu.CompilerParams(vmem_limit_bytes=24 << 20),
        name="window_attend",
    )(q, win, bias)


def place_kernel(page_rows, slots, row_ref, cache_ref, inbox_ref, out_ref, sem):
    def copy(slot):
        return pltpu.make_async_copy(
            inbox_ref.at[slot], out_ref.at[pl.ds(row_ref[slot] * page_rows, page_rows)], sem
        )

    def start(slot, carry):
        @pl.when(row_ref[slot] >= 0)
        def _():
            copy(slot).start()

        return carry

    def wait(slot, carry):
        @pl.when(row_ref[slot] >= 0)
        def _():
            copy(slot).wait()

        return carry

    lax.fori_loop(0, slots, start, 0)
    lax.fori_loop(0, slots, wait, 0)


def place_pages(rows, cache, inbox):
    return pl.pallas_call(
        functools.partial(place_kernel, PAGE, inbox.shape[0]),
        out_shape=jax.ShapeDtypeStruct(cache.shape, cache.dtype),
        in_specs=[
            pl.BlockSpec(memory_space=pltpu.SMEM),
            pl.BlockSpec(memory_space=pl.ANY),
            VMEM_SPEC,
        ],
        out_specs=pl.BlockSpec(memory_space=pl.ANY),
        scratch_shapes=[pltpu.SemaphoreType.DMA],
        input_output_aliases={1: 0},
        name="place_pages",
    )(rows, cache, inbox)


def shards(
    hidden_in,
    queries,
    keyvals,
    out_weight,
    kv_gain,
    kv_weight,
    cache,
    page_home,
    cache_len,
    beam_state,
    parents,
    beam_gain,
    query_weight,
    beam_out_weight,
):
    n_tok = lax.axis_size("tokens")
    n_head = lax.axis_size("heads")
    tok_rows = hidden_in.shape[0]
    me = lax.axis_index("tokens")
    reach_back = -(-WINDOW // tok_rows)

    state = jnp.take(beam_state, parents, axis=0)
    q, weight_t, win, kvr = entry(
        n_tok,
        n_head,
        state,
        beam_gain[0:1],
        query_weight[0],
        out_weight.T,
        jnp.swapaxes(keyvals, 0, 1),
        kv_weight.reshape(n_head, -1, 2 * DH),
    )

    cache_rows = cache.shape[0]
    pages_here = cache_rows // PAGE
    local_page = jnp.where(page_home // pages_here == me, page_home % pages_here, -1)
    page_ids = jnp.arange(pages_here, dtype=jnp.int32)
    written = jnp.any(page_ids[:, None] == local_page[None, :], axis=1)
    row_ids = me * cache_rows + jnp.arange(cache_rows, dtype=jnp.int32)
    kept = (row_ids < cache_len[0]) & ~jnp.repeat(written, PAGE)
    bias = jnp.where(kept, 0.0, -1e30).astype(jnp.float32)[None, :]
    old_keys = cache[:, 0]
    old_values = jnp.concatenate([cache[:, 1], jnp.ones_like(old_keys)], axis=1)
    old = (old_keys, old_values, bias)
    carry = attend(q, old=old)

    back = jnp.arange(reach_back + 1, dtype=jnp.int32)
    window_bias = jnp.repeat(jnp.where(back <= me, 0.0, -1e30).astype(jnp.float32), tok_rows)
    attended = window_attend(queries, win, window_bias[None, :])
    stretch_hidden, fresh = fresh_rows(
        n_head, attended, weight_t.reshape(-1, weight_t.shape[2]), hidden_in, kv_gain, kvr
    )

    own_pages = tok_rows // PAGE
    pages = fresh.reshape(own_pages, PAGE, -1)
    shift = page_home[0] // pages_here
    empty = jnp.zeros((n_tok - own_pages, *pages.shape[1:]), pages.dtype)
    ring = jnp.concatenate([pages, empty, pages, empty], axis=0)
    begin = (2 * n_tok * own_pages - shift - own_pages * me) % n_tok
    outbox = lax.dynamic_slice_in_dim(ring, begin, n_tok, 0)
    source = jnp.arange(n_tok, dtype=jnp.int32)
    which = (me - shift - own_pages * source + 2 * n_tok * own_pages) % n_tok
    landing = jnp.where(
        which < own_pages,
        jnp.take(page_home, jnp.minimum(own_pages * source + which, page_home.shape[0] - 1))
        % pages_here,
        -1,
    )

    fresh_keys = fresh[:, :DH]
    fresh_values = jnp.concatenate([fresh[:, DH:], jnp.ones_like(fresh_keys)], axis=1)
    new = (fresh_keys, fresh_values)
    o, lse = attend(q, fresh=new, carry=carry)
    state, q, inbox = beam_step(
        n_tok,
        n_head,
        2,
        state,
        out=(o, lse, beam_out_weight[0]),
        query=(beam_gain[1:2], query_weight[1]),
        pages=outbox,
    )
    new_cache = place_pages(landing, cache, inbox.reshape(n_tok, PAGE, *cache.shape[1:]))
    o, lse = attend(q, old=old, fresh=new)
    (state,) = beam_step(n_tok, n_head, 3, state, out=(o, lse, beam_out_weight[1]))
    return (stretch_hidden, new_cache, state)


def solution(mesh):
    tokens = "tokens"
    placed = (
        P(tokens, "heads"),
        P(tokens, "heads"),
        P(tokens, None, "heads"),
        P("heads", tokens),
        P("heads"),
        P(None, None, "heads"),
        P(tokens, None, "heads"),
        P(),
        P(),
        P(None, tokens),
        P(),
        P(None, tokens),
        P(None, tokens, "heads"),
        P(None, "heads", tokens),
    )
    return jax.shard_map(
        shards,
        mesh=mesh,
        in_specs=placed,
        out_specs=(P(tokens, "heads"), P(tokens, None, "heads"), P(None, tokens)),
        check_vma=False,
    )
```

```python
import functools
import math

import jax
import jax.numpy as jnp
from jax import lax
from jax.experimental import pallas as pl
from jax.experimental.pallas import tpu as pltpu
from jax.sharding import PartitionSpec as P

D = 5120
DH = 128
WINDOW = 1024
PAGE = 16
LAYERS = 2
EPSILON = 1e-06
SCALE = DH ** (-0.5)
SCALE2 = SCALE * math.log2(math.e)
MESH = pl.DeviceIdType.MESH
VMEM_SPEC = pl.BlockSpec(memory_space=pltpu.VMEM)


def scatter_start(send, recv, sems, axis, count, me):
    def one(step, carry):
        peer = lax.rem(me + step, count)
        pltpu.make_async_remote_copy(
            src_ref=send.at[peer],
            dst_ref=recv.at[me],
            send_sem=sems.at[0],
            recv_sem=sems.at[1],
            device_id={axis: peer},
            device_id_type=MESH,
        ).start()
        return carry

    lax.fori_loop(1, count, one, 0)


def gather_start(held, sems, axis, count, me):
    def one(step, carry):
        peer = lax.rem(me + step, count)
        pltpu.make_async_remote_copy(
            src_ref=held.at[me],
            dst_ref=held.at[me],
            send_sem=sems.at[0],
            recv_sem=sems.at[1],
            device_id={axis: peer},
            device_id_type=MESH,
        ).start()
        return carry

    lax.fori_loop(1, count, one, 0)


def finish(held, sems, axis, count, me):
    everything = held.at[pl.ds(0, count - 1)]
    pltpu.make_async_remote_copy(
        src_ref=everything,
        dst_ref=everything,
        send_sem=sems.at[0],
        recv_sem=sems.at[1],
        device_id={axis: lax.rem(me + 1, count)},
        device_id_type=MESH,
    ).wait()


def greet(axis, count, me):
    barrier = pltpu.get_barrier_semaphore()

    def one(step, carry):
        pl.semaphore_signal(
            barrier, inc=1, device_id={axis: lax.rem(me + step, count)}, device_id_type=MESH
        )
        return carry

    lax.fori_loop(1, count, one, 0)


def page_slot(home_ref, me, own_pages, pages_here, n_tok, slot):
    shift = lax.div(home_ref[0], pages_here)
    which = lax.rem(me - shift - own_pages * slot + 2 * n_tok * own_pages, n_tok)
    page = home_ref[own_pages * slot + jnp.minimum(which, own_pages - 1)]
    return jnp.where(which < own_pages, lax.rem(page, pages_here), -1)


def rest_kernel(
    n_tok,
    n_head,
    subs,
    subs2,
    block,
    split_at,
    home_ref,
    len_ref,
    att_ref,
    hid_ref,
    gain_ref,
    q_ref,
    state_ref,
    beam_gain_ref,
    wt_hbm,
    kvr_hbm,
    keys_hbm,
    values_hbm,
    wo_hbm,
    wq_hbm,
    hid_out_ref,
    inbox_ref,
    state_out_ref,
    wt,
    part,
    s_buf,
    r_buf,
    part2,
    s_buf2,
    r_buf2,
    squares,
    kvi,
    kvd,
    spread,
    keys,
    values,
    wo,
    wq,
    bias,
    acc_s,
    top_s,
    fk,
    fv,
    pages,
    outbox,
    inbox,
    lse_s,
    oa_send,
    ob_send,
    oa_recv,
    ob_recv,
    oa_held,
    ob_held,
    b_send,
    b_recv,
    s_held,
    q_send,
    q_recv,
    qa_held,
    qb_held,
    load_sems,
    w_sems,
    s_sems,
    r_sems,
    s_sems2,
    r_sems2,
    sq_sems,
    page_sems,
    tok_sems,
    head_sems,
):
    f32, bf16 = jnp.float32, jnp.bfloat16
    me = lax.axis_index("heads")
    me_t = lax.axis_index("tokens")
    tok = ("tokens", n_tok, me_t)
    head = ("heads", n_head, me)
    tokens, width = hid_ref.shape
    heads_here = width // DH
    half = tokens // 2
    middle = n_head // 2
    rows_sub = half // subs
    rows_sub2 = tokens // subs2
    wrap = lambda value: lax.rem(value + 2 * n_head, n_head)
    lanes = [(sub, way) for sub in range(subs) for way in (0, 1)]
    sign = (1, -1)
    at_rows = lambda sub, way: slice(way * half + sub * rows_sub, way * half + (sub + 1) * rows_sub)

    def load(c):
        rows = pl.ds(pl.multiple_of(c * width, width), width)
        return pltpu.make_async_copy(wt_hbm.at[rows], wt.at[c], w_sems.at[c])

    lax.fori_loop(0, n_head, lambda c, k: (load(c).start(), k)[1], 0)
    loads = [
        pltpu.make_async_copy(src, dst, load_sems.at[k])
        for k, (src, dst) in enumerate(
            [(kvr_hbm, kvi), (keys_hbm, keys), (values_hbm, values), (wo_hbm, wo), (wq_hbm, wq)]
        )
    ]
    for copy in loads:
        copy.start()
    greet(*head)
    greet(*tok)

    cache_rows = keys.shape[0]
    pages_here = cache_rows // PAGE
    own_pages = tokens // PAGE
    lane = lax.broadcasted_iota(jnp.int32, (1, cache_rows), 1)
    kept = (me_t * cache_rows + lane) < len_ref[0]
    page_of = lane // PAGE
    for slot in range(n_tok):
        landing = page_slot(home_ref, me_t, own_pages, pages_here, n_tok, slot)
        kept = kept & (page_of != landing)
    bias[...] = jnp.where(kept, 0.0, -1e30).astype(f32)

    pl.semaphore_wait(pltpu.get_barrier_semaphore(), n_head + n_tok - 2)

    def product(c):
        load(c).wait()
        part[c] = lax.dot_general(
            att_ref[...], wt[c], (((1,), (1,)), ((), ())), preferred_element_type=f32
        )

    def sum_copy(step, sub, way):
        return pltpu.make_async_remote_copy(
            src_ref=s_buf.at[step, way, sub],
            dst_ref=r_buf.at[step, way, sub],
            send_sem=s_sems.at[step, way, sub],
            recv_sem=r_sems.at[step, way, sub],
            device_id={"heads": wrap(me + sign[way])},
            device_id_type=MESH,
        )

    def soft(q, acc, top, keys_b, values_b, bias_b):
        s = lax.dot_general(q, keys_b, (((1,), (1,)), ((), ())), preferred_element_type=f32)
        if bias_b is not None:
            s = s + bias_b
        here = jnp.maximum(top, jnp.max(s, axis=1, keepdims=True))
        p = jnp.exp2((s - here) * SCALE2).astype(bf16)
        shrink = jnp.exp2((top - here) * SCALE2)
        both = jnp.concatenate([values_b, jnp.ones_like(values_b)], axis=1)
        return acc * shrink + jnp.dot(p, both, preferred_element_type=f32), here

    def soft_old(q):
        acc = jnp.zeros((q.shape[0], 2 * DH), f32)
        top = jnp.full((q.shape[0], 1), -1e30, f32)
        for b in range(cache_rows // block):
            at = slice(b * block, (b + 1) * block)
            acc, top = soft(q, acc, top, keys[at, :], values[at, :], bias[:, at])
        return acc, top

    def spread_kv(c):
        spread[...] = kvi[c].astype(f32)
        count = width
        kvd[c, :, :DH] = spread[pl.ds(0, count, stride=2), :].astype(bf16)
        kvd[c, :, DH:] = spread[pl.ds(1, count, stride=2), :].astype(bf16)

    product(wrap(me - 1))
    product(wrap(me + 1))

    def reduce_step(step, carry):
        for sub, way in lanes:
            c = wrap(me - sign[way] * (1 + step))
            own = part[c, at_rows(sub, way), :]

            @pl.when(step == 0)
            def _():
                s_buf[step, way, sub] = own.astype(bf16)

            @pl.when(step > 0)
            def _():
                sum_copy(step - 1, sub, way).wait_recv()
                s_buf[step, way, sub] = (own + r_buf[step - 1, way, sub].astype(f32)).astype(bf16)

            sum_copy(step, sub, way).start()

        @pl.when(step < middle - 1)
        def _():
            product(wrap(me - 2 - step))
            product(lax.select(step == middle - 2, me, wrap(me + 2 + step)))

        @pl.when(step == 1)
        def _():
            for copy in loads:
                copy.wait()

        @pl.when(step >= n_head - 1 - heads_here)
        def _():
            g = jnp.maximum(step - (n_head - 1 - heads_here), 0)
            q = q_ref[:, pl.ds(pl.multiple_of(g * DH, DH), DH)]
            acc, top = soft_old(q)
            acc_s[g] = acc
            top_s[g] = jnp.broadcast_to(top, (top.shape[0], DH))

        @pl.when(step >= middle - 1)
        def _():
            first = (step - (middle - 1)) * 2
            spread_kv(first)
            spread_kv(first + 1)

        return carry

    lax.fori_loop(0, n_head - 1, reduce_step, 0)

    last = n_head - 2
    for sub, way in lanes:
        rows = at_rows(sub, way)
        sum_copy(last, sub, way).wait_recv()
        total = part[me, rows, :] + r_buf[last, way, sub].astype(f32)
        hid_out_ref[rows, :] = (hid_ref[rows, :].astype(f32) + total).astype(bf16)

    hidden = hid_out_ref[...].astype(f32)
    scaled = (hidden * gain_ref[...].astype(f32)).astype(bf16)

    def product2(c):
        part2[c] = jnp.dot(scaled, kvd[c], preferred_element_type=f32)

    count = (middle, n_head - 1 - middle)

    def chunk(step, way):
        return wrap(me + middle - step) if way == 0 else wrap(me - count[1] + step)

    def share_copy(step, sub, way):
        return pltpu.make_async_remote_copy(
            src_ref=s_buf2.at[step, way, sub],
            dst_ref=r_buf2.at[step, way, sub],
            send_sem=s_sems2.at[step, way, sub],
            recv_sem=r_sems2.at[step, way, sub],
            device_id={"heads": wrap(me + sign[way])},
            device_id_type=MESH,
        )

    product2(chunk(0, 0))
    product2(chunk(0, 1))
    for step in range(middle):
        for sub in range(subs2):
            rows = slice(sub * rows_sub2, (sub + 1) * rows_sub2)
            for way in (0, 1):
                if step >= count[way]:
                    continue
                value = part2[chunk(step, way), rows, :]
                if step:
                    share_copy(step - 1, sub, way).wait_recv()
                    value = value + r_buf2[step - 1, way, sub].astype(f32)
                s_buf2[step, way, sub] = value.astype(bf16)
                share_copy(step, sub, way).start()
        if step == 0:
            flat = (hidden * hidden).astype(bf16)
            ones = jnp.ones((8, width), bf16)
            squares[me] = lax.dot_general(
                ones, flat, (((1,), (1,)), ((), ())), preferred_element_type=f32
            )
            gather_start(squares, sq_sems, *head)
        for way in (0, 1):
            if step + 1 < count[way]:
                product2(chunk(step + 1, way))
        if step == middle - 1:
            product2(me)
    finish(squares, sq_sems, *head)
    mean = jnp.transpose(jnp.sum(squares[...], axis=0))[:, :1] / D
    factor = lax.rsqrt(mean + EPSILON)
    for sub in range(subs2):
        rows = slice(sub * rows_sub2, (sub + 1) * rows_sub2)
        total = part2[me, rows, :]
        for way in (0, 1):
            share_copy(count[way] - 1, sub, way).wait_recv()
            total = total + r_buf2[count[way] - 1, way, sub].astype(f32)
        fresh = total * factor[rows]
        fk[rows, :] = fresh[:, :DH].astype(bf16)
        fv[rows, :] = fresh[:, DH:].astype(bf16)

    lane8 = lax.broadcasted_iota(jnp.int32, (tokens, DH), 1)
    sends = (oa_send, ob_send)
    spans = ((0, split_at), (split_at, heads_here))

    def put_head(layer, group, g, acc, top):
        amount = acc[:, DH:]
        out = (acc[:, :DH] / amount).reshape(n_tok, -1, DH).astype(bf16)
        at = pl.multiple_of((g - spans[group][0]) * DH, DH)
        sends[group][layer, :, :, pl.ds(at, DH)] = out
        value = top * SCALE2 + jnp.log2(amount)
        mine = (lane8 % 8 == g) & (lane8 < 24)
        lse_s[...] = jnp.where(mine, value, lse_s[...])

    def send_group(layer, group):
        value = lse_s[...]
        high = value.astype(bf16).astype(f32)
        mid = (value - high).astype(bf16).astype(f32)
        low = value - high - mid
        packed = jnp.where(lane8 < 8, high, jnp.where(lane8 < 16, mid, low))
        wide = (spans[group][1] - spans[group][0]) * DH
        sends[group][layer, :, :, wide:] = packed.reshape(n_tok, -1, DH).astype(bf16)
        recv = (oa_recv, ob_recv)[group].at[layer]
        scatter_start(sends[group].at[layer], recv, tok_sems.at[layer, group], *tok)

    def mix_group(layer, group):
        recv = (oa_recv, ob_recv)[group].at[layer]
        held = (oa_held, ob_held)[group].at[layer]
        low, high = spans[group]
        wide = (high - low) * DH
        recv[me_t] = sends[group][layer, me_t]
        finish(recv, tok_sems.at[layer, group], *tok)
        packed = recv[:, :, wide:].astype(f32)
        lse = (
            packed[:, :, low:high]
            + packed[:, :, 8 + low : 8 + high]
            + packed[:, :, 16 + low : 16 + high]
        )
        weight = jnp.exp2(lse - jnp.max(lse, axis=0, keepdims=True))
        share = weight / jnp.sum(weight, axis=0, keepdims=True)
        for k in range(high - low):
            cols = slice(k * DH, (k + 1) * DH)
            mixed = jnp.sum(recv[:, :, cols].astype(f32) * share[:, :, k : k + 1], axis=0)
            held[me_t, :, cols] = mixed.astype(bf16)
        gather_start(held, tok_sems.at[layer, 2 + group], *tok)

    def branch_of(layer, group):
        held = (oa_held, ob_held)[group].at[layer]
        finish(held, tok_sems.at[layer, 2 + group], *tok)
        low, high = spans[group]
        wide = (high - low) * DH
        whole = held[...].astype(f32).reshape(-1, wide).astype(bf16)
        return lax.dot_general(
            whole,
            wo[layer, :, low * DH : high * DH],
            (((1,), (1,)), ((), ())),
            preferred_element_type=f32,
        )

    def project(layer, before):
        mix_group(layer, 0)
        mix_group(layer, 1)
        branch = branch_of(layer, 0) + branch_of(layer, 1)
        send, recv, held = b_send.at[layer], b_recv.at[layer], s_held.at[layer]
        send[...] = branch.reshape(send.shape).astype(bf16)
        scatter_start(send, recv, head_sems.at[layer, 0], *head)
        recv[me] = send[me]
        finish(recv, head_sems.at[layer, 0], *head)
        total = jnp.sum(recv[...].astype(f32), axis=0)
        held[me] = (before[me].astype(f32) + total).astype(bf16)
        gather_start(held, head_sems.at[layer, 1], *head)
        finish(held, head_sems.at[layer, 1], *head)

    lse_s[...] = jnp.zeros(lse_s.shape, f32)
    for group in (0, 1):
        for g in range(*spans[group]):
            q = q_ref[:, g * DH : (g + 1) * DH]
            acc, top = soft(q, acc_s[g], top_s[g][:, :1], fk[...], fv[...], None)
            put_head(0, group, g, acc, top)
        send_group(0, group)

    spread[pl.ds(0, tokens, stride=2), :] = fk[...].astype(f32)
    spread[pl.ds(1, tokens, stride=2), :] = fv[...].astype(f32)
    pages[0:own_pages] = spread[0 : 2 * tokens, :].reshape(own_pages, -1, DH).astype(bf16)
    pages[own_pages:] = jnp.zeros((n_tok - own_pages, *pages.shape[1:]), bf16)
    shift = lax.div(home_ref[0], pages_here)

    def stage(peer, carry):
        which = lax.rem(peer - shift - own_pages * me_t + 2 * n_tok * own_pages, n_tok)
        outbox[peer] = pages[which]
        return carry

    lax.fori_loop(0, n_tok, stage, 0)
    scatter_start(outbox, inbox, page_sems, *tok)
    inbox[me_t] = outbox[me_t]

    project(0, state_ref)
    state = s_held[0].astype(f32).reshape(tokens, -1)
    sq = jnp.sum(state * state, axis=1, keepdims=True)
    scaled = (state * beam_gain_ref[...].astype(f32)).astype(bf16)
    share_q = jnp.dot(scaled, wq[...], preferred_element_type=f32)
    rows = tokens // n_tok
    q_send[:, :, :width] = share_q.reshape(n_tok, rows, width).astype(bf16)
    q_send[:, :, width:] = jnp.broadcast_to(sq, (tokens, DH)).reshape(n_tok, rows, DH).astype(bf16)
    scatter_start(q_send, q_recv, tok_sems.at[2, 0], *tok)
    q_recv[me_t] = q_send[me_t]
    finish(q_recv, tok_sems.at[2, 0], *tok)
    total = jnp.sum(q_recv[...].astype(f32), axis=0)
    scale = lax.rsqrt(total[:, width : width + 1] / D + EPSILON)
    ready = (total[:, :width] * scale).astype(bf16)
    cut = split_at * DH
    qa_held[me_t] = ready[:, :cut]
    gather_start(qa_held, tok_sems.at[2, 1], *tok)
    qb_held[me_t] = ready[:, cut:]
    gather_start(qb_held, tok_sems.at[2, 2], *tok)
    for group, held in ((0, qa_held), (1, qb_held)):
        finish(held, tok_sems.at[2, 1 + group], *tok)

        def one_head(g, carry, group=group, held=held):
            at = pl.multiple_of((g - spans[group][0]) * DH, DH)
            q = held[:, :, pl.ds(at, DH)].astype(f32).reshape(-1, DH).astype(bf16)
            acc, top = soft_old(q)
            acc, top = soft(q, acc, top, fk[...], fv[...], None)
            put_head(1, group, g, acc, top)
            return carry

        lax.fori_loop(*spans[group], one_head, 0)
        send_group(1, group)
    project(1, s_held.at[0])
    state_out_ref[...] = s_held[1]
    finish(inbox, page_sems, *tok)
    inbox_ref[...] = inbox[...]

    def drain(step, carry):
        for sub, way in lanes:
            sum_copy(step, sub, way).wait_send()
        return carry

    lax.fori_loop(0, n_head - 1, drain, 0)
    for way in (0, 1):
        for step in range(count[way]):
            for sub in range(subs2):
                share_copy(step, sub, way).wait_send()


def rest(
    n_tok,
    n_head,
    page_home,
    cache_len,
    attended,
    hidden,
    gain,
    q,
    state,
    beam_gain,
    weight_t,
    kvr,
    keys,
    values,
    wo,
    wq,
    subs=2,
    subs2=2,
    block=512,
):
    tokens, width = hidden.shape
    beams, cols = state.shape
    bf16, f32 = jnp.bfloat16, jnp.float32
    heads_here = width // DH
    split_at = (heads_here + 1) // 2
    wide_a, wide_b = split_at * DH, (heads_here - split_at) * DH
    rows = beams // n_tok
    state3 = state.reshape(n_head, beams // n_head, cols)
    pieces = (2, subs, tokens // 2 // subs, width)
    pieces2 = (2, subs2, tokens // subs2, 2 * DH)
    box = (n_tok, 2 * PAGE, DH)
    smem = pl.BlockSpec(memory_space=pltpu.SMEM)
    any_spec = pl.BlockSpec(memory_space=pl.ANY)
    vmem, dma = pltpu.VMEM, pltpu.SemaphoreType.DMA
    return pl.pallas_call(
        functools.partial(rest_kernel, n_tok, n_head, subs, subs2, block, split_at),
        out_shape=[
            jax.ShapeDtypeStruct(hidden.shape, bf16),
            jax.ShapeDtypeStruct(box, bf16),
            jax.ShapeDtypeStruct(state3.shape, bf16),
        ],
        in_specs=[smem] * 2 + [VMEM_SPEC] * 6 + [any_spec] * 6,
        out_specs=[VMEM_SPEC] * 3,
        scratch_shapes=[
            vmem((n_head, width, width), bf16),
            vmem((n_head, tokens, width), f32),
            vmem((n_head - 1, *pieces), bf16),
            vmem((n_head - 1, *pieces), bf16),
            vmem((n_head, tokens, 2 * DH), f32),
            vmem((n_head // 2, *pieces2), bf16),
            vmem((n_head // 2, *pieces2), bf16),
            vmem((n_head, 8, tokens), f32),
            vmem(kvr.shape, bf16),
            vmem((n_head, width, 2 * DH), bf16),
            vmem((2 * width, DH), f32),
            vmem(keys.shape, bf16),
            vmem(values.shape, bf16),
            vmem(wo.shape, bf16),
            vmem(wq.shape, bf16),
            vmem((1, keys.shape[0]), f32),
            vmem((heads_here, beams, 2 * DH), f32),
            vmem((heads_here, beams, DH), f32),
            vmem((tokens, DH), bf16),
            vmem((tokens, DH), bf16),
            vmem(box, bf16),
            vmem(box, bf16),
            vmem(box, bf16),
            vmem((beams, DH), f32),
            vmem((LAYERS, n_tok, rows, wide_a + DH), bf16),
            vmem((LAYERS, n_tok, rows, wide_b + DH), bf16),
            vmem((LAYERS, n_tok, rows, wide_a + DH), bf16),
            vmem((LAYERS, n_tok, rows, wide_b + DH), bf16),
            vmem((LAYERS, n_tok, rows, wide_a), bf16),
            vmem((LAYERS, n_tok, rows, wide_b), bf16),
            vmem((LAYERS, *state3.shape), bf16),
            vmem((LAYERS, *state3.shape), bf16),
            vmem((LAYERS, *state3.shape), bf16),
            vmem((n_tok, rows, width + DH), bf16),
            vmem((n_tok, rows, width + DH), bf16),
            vmem((n_tok, rows, wide_a), bf16),
            vmem((n_tok, rows, wide_b), bf16),
            dma((5,)),
            dma((n_head,)),
            dma((n_head - 1, 2, subs)),
            dma((n_head - 1, 2, subs)),
            dma((n_head // 2, 2, subs2)),
            dma((n_head // 2, 2, subs2)),
            dma((2,)),
            dma((2,)),
            dma((LAYERS + 1, 4, 2)),
            dma((LAYERS, 2, 2)),
        ],
        compiler_params=pltpu.CompilerParams(
            collective_id=2, has_side_effects=True, vmem_limit_bytes=56 << 20
        ),
        name="rest",
    )(
        page_home,
        cache_len,
        attended,
        hidden,
        gain[None, :],
        q,
        state3,
        beam_gain,
        weight_t,
        kvr,
        keys,
        values,
        wo,
        wq,
    )


def entry_kernel(
    n_tok,
    n_head,
    side,
    state_ref,
    gain_ref,
    wq_ref,
    query_ref,
    own_w,
    own_kv,
    kvw,
    cache,
    q_out_ref,
    att_ref,
    whole_w,
    kvr,
    keys_out,
    values_out,
    base_out,
    win,
    cache_v,
    keys,
    values,
    spread,
    q_send,
    q_recv,
    q_held,
    q_sems,
    w_sems,
    pair_sems,
    win_sems,
    kv_sems,
    kv_pair_sems,
    local_sems,
):
    me = lax.axis_index("tokens")
    me_h = lax.axis_index("heads")
    core = lax.rem(me, 2)
    y = lax.rem(me // 2, side)
    x = me // (2 * side)
    wide = n_tok // (2 * side)
    partner = me + 1 - 2 * core
    at = lambda i, j: (
        lax.rem(x + i + 2 * wide, wide) * side + lax.rem(y + j + 2 * side, side)
    ) * 2 + core
    cache_in = pltpu.make_async_copy(cache, cache_v, local_sems.at[3])
    cache_in.start()
    greet("tokens", n_tok, me)
    greet("heads", n_head, me_h)
    pl.semaphore_wait(pltpu.get_barrier_semaphore(), n_tok + n_head - 2)

    state = state_ref[...].astype(jnp.float32)
    squares = jnp.sum(state * state, axis=1, keepdims=True)
    scaled = (state * gain_ref[...].astype(jnp.float32)).astype(jnp.bfloat16)
    part = jnp.dot(scaled, wq_ref[...], preferred_element_type=jnp.float32)
    width = part.shape[1]
    rows = part.shape[0] // n_tok
    q_send[:, :, :width] = part.reshape(n_tok, rows, width).astype(jnp.bfloat16)
    q_send[:, :, width:] = (
        jnp.broadcast_to(squares, (part.shape[0], DH)).reshape(n_tok, rows, DH).astype(jnp.bfloat16)
    )
    scatter_start(q_send, q_recv, q_sems.at[0], "tokens", n_tok, me)
    q_recv[me] = q_send[me]

    def remote(src, dst, sems, target, axis="tokens"):
        return pltpu.make_async_remote_copy(
            src_ref=src,
            dst_ref=dst,
            send_sem=sems.at[0],
            recv_sem=sems.at[1],
            device_id={axis: target},
            device_id_type=MESH,
        )

    back = lambda b: lax.rem(me - b + n_tok, n_tok)
    ahead = lambda b: lax.rem(me + b, n_tok)
    win_two = remote(own_kv, win.at[2], win_sems.at[0], ahead(2))
    win_four = remote(own_kv, win.at[4], win_sems.at[1], ahead(4))
    win_two.start()
    win_four.start()

    depth = own_w.shape[0]
    piece = depth // 4
    block = lambda half, i, j: at(i, j) if half == 0 else at(j, i)

    def rows_of(half, part_at=None):
        if part_at is None:
            return pl.ds(half * 2 * piece, 2 * piece)
        return pl.ds((half * 2 + part_at) * piece, piece)

    slots = {}
    for half in (0, 1):
        for name in ("a+", "a-", "f+", "f-"):
            slots[half, name] = len(slots)
        for i in (0, -1, 1, 2):
            for name in ("a+", "a-", "f+", "f-"):
                slots[half, i, name] = len(slots)

    def first(half, name):
        way = 1 if name[1] == "+" else -1
        target = block(half, way, 0)
        if name[0] == "a":
            where = rows_of(half)
            return remote(
                own_w.at[where], whole_w.at[me, where], w_sems.at[slots[half, name]], target
            )
        ref = whole_w.at[block(half, -way, 0), rows_of(half, 0 if way == 1 else 1)]
        return remote(ref, ref, w_sems.at[slots[half, name]], target)

    def first_in(half, name):
        way = 1 if name[1] == "+" else -1
        if name[0] == "a":
            ref = whole_w.at[block(half, -way, 0), rows_of(half)]
        else:
            ref = whole_w.at[block(half, -2 * way, 0), rows_of(half, 0 if way == 1 else 1)]
        return remote(ref, ref, w_sems.at[slots[half, name]], block(half, way, 0))

    def second(half, i, name):
        way = 1 if name[1] == "+" else -1
        target = block(half, 0, way)
        if name[0] == "a":
            where = rows_of(half)
            dst = whole_w.at[block(half, i, 0), where]
            src = own_w.at[where] if i == 0 else dst
        else:
            src = dst = whole_w.at[block(half, i, -way), rows_of(half, 0 if way == 1 else 1)]
        return remote(src, dst, w_sems.at[slots[half, i, name]], target)

    def second_in(half, i, name):
        way = 1 if name[1] == "+" else -1
        if name[0] == "a":
            ref = whole_w.at[block(half, i, -way), rows_of(half)]
        else:
            ref = whole_w.at[block(half, i, -2 * way), rows_of(half, 0 if way == 1 else 1)]
        return remote(ref, ref, w_sems.at[slots[half, i, name]], block(half, 0, way))

    def share(half, i, j):
        where = rows_of(half)
        dst = whole_w.at[block(half, i, j), where]
        src = own_w.at[where] if (i, j) == (0, 0) else dst
        remote(src, dst, pair_sems, partner).start()

    halves = (0, 1)
    for half in halves:
        for name in ("a+", "a-"):
            first(half, name).start()
    for half in halves:
        for name in ("a+", "a-"):
            second(half, 0, name).start()
    for half in halves:
        share(half, 0, 0)

    kv_rows = kvw.shape[1] // 2
    kv_half = pl.ds(pl.multiple_of(core * kv_rows, kv_rows), kv_rows)

    def kv_out(k):
        target = lax.rem(me_h + k, n_head)
        return remote(
            kvw.at[target, kv_half], kvr.at[me_h, kv_half], kv_sems.at[k - 1], target, "heads"
        )

    def kv_in(k):
        ref = kvr.at[lax.rem(me_h - k + n_head, n_head), kv_half]
        return remote(ref, ref, kv_sems.at[k - 1], lax.rem(me_h + k, n_head), "heads")

    order = sorted(range(1, n_head), key=lambda k: min(k, n_head - k))
    for k in order:
        kv_out(k).start()

    own_copies = [
        pltpu.make_async_copy(own_w, whole_w.at[me], local_sems.at[0]),
        pltpu.make_async_copy(own_kv, win.at[0], local_sems.at[1]),
        pltpu.make_async_copy(kvw.at[me_h], kvr.at[me_h], local_sems.at[2]),
    ]
    for copy in own_copies:
        copy.start()

    finish(q_recv, q_sems.at[0], "tokens", n_tok, me)
    total = jnp.sum(q_recv[...].astype(jnp.float32), axis=0)
    factor = lax.rsqrt(total[:, width : width + 1] / D + EPSILON)
    q_held[me] = (total[:, :width] * factor).astype(jnp.bfloat16)
    gather_start(q_held, q_sems.at[1], "tokens", n_tok, me)

    own_copies[1].wait()
    cache_in.wait()
    base_copy = pltpu.make_async_copy(cache_v, base_out, local_sems.at[4])
    base_copy.start()
    parts = cache_v.shape[0] // spread.shape[0]

    def split(k):
        size = spread.shape[0]
        spread[...] = cache_v[k * size : (k + 1) * size, :].astype(jnp.float32)
        at = slice(k * size // 2, (k + 1) * size // 2)
        keys[at, :] = spread[pl.ds(0, size // 2, stride=2), :].astype(jnp.bfloat16)
        values[at, :] = spread[pl.ds(1, size // 2, stride=2), :].astype(jnp.bfloat16)

    def attend_window(g):
        cols = slice(g * DH, (g + 1) * DH)
        q = query_ref[:, cols]
        count = q.shape[0]
        acc = jnp.zeros((count, 2 * DH), jnp.float32)
        top = jnp.full((count, 1), -1e30, jnp.float32)
        row = lax.broadcasted_iota(jnp.int32, (count, count), 0)
        col = lax.broadcasted_iota(jnp.int32, (count, count), 1)
        ones = jnp.ones((count, DH), jnp.bfloat16)
        reach = win.shape[0]
        for b in range(reach):
            s = lax.dot_general(
                q, win[b, 0], (((1,), (1,)), ((), ())), preferred_element_type=jnp.float32
            )
            if b == 0:
                s = jnp.where(col <= row, s, -1e30)
            else:
                s = s + jnp.where(me >= b, jnp.float32(0.0), jnp.float32(-1e30))
            if b == reach - 1:
                s = jnp.where(col > row, s, -1e30)
            here = jnp.maximum(top, jnp.max(s, axis=1, keepdims=True))
            p = jnp.exp2((s - here) * SCALE2).astype(jnp.bfloat16)
            shrink = jnp.exp2((top - here) * SCALE2)
            both = jnp.concatenate([win[b, 1], ones], axis=1)
            acc = acc * shrink + jnp.dot(p, both, preferred_element_type=jnp.float32)
            top = here
        att_ref[:, cols] = (acc[:, :DH] / acc[:, DH:]).astype(jnp.bfloat16)

    early = [functools.partial(split, k) for k in range(parts)]
    late = [functools.partial(attend_window, g) for g in range(query_ref.shape[1] // DH)]

    def fill(work, amount=1):
        for _ in range(amount):
            if work:
                work.pop(0)()

    win_in = lambda b, k: remote(win.at[b], win.at[b], win_sems.at[k], partner)

    def relay(src, dst, k):
        return remote(win.at[src], win.at[dst], win_sems.at[k], partner)

    for name in ("a+", "a-"):
        way = 1 if name[1] == "+" else -1
        for half in halves:
            first_in(half, name).wait_recv()
            first(half, "f" + name[1]).start()
            for other in ("a+", "a-"):
                second(half, -way, other).start()
            share(half, -way, 0)
        fill(early)
    win_in(2, 0).wait_recv()
    relay(2 * core, 1, 2).start()
    for name in ("a+", "a-"):
        way = 1 if name[1] == "+" else -1
        for half in halves:
            second_in(half, 0, name).wait_recv()
            second(half, 0, "f" + name[1]).start()
            share(half, 0, -way)
        fill(early)
    for half in halves:
        first_in(half, "f+").wait_recv()
        first_in(half, "f-").wait_recv()
        for other in ("a+", "a-"):
            second(half, 2, other).start()
        share(half, 2, 0)
    win_in(4, 1).wait_recv()
    relay(2 + 2 * core, 3, 3).start()
    for i in (-1, 1):
        for name in ("a+", "a-"):
            way = 1 if name[1] == "+" else -1
            for half in halves:
                second_in(half, i, name).wait_recv()
                second(half, i, "f" + name[1]).start()
                share(half, i, -way)
            fill(early)
    fill(early, parts)
    keys_copy = pltpu.make_async_copy(keys, keys_out, local_sems.at[5])
    values_copy = pltpu.make_async_copy(values, values_out, local_sems.at[6])
    keys_copy.start()
    values_copy.start()
    win_in(1, 2).wait_recv()
    win_in(3, 3).wait_recv()
    finish(q_held, q_sems.at[1], "tokens", n_tok, me)
    q_out_ref[...] = q_held[...].astype(jnp.float32).reshape(-1, width).astype(jnp.bfloat16)

    def kv_share(k):
        ref = kvr.at[lax.rem(me_h - k + n_head, n_head), kv_half]
        return remote(ref, ref, kv_pair_sems.at[k - 1], partner)

    def kv_share_in(k):
        other = pl.ds(pl.multiple_of((1 - core) * kv_rows, kv_rows), kv_rows)
        ref = kvr.at[lax.rem(me_h - k + n_head, n_head), other]
        return remote(ref, ref, kv_pair_sems.at[k - 1], partner)

    for k in order[: n_head // 2]:
        kv_in(k).wait_recv()
        kv_share(k).start()
    fill(late)
    for half in halves:
        second_in(half, 0, "f+").wait_recv()
        second_in(half, 0, "f-").wait_recv()
        share(half, 0, 2)
    for name in ("a+", "a-"):
        way = 1 if name[1] == "+" else -1
        for half in halves:
            second_in(half, 2, name).wait_recv()
            second(half, 2, "f" + name[1]).start()
            share(half, 2, -way)
        fill(late)
    for i in (-1, 1, 2):
        for half in halves:
            second_in(half, i, "f+").wait_recv()
            second_in(half, i, "f-").wait_recv()
            share(half, i, 2)
        if i != 2:
            fill(late)
    fill(late, len(late))
    for k in order[n_head // 2 :]:
        kv_in(k).wait_recv()
        kv_share(k).start()

    relay(2 * core, 1, 2).wait_send()
    relay(2 + 2 * core, 3, 3).wait_send()
    win_two.wait_send()
    win_four.wait_send()
    for half in halves:
        for name in ("a+", "a-", "f+", "f-"):
            first(half, name).wait_send()
            for i in (0, -1, 1, 2):
                second(half, i, name).wait_send()
    for k in order:
        kv_out(k).wait_send()
        kv_share(k).wait_send()
        kv_share_in(k).wait_recv()
    half_of_all = whole_w.at[pl.ds(0, n_tok // 2)]
    remote(half_of_all, half_of_all, pair_sems, partner).wait()
    own_copies[0].wait()
    own_copies[2].wait()
    base_copy.wait()
    keys_copy.wait()
    values_copy.wait()


def entry(n_tok, n_head, state, gain, wq, queries, own_w, own_kv, kvw, cache, side=4):
    bf16 = jnp.bfloat16
    half_cache = (cache.shape[0] // 2, DH)
    beams = state.shape[0]
    width = wq.shape[1]
    rows = beams // n_tok
    any_spec = pl.BlockSpec(memory_space=pl.ANY)
    reach = WINDOW // own_kv.shape[1] + 1
    return pl.pallas_call(
        functools.partial(entry_kernel, n_tok, n_head, side),
        out_shape=[
            jax.ShapeDtypeStruct((beams, width), bf16),
            jax.ShapeDtypeStruct(queries.shape, bf16),
            jax.ShapeDtypeStruct((n_tok, *own_w.shape), bf16),
            jax.ShapeDtypeStruct(kvw.shape, bf16),
            jax.ShapeDtypeStruct(half_cache, bf16),
            jax.ShapeDtypeStruct(half_cache, bf16),
            jax.ShapeDtypeStruct(cache.shape, bf16),
        ],
        in_specs=[VMEM_SPEC] * 4 + [any_spec] * 4,
        out_specs=[VMEM_SPEC] * 2 + [any_spec] * 5,
        scratch_shapes=[
            pltpu.VMEM((reach, *own_kv.shape), bf16),
            pltpu.VMEM(cache.shape, bf16),
            pltpu.VMEM(half_cache, bf16),
            pltpu.VMEM(half_cache, bf16),
            pltpu.VMEM((cache.shape[0] // 8, DH), jnp.float32),
            pltpu.VMEM((n_tok, rows, width + DH), bf16),
            pltpu.VMEM((n_tok, rows, width + DH), bf16),
            pltpu.VMEM((n_tok, rows, width), bf16),
            pltpu.SemaphoreType.DMA((2, 2)),
            pltpu.SemaphoreType.DMA((40, 2)),
            pltpu.SemaphoreType.DMA((2,)),
            pltpu.SemaphoreType.DMA((4, 2)),
            pltpu.SemaphoreType.DMA((n_head - 1, 2)),
            pltpu.SemaphoreType.DMA((n_head - 1, 2)),
            pltpu.SemaphoreType.DMA((7,)),
        ],
        compiler_params=pltpu.CompilerParams(
            collective_id=1, has_side_effects=True, vmem_limit_bytes=24 << 20
        ),
        name="entry",
    )(state, gain, wq, queries, own_w, own_kv, kvw, cache)


def place_kernel(n_tok, own_pages, home_ref, base_ref, inbox_ref, out_ref, sem):
    me = lax.axis_index("tokens")
    rows = inbox_ref.shape[1]
    pages_here = out_ref.shape[0] // rows

    def each(act):
        def one(slot, carry):
            page = page_slot(home_ref, me, own_pages, pages_here, n_tok, slot)

            @pl.when(page >= 0)
            def _():
                at = pl.ds(pl.multiple_of(page * rows, rows), rows)
                act(pltpu.make_async_copy(inbox_ref.at[slot], out_ref.at[at], sem))

            return carry

        lax.fori_loop(0, n_tok, one, 0)

    each(lambda copy: copy.start())
    each(lambda copy: copy.wait())


def place_pages(n_tok, own_pages, page_home, base, inbox):
    return pl.pallas_call(
        functools.partial(place_kernel, n_tok, own_pages),
        out_shape=jax.ShapeDtypeStruct(base.shape, base.dtype),
        in_specs=[
            pl.BlockSpec(memory_space=pltpu.SMEM),
            pl.BlockSpec(memory_space=pl.ANY),
            VMEM_SPEC,
        ],
        out_specs=pl.BlockSpec(memory_space=pl.ANY),
        scratch_shapes=[pltpu.SemaphoreType.DMA],
        input_output_aliases={1: 0},
        name="place_pages",
    )(page_home, base, inbox)


def shards(
    hidden_in,
    queries,
    keyvals,
    out_weight,
    kv_gain,
    kv_weight,
    cache,
    page_home,
    cache_len,
    beam_state,
    parents,
    beam_gain,
    query_weight,
    beam_out_weight,
):
    n_tok = lax.axis_size("tokens")
    n_head = lax.axis_size("heads")
    state = jnp.take(beam_state, parents, axis=0)
    q, attended, weight_t, kvr, keys, values, base = entry(
        n_tok,
        n_head,
        state,
        beam_gain[0:1],
        query_weight[0],
        queries,
        out_weight.T,
        jnp.swapaxes(keyvals, 0, 1),
        kv_weight.reshape(n_head, -1, DH),
        cache.reshape(-1, DH),
    )
    stretch_hidden, inbox, beams_out = rest(
        n_tok,
        n_head,
        page_home,
        cache_len,
        attended,
        hidden_in,
        kv_gain,
        q,
        state,
        beam_gain[1:2],
        weight_t.reshape(-1, weight_t.shape[2]),
        kvr,
        keys,
        values,
        jnp.swapaxes(beam_out_weight, 1, 2),
        query_weight[1],
    )
    new_cache = place_pages(n_tok, hidden_in.shape[0] // PAGE, page_home, base, inbox)
    return (stretch_hidden, new_cache.reshape(cache.shape), beams_out.reshape(state.shape))


def solution(mesh):
    tokens = "tokens"
    placed = (
        P(tokens, "heads"),
        P(tokens, "heads"),
        P(tokens, None, "heads"),
        P("heads", tokens),
        P("heads"),
        P(None, None, "heads"),
        P(tokens, None, "heads"),
        P(),
        P(),
        P(None, tokens),
        P(),
        P(None, tokens),
        P(None, tokens, "heads"),
        P(None, "heads", tokens),
    )
    return jax.shard_map(
        shards,
        mesh=mesh,
        in_specs=placed,
        out_specs=(P(tokens, "heads"), P(tokens, None, "heads"), P(None, tokens)),
        check_vma=False,
    )
```

```python
import functools
import math

import jax
import jax.numpy as jnp
from jax import lax
from jax.experimental import pallas as pl
from jax.experimental.pallas import tpu as pltpu
from jax.sharding import PartitionSpec as P

D = 5120
DH = 128
WINDOW = 1024
PAGE = 16
LAYERS = 2
EPSILON = 1e-06
SCALE = DH ** (-0.5)
SCALE2 = SCALE * math.log2(math.e)
MESH = pl.DeviceIdType.MESH
VMEM_SPEC = pl.BlockSpec(memory_space=pltpu.VMEM)


def scatter_start(send, recv, sems, axis, count, me):
    def one(step, carry):
        peer = lax.rem(me + step, count)
        pltpu.make_async_remote_copy(
            src_ref=send.at[peer],
            dst_ref=recv.at[me],
            send_sem=sems.at[0],
            recv_sem=sems.at[1],
            device_id={axis: peer},
            device_id_type=MESH,
        ).start()
        return carry

    lax.fori_loop(1, count, one, 0)


def gather_start(held, sems, axis, count, me):
    def one(step, carry):
        peer = lax.rem(me + step, count)
        pltpu.make_async_remote_copy(
            src_ref=held.at[me],
            dst_ref=held.at[me],
            send_sem=sems.at[0],
            recv_sem=sems.at[1],
            device_id={axis: peer},
            device_id_type=MESH,
        ).start()
        return carry

    lax.fori_loop(1, count, one, 0)


def finish(held, sems, axis, count, me):
    everything = held.at[pl.ds(0, count - 1)]
    pltpu.make_async_remote_copy(
        src_ref=everything,
        dst_ref=everything,
        send_sem=sems.at[0],
        recv_sem=sems.at[1],
        device_id={axis: lax.rem(me + 1, count)},
        device_id_type=MESH,
    ).wait()


def greet(axis, count, me):
    barrier = pltpu.get_barrier_semaphore()

    def one(step, carry):
        pl.semaphore_signal(
            barrier, inc=1, device_id={axis: lax.rem(me + step, count)}, device_id_type=MESH
        )
        return carry

    lax.fori_loop(1, count, one, 0)


def page_slot(home_ref, me, own_pages, pages_here, n_tok, slot):
    shift = lax.div(home_ref[0], pages_here)
    which = lax.rem(me - shift - own_pages * slot + 2 * n_tok * own_pages, n_tok)
    page = home_ref[own_pages * slot + jnp.minimum(which, own_pages - 1)]
    return jnp.where(which < own_pages, lax.rem(page, pages_here), -1)


def whole_kernel(
    n_tok,
    n_head,
    side,
    subs,
    subs2,
    block,
    split_at,
    home_hbm,
    len_hbm,
    parents_hbm,
    query_hbm,
    hid_hbm,
    gain_hbm,
    beams_hbm,
    beam_gain_hbm,
    own_w,
    own_kv,
    kvw,
    cache,
    wo_hbm,
    wq_hbm,
    hid_out_hbm,
    inbox_hbm,
    state_out_hbm,
    state_end,
    hid_out_ref,
    home_ref,
    len_ref,
    parents_ref,
    query_ref,
    hid_ref,
    gain_ref,
    beams_ref,
    beam_gain_ref,
    whole_w,
    win,
    win_k,
    win_v,
    att,
    state_ref,
    cache_v,
    part,
    s_buf,
    r_buf,
    part2,
    s_buf2,
    r_buf2,
    squares,
    kvr,
    kvd,
    spread,
    keys,
    values,
    wo,
    wq,
    bias,
    acc_s,
    top_s,
    fk,
    fv,
    pages,
    outbox,
    inbox,
    lse_s,
    oa_send,
    ob_send,
    oa_recv,
    ob_recv,
    oa_held,
    ob_held,
    b_send,
    b_recv,
    s_held,
    q_send,
    q_recv,
    qa_held,
    qb_held,
    q0_held,
    local_sems,
    in_sems,
    w_sems,
    pair_sems,
    win_sems,
    kv_sems,
    kv_pair_sems,
    s_sems,
    r_sems,
    s_sems2,
    r_sems2,
    sq_sems,
    page_sems,
    tok_sems,
    head_sems,
):
    f32, bf16 = jnp.float32, jnp.bfloat16
    me = lax.axis_index("tokens")
    me_h = lax.axis_index("heads")
    tok = ("tokens", n_tok, me)
    head = ("heads", n_head, me_h)
    core = lax.rem(me, 2)
    y = lax.rem(me // 2, side)
    x = me // (2 * side)
    wide = n_tok // (2 * side)
    partner = me + 1 - 2 * core
    at = lambda i, j: (
        lax.rem(x + i + 2 * wide, wide) * side + lax.rem(y + j + 2 * side, side)
    ) * 2 + core
    cache_in = pltpu.make_async_copy(cache, cache_v, local_sems.at[3])
    wq_in = pltpu.make_async_copy(wq_hbm, wq, local_sems.at[0])
    wo_in = pltpu.make_async_copy(
        wo_hbm, wo.at[:, pl.ds(0, wo_hbm.shape[1])], local_sems.at[4]
    )
    small_in = [
        pltpu.make_async_copy(src, dst, in_sems.at[k])
        for k, (src, dst) in enumerate(
            [
                (parents_hbm, parents_ref),
                (beams_hbm, beams_ref.at[pl.ds(0, beams_hbm.shape[0])]),
                (beam_gain_hbm, beam_gain_ref),
                (home_hbm, home_ref),
                (len_hbm, len_ref),
                (query_hbm, query_ref),
                (hid_hbm, hid_ref),
                (gain_hbm, gain_ref),
            ]
        )
    ]
    for copy in small_in[:3]:
        copy.start()
    wq_in.start()
    for copy in small_in[3:]:
        copy.start()
    cache_in.start()
    wo_in.start()
    greet(*tok)
    greet(*head)

    tokens, width = hid_ref.shape
    beams = beams_hbm.shape[1]
    beams_ref[beams_hbm.shape[0] :] = jnp.zeros((beams_ref.shape[0] - beams_hbm.shape[0], beams), bf16)
    wo[:, wo_hbm.shape[1] :] = jnp.zeros((LAYERS, wo.shape[1] - wo_hbm.shape[1], width), bf16)
    source = lax.broadcasted_iota(jnp.int32, (beams, beams), 0)
    for copy in small_in[:3]:
        copy.wait()
    picked = jnp.transpose(jnp.where(source == parents_ref[...], 1.0, 0.0).astype(f32))
    picked = picked.astype(bf16)
    cols = wq.shape[1]
    extra = cols - DH
    strips = DH // extra

    def both_of(lhs, ref, lead):
        first = ref[lead, :DH] if lead is not None else ref[:DH]
        other = ref[lead, DH:] if lead is not None else ref[DH:]
        dims = (((1,), (1,)), ((), ()))
        return (
            lax.dot_general(lhs, first, dims, preferred_element_type=f32),
            lax.dot_general(lhs, other, dims, preferred_element_type=f32),
        )

    def pack(ref, main, rest):
        high = beams // n_head
        ref[:, :high, :] = main.reshape(n_head, high, DH).astype(bf16)
        strip = rest.reshape(n_head, strips, high // strips, DH)
        total = strip[:, 0]
        for k in range(1, strips):
            total = total + pltpu.roll(strip[:, k], k * extra, 2)
        ref[:, high:, :] = total.astype(bf16)

    def unpack(value):
        high = beams // n_head
        main = value[:, :high].reshape(beams, DH)
        strip = value[:, high:]
        inside = lax.broadcasted_iota(jnp.int32, strip.shape, 2) < extra
        parts = [
            jnp.where(inside, pltpu.roll(strip, (DH - k * extra) % DH, 2), 0.0)
            for k in range(strips)
        ]
        return main, jnp.stack(parts, axis=1).reshape(beams, DH)

    state = both_of(picked, beams_ref, None)
    pack(state_ref, *state)
    wq_in.wait()

    def send_query(layer, state):
        main, rest = state
        sq = jnp.sum(main * main + rest * rest, axis=1, keepdims=True)
        gain = beam_gain_ref[layer : layer + 1, :].astype(f32)
        share_q = jnp.dot(
            (main * gain[:, :DH]).astype(bf16), wq[layer, :DH], preferred_element_type=f32
        ) + jnp.dot(
            (rest[:, :extra] * gain[:, DH:]).astype(bf16), wq[layer, DH:], preferred_element_type=f32
        )
        rows = beams // n_tok
        q_send[layer, :, :, :width] = share_q.reshape(n_tok, rows, width).astype(bf16)
        q_send[layer, :, :, width:] = (
            jnp.broadcast_to(sq, (beams, DH)).reshape(n_tok, rows, DH).astype(bf16)
        )
        return lambda: scatter_start(q_send.at[layer], q_recv.at[layer], tok_sems.at[2 + layer, 0], *tok)

    def sum_query(layer):
        recv = q_recv.at[layer]
        recv[me] = q_send[layer, me]
        finish(recv, tok_sems.at[2 + layer, 0], *tok)
        total = jnp.sum(recv[...].astype(f32), axis=0)
        scale = lax.rsqrt(total[:, width : width + 1] / D + EPSILON)
        return (total[:, :width] * scale).astype(bf16)

    start_query = send_query(0, state)

    cache_rows = keys.shape[0]
    pages_here = cache_rows // PAGE
    own_pages = tokens // PAGE
    lane = lax.broadcasted_iota(jnp.int32, (1, cache_rows), 1)
    for copy in small_in[3:]:
        copy.wait()
    kept = (me * cache_rows + lane) < len_ref[0]
    page_of = lane // PAGE
    for slot in range(n_tok):
        landing = page_slot(home_ref, me, own_pages, pages_here, n_tok, slot)
        kept = kept & (page_of != landing)
    bias[...] = jnp.where(kept, 0.0, -1e30).astype(f32)

    pl.semaphore_wait(pltpu.get_barrier_semaphore(), n_tok + n_head - 2)
    start_query()

    def remote(src, dst, sems, target, axis="tokens"):
        return pltpu.make_async_remote_copy(
            src_ref=src,
            dst_ref=dst,
            send_sem=sems.at[0],
            recv_sem=sems.at[1],
            device_id={axis: target},
            device_id_type=MESH,
        )

    back = lambda b: lax.rem(me - b + n_tok, n_tok)
    ahead = lambda b: lax.rem(me + b, n_tok)
    win_two = remote(own_kv, win.at[2], win_sems.at[0], ahead(2))
    win_four = remote(own_kv, win.at[4], win_sems.at[1], ahead(4))
    win_two.start()
    win_four.start()

    depth = own_w.shape[0]
    cut_w = depth * 2 // 5
    spot = lambda half, i, j: at(i, j) if half == 0 else at(j, i)

    def rows_of(half, stage=None, part_at=None):
        begin, size = (0, cut_w) if half == 0 else (cut_w, depth - cut_w)
        if part_at is None:
            return pl.ds(begin, size)
        up = size // 2 if half == stage else 16
        return pl.ds(begin, up) if part_at == 0 else pl.ds(begin + up, size - up)

    slots = {}
    for half in (0, 1):
        for name in ("a+", "a-", "f+", "f-"):
            slots[half, name] = len(slots)
        for i in (0, -1, 1, 2):
            for name in ("a+", "a-", "f+", "f-"):
                slots[half, i, name] = len(slots)

    def first(half, name):
        way = 1 if name[1] == "+" else -1
        target = spot(half, way, 0)
        if name[0] == "a":
            where = rows_of(half)
            return remote(
                own_w.at[where], whole_w.at[me, where], w_sems.at[slots[half, name]], target
            )
        ref = whole_w.at[spot(half, -way, 0), rows_of(half, 0, 0 if way == 1 else 1)]
        return remote(ref, ref, w_sems.at[slots[half, name]], target)

    def first_in(half, name):
        way = 1 if name[1] == "+" else -1
        if name[0] == "a":
            ref = whole_w.at[spot(half, -way, 0), rows_of(half)]
        else:
            ref = whole_w.at[spot(half, -2 * way, 0), rows_of(half, 0, 0 if way == 1 else 1)]
        return remote(ref, ref, w_sems.at[slots[half, name]], spot(half, way, 0))

    def second(half, i, name):
        way = 1 if name[1] == "+" else -1
        target = spot(half, 0, way)
        if name[0] == "a":
            where = rows_of(half)
            dst = whole_w.at[spot(half, i, 0), where]
            src = own_w.at[where] if i == 0 else dst
        else:
            src = dst = whole_w.at[spot(half, i, -way), rows_of(half, 1, 0 if way == 1 else 1)]
        return remote(src, dst, w_sems.at[slots[half, i, name]], target)

    def second_in(half, i, name):
        way = 1 if name[1] == "+" else -1
        if name[0] == "a":
            ref = whole_w.at[spot(half, i, -way), rows_of(half)]
        else:
            ref = whole_w.at[spot(half, i, -2 * way), rows_of(half, 1, 0 if way == 1 else 1)]
        return remote(ref, ref, w_sems.at[slots[half, i, name]], spot(half, 0, way))

    def share(half, i, j):
        where = rows_of(half)
        dst = whole_w.at[spot(half, i, j), where]
        src = own_w.at[where] if (i, j) == (0, 0) else dst
        remote(src, dst, pair_sems, partner).start()

    halves = (0, 1)
    for half in halves:
        for name in ("a+", "a-"):
            first(half, name).start()
    for half in halves:
        for name in ("a+", "a-"):
            second(half, 0, name).start()
    for half in halves:
        share(half, 0, 0)

    kv_rows = kvw.shape[1] // 2
    kv_half = pl.ds(pl.multiple_of(core * kv_rows, kv_rows), kv_rows)

    def kv_out(k):
        target = lax.rem(me_h + k, n_head)
        return remote(
            kvw.at[target, kv_half], kvr.at[me_h, kv_half], kv_sems.at[k - 1], target, "heads"
        )

    def kv_in(k):
        ref = kvr.at[lax.rem(me_h - k + n_head, n_head), kv_half]
        return remote(ref, ref, kv_sems.at[k - 1], lax.rem(me_h + k, n_head), "heads")

    order = sorted(range(1, n_head), key=lambda k: min(k, n_head - k))
    for k in order:
        kv_out(k).start()

    own_copies = [
        pltpu.make_async_copy(own_w, whole_w.at[me], local_sems.at[5]),
        pltpu.make_async_copy(own_kv, win.at[0], local_sems.at[1]),
        pltpu.make_async_copy(kvw.at[me_h], kvr.at[me_h], local_sems.at[2]),
    ]
    for copy in own_copies:
        copy.start()

    own_copies[1].wait()
    cache_in.wait()
    size = cache_rows // 4
    parts = cache_v.shape[0] // size

    def split(k):
        spread[0:size, :] = cache_v[k * size : (k + 1) * size, :].astype(jnp.float32)
        at = slice(k * size // 2, (k + 1) * size // 2)
        keys[at, :] = spread[pl.ds(0, size // 2, stride=2), :].astype(jnp.bfloat16)
        values[at, :] = spread[pl.ds(1, size // 2, stride=2), :].astype(jnp.bfloat16)

    def split_window(b):
        spread[0 : 2 * tokens, :] = win[b].astype(f32)
        win_k[b] = spread[pl.ds(0, tokens, stride=2), :].astype(bf16)
        win_v[b] = spread[pl.ds(1, tokens, stride=2), :].astype(bf16)

    def attend_window(g):
        cols = slice(g * DH, (g + 1) * DH)
        q = query_ref[:, cols]
        count = q.shape[0]
        acc = jnp.zeros((count, 2 * DH), jnp.float32)
        top = jnp.full((count, 1), -1e30, jnp.float32)
        row = lax.broadcasted_iota(jnp.int32, (count, count), 0)
        col = lax.broadcasted_iota(jnp.int32, (count, count), 1)
        ones = jnp.ones((count, DH), jnp.bfloat16)
        reach = win.shape[0]
        for b in range(reach):
            s = lax.dot_general(
                q, win_k[b], (((1,), (1,)), ((), ())), preferred_element_type=jnp.float32
            )
            if b == 0:
                s = jnp.where(col <= row, s, -1e30)
            else:
                s = s + jnp.where(me >= b, jnp.float32(0.0), jnp.float32(-1e30))
            if b == reach - 1:
                s = jnp.where(col > row, s, -1e30)
            here = jnp.maximum(top, jnp.max(s, axis=1, keepdims=True))
            p = jnp.exp2((s - here) * SCALE2).astype(jnp.bfloat16)
            shrink = jnp.exp2((top - here) * SCALE2)
            both = jnp.concatenate([win_v[b], ones], axis=1)
            acc = acc * shrink + jnp.dot(p, both, preferred_element_type=jnp.float32)
            top = here
        att[:, cols] = (acc[:, :DH] / acc[:, DH:]).astype(jnp.bfloat16)

    def soft(q, acc, top, keys_b, values_b, bias_b):
        s = lax.dot_general(q, keys_b, (((1,), (1,)), ((), ())), preferred_element_type=f32)
        if bias_b is not None:
            s = s + bias_b
        here = jnp.maximum(top, jnp.max(s, axis=1, keepdims=True))
        p = jnp.exp2((s - here) * SCALE2).astype(bf16)
        shrink = jnp.exp2((top - here) * SCALE2)
        both = jnp.concatenate([values_b, jnp.ones_like(values_b)], axis=1)
        return acc * shrink + jnp.dot(p, both, preferred_element_type=f32), here

    def head_of(held, g):
        at = pl.multiple_of(g * DH, DH)
        return held[:, :, pl.ds(at, DH)].astype(f32).reshape(-1, DH).astype(bf16)

    def soft_old(q):
        acc = jnp.zeros((q.shape[0], 2 * DH), f32)
        top = jnp.full((q.shape[0], 1), -1e30, f32)
        for b in range(cache_rows // block):
            at = slice(b * block, (b + 1) * block)
            acc, top = soft(q, acc, top, keys[at, :], values[at, :], bias[:, at])
        return acc, top

    heads_here = width // DH
    third = -(-heads_here // 3)
    old_spans = {-1: (0, third), 1: (third, 2 * third), 2: (2 * third, heads_here)}
    early = [functools.partial(split, k) for k in range(parts)]
    late = [functools.partial(attend_window, g) for g in range(query_ref.shape[1] // DH)]

    def fill(work, amount=1):
        for _ in range(amount):
            if work:
                work.pop(0)()

    win_in = lambda b, k: remote(win.at[b], win.at[b], win_sems.at[k], partner)

    def relay(src, dst, k):
        return remote(win.at[src], win.at[dst], win_sems.at[k], partner)

    for name in ("a+", "a-"):
        way = 1 if name[1] == "+" else -1
        for half in halves:
            first_in(half, name).wait_recv()
            first(half, "f" + name[1]).start()
            for other in ("a+", "a-"):
                second(half, -way, other).start()
            share(half, -way, 0)
        fill(early)
    q0_held[me] = sum_query(0)
    gather_start(q0_held, tok_sems.at[2, 1], *tok)
    win_in(2, 0).wait_recv()
    relay(2 * core, 1, 2).start()
    for name in ("a+", "a-"):
        way = 1 if name[1] == "+" else -1
        for half in halves:
            second_in(half, 0, name).wait_recv()
            second(half, 0, "f" + name[1]).start()
            share(half, 0, -way)
        fill(early)
    for half in halves:
        first_in(half, "f+").wait_recv()
        first_in(half, "f-").wait_recv()
        for other in ("a+", "a-"):
            second(half, 2, other).start()
        share(half, 2, 0)
    win_in(4, 1).wait_recv()
    relay(2 + 2 * core, 3, 3).start()
    for i in (-1, 1):
        for name in ("a+", "a-"):
            way = 1 if name[1] == "+" else -1
            for half in halves:
                second_in(half, i, name).wait_recv()
                second(half, i, "f" + name[1]).start()
                share(half, i, -way)
            fill(early)
    fill(early, parts)
    win_in(1, 2).wait_recv()
    win_in(3, 3).wait_recv()
    for b in range(win.shape[0]):
        split_window(b)
    def kv_share(k):
        ref = kvr.at[lax.rem(me_h - k + n_head, n_head), kv_half]
        return remote(ref, ref, kv_pair_sems.at[k - 1], partner)

    def kv_share_in(k):
        other = pl.ds(pl.multiple_of((1 - core) * kv_rows, kv_rows), kv_rows)
        ref = kvr.at[lax.rem(me_h - k + n_head, n_head), other]
        return remote(ref, ref, kv_pair_sems.at[k - 1], partner)

    fill(late)
    for half in halves:
        second_in(half, 0, "f+").wait_recv()
        second_in(half, 0, "f-").wait_recv()
        share(half, 0, 2)
    for name in ("a+", "a-"):
        way = 1 if name[1] == "+" else -1
        for half in halves:
            second_in(half, 2, name).wait_recv()
            second(half, 2, "f" + name[1]).start()
            share(half, 2, -way)
        fill(late)
    for i in (-1, 1, 2):
        for half in halves:
            second_in(half, i, "f+").wait_recv()
            second_in(half, i, "f-").wait_recv()
            share(half, i, 2)
        if i == -1:
            fill(late, len(late))
            finish(q0_held, tok_sems.at[2, 1], *tok)
        low, high = old_spans[i]

        def old_head(g, carry):
            acc, top = soft_old(head_of(q0_held, g))
            acc_s[g] = acc
            top_s[g] = jnp.broadcast_to(top, (beams, DH))
            return carry

        lax.fori_loop(low, high, old_head, 0)
    half_of_all = whole_w.at[pl.ds(0, n_tok // 2)]
    pair_all = remote(half_of_all, half_of_all, pair_sems, partner)
    pair_all.wait_recv()
    own_copies[0].wait()

    heads_here = width // DH
    half_rows = tokens // 2
    middle = n_head // 2
    rows_sub = half_rows // subs
    rows_sub2 = tokens // subs2
    wrap = lambda value: lax.rem(value + 2 * n_head, n_head)
    lanes = [(sub, way) for sub in range(subs) for way in (0, 1)]
    sign = (1, -1)
    at_rows = lambda sub, way: slice(way * half_rows + sub * rows_sub, way * half_rows + (sub + 1) * rows_sub)

    def product(c):
        per = n_tok // n_head
        w = whole_w[pl.ds(c * per, per)].reshape(width, width)
        part[c] = lax.dot_general(
            att[...], w, (((1,), (1,)), ((), ())), preferred_element_type=f32
        )

    def sum_copy(step, sub, way):
        return pltpu.make_async_remote_copy(
            src_ref=s_buf.at[step, way, sub],
            dst_ref=r_buf.at[step, way, sub],
            send_sem=s_sems.at[step, way, sub],
            recv_sem=r_sems.at[step, way, sub],
            device_id={"heads": wrap(me_h + sign[way])},
            device_id_type=MESH,
        )

    def spread_kv(c):
        count = width
        spread[0 : 2 * count, :] = kvr[c].astype(f32)
        kvd[c, :, :DH] = spread[pl.ds(0, count, stride=2), :].astype(bf16)
        kvd[c, :, DH:] = spread[pl.ds(1, count, stride=2), :].astype(bf16)

    product(wrap(me_h - 1))
    product(wrap(me_h + 1))

    def work(step, slot):
        if slot < 2:

            @pl.when(step < middle - 1)
            def _():
                if slot == 0:
                    product(wrap(me_h - 2 - step))
                else:
                    product(lax.select(step == middle - 2, me_h, wrap(me_h + 2 + step)))

            @pl.when(step >= n_head - 3)
            def _():
                spread_kv((step - (n_head - 3)) * 4 + slot * 2)
                spread_kv((step - (n_head - 3)) * 4 + slot * 2 + 1)

    def reduce_step(step, carry):
        for sub in range(subs):
            for way in (0, 1):
                c = wrap(me_h - sign[way] * (1 + step))
                own = part[c, at_rows(sub, way), :]

                @pl.when(step == 0)
                def _():
                    s_buf[step, way, sub] = own.astype(bf16)

                @pl.when(step > 0)
                def _():
                    sum_copy(step - 1, sub, way).wait_recv()
                    s_buf[step, way, sub] = (
                        own + r_buf[step - 1, way, sub].astype(f32)
                    ).astype(bf16)

                sum_copy(step, sub, way).start()
            if sub == 0:

                @pl.when(step == n_head - 3)
                def _():
                    for k in order:
                        kv_share_in(k).wait_recv()
                    own_copies[2].wait()

            for slot in range(sub * 2 // subs, (sub + 1) * 2 // subs):
                work(step, slot)

        @pl.when(step == middle - 1)
        def _():
            for k in order:
                kv_in(k).wait_recv()
                kv_share(k).start()

        return carry

    lax.fori_loop(0, n_head - 1, reduce_step, 0)

    last = n_head - 2
    for sub, way in lanes:
        rows = at_rows(sub, way)
        sum_copy(last, sub, way).wait_recv()
        total = part[me_h, rows, :] + r_buf[last, way, sub].astype(f32)
        hid_out_ref[rows, :] = (hid_ref[rows, :].astype(f32) + total).astype(bf16)

    hid_out = pltpu.make_async_copy(hid_out_ref, hid_out_hbm, local_sems.at[0])
    hid_out.start()

    hidden = hid_out_ref[...].astype(f32)
    scaled = (hidden * gain_ref[...].astype(f32)).astype(bf16)

    def product2(c):
        part2[c] = jnp.dot(scaled, kvd[c], preferred_element_type=f32)

    count = (middle, n_head - 1 - middle)

    def chunk(step, way):
        return wrap(me_h + middle - step) if way == 0 else wrap(me_h - count[1] + step)

    def share_copy(step, sub, way):
        return pltpu.make_async_remote_copy(
            src_ref=s_buf2.at[step, way, sub],
            dst_ref=r_buf2.at[step, way, sub],
            send_sem=s_sems2.at[step, way, sub],
            recv_sem=r_sems2.at[step, way, sub],
            device_id={"heads": wrap(me_h + sign[way])},
            device_id_type=MESH,
        )

    product2(chunk(0, 0))
    product2(chunk(0, 1))
    for step in range(middle):
        for sub in range(subs2):
            rows = slice(sub * rows_sub2, (sub + 1) * rows_sub2)
            for way in (0, 1):
                if step >= count[way]:
                    continue
                value = part2[chunk(step, way), rows, :]
                if step:
                    share_copy(step - 1, sub, way).wait_recv()
                    value = value + r_buf2[step - 1, way, sub].astype(f32)
                s_buf2[step, way, sub] = value.astype(bf16)
                share_copy(step, sub, way).start()
        if step == 0:
            flat = (hidden * hidden).astype(bf16)
            ones = jnp.ones((8, width), bf16)
            squares[me_h] = lax.dot_general(
                ones, flat, (((1,), (1,)), ((), ())), preferred_element_type=f32
            )
            gather_start(squares, sq_sems, *head)
        for way in (0, 1):
            if step + 1 < count[way]:
                product2(chunk(step + 1, way))
        if step == middle - 1:
            product2(me_h)
    finish(squares, sq_sems, *head)
    mean = jnp.transpose(jnp.sum(squares[...], axis=0))[:, :1] / D
    factor = lax.rsqrt(mean + EPSILON)
    for sub in range(subs2):
        rows = slice(sub * rows_sub2, (sub + 1) * rows_sub2)
        total = part2[me_h, rows, :]
        for way in (0, 1):
            share_copy(count[way] - 1, sub, way).wait_recv()
            total = total + r_buf2[count[way] - 1, way, sub].astype(f32)
        fresh = total * factor[rows]
        fk[rows, :] = fresh[:, :DH].astype(bf16)
        fv[rows, :] = fresh[:, DH:].astype(bf16)

    lane8 = lax.broadcasted_iota(jnp.int32, (tokens, DH), 1)
    sends = (oa_send, ob_send)
    spans = ((0, split_at), (split_at, heads_here))

    def put_head(layer, group, g, acc, top):
        amount = acc[:, DH:]
        out = (acc[:, :DH] / amount).reshape(n_tok, -1, DH).astype(bf16)
        at = pl.multiple_of((g - spans[group][0]) * DH, DH)
        sends[group][layer, :, :, pl.ds(at, DH)] = out
        value = top * SCALE2 + jnp.log2(amount)
        mine = (lane8 % 8 == g) & (lane8 < 24)
        lse_s[...] = jnp.where(mine, value, lse_s[...])

    def send_group(layer, group):
        value = lse_s[...]
        high = value.astype(bf16).astype(f32)
        mid = (value - high).astype(bf16).astype(f32)
        low = value - high - mid
        packed = jnp.where(lane8 < 8, high, jnp.where(lane8 < 16, mid, low))
        wide = (spans[group][1] - spans[group][0]) * DH
        sends[group][layer, :, :, wide:] = packed.reshape(n_tok, -1, DH).astype(bf16)
        recv = (oa_recv, ob_recv)[group].at[layer]
        scatter_start(sends[group].at[layer], recv, tok_sems.at[layer, group], *tok)

    def mix_group(layer, group):
        recv = (oa_recv, ob_recv)[group].at[layer]
        held = (oa_held, ob_held)[group].at[layer]
        low, high = spans[group]
        wide = (high - low) * DH
        recv[me] = sends[group][layer, me]
        finish(recv, tok_sems.at[layer, group], *tok)
        packed = recv[:, :, wide:].astype(f32)
        lse = (
            packed[:, :, low:high]
            + packed[:, :, 8 + low : 8 + high]
            + packed[:, :, 16 + low : 16 + high]
        )
        weight = jnp.exp2(lse - jnp.max(lse, axis=0, keepdims=True))
        share = weight / jnp.sum(weight, axis=0, keepdims=True)
        for k in range(high - low):
            cols = slice(k * DH, (k + 1) * DH)
            mixed = jnp.sum(recv[:, :, cols].astype(f32) * share[:, :, k : k + 1], axis=0)
            held[me, :, cols] = mixed.astype(bf16)
        gather_start(held, tok_sems.at[layer, 2 + group], *tok)

    def branch_of(layer, group):
        held = (oa_held, ob_held)[group].at[layer]
        finish(held, tok_sems.at[layer, 2 + group], *tok)
        low, high = spans[group]
        wide = (high - low) * DH
        whole = held[...].astype(f32).reshape(-1, wide).astype(bf16)
        return both_of(whole, wo.at[:, :, pl.ds(low * DH, wide)], layer)

    def project(layer, before):
        mix_group(layer, 0)
        mix_group(layer, 1)
        one, two = branch_of(layer, 0), branch_of(layer, 1)
        send, recv, held = b_send.at[layer], b_recv.at[layer], s_held.at[layer]
        pack(send, one[0] + two[0], one[1] + two[1])
        scatter_start(send, recv, head_sems.at[layer, 0], *head)
        recv[me_h] = send[me_h]
        finish(recv, head_sems.at[layer, 0], *head)
        total = jnp.sum(recv[...].astype(f32), axis=0)
        held[me_h] = (before[me_h].astype(f32) + total).astype(bf16)
        gather_start(held, head_sems.at[layer, 1], *head)
        finish(held, head_sems.at[layer, 1], *head)

    lse_s[...] = jnp.zeros(lse_s.shape, f32)
    for group in (0, 1):
        for g in range(*spans[group]):
            acc, top = soft(head_of(q0_held, g), acc_s[g], top_s[g][:, :1], fk[...], fv[...], None)
            put_head(0, group, g, acc, top)
        send_group(0, group)

    spread[pl.ds(0, tokens, stride=2), :] = fk[...].astype(f32)
    spread[pl.ds(1, tokens, stride=2), :] = fv[...].astype(f32)
    pages[0:own_pages] = spread[0 : 2 * tokens, :].reshape(own_pages, -1, DH).astype(bf16)
    pages[own_pages:] = jnp.zeros((n_tok - own_pages, *pages.shape[1:]), bf16)
    shift = lax.div(home_ref[0], pages_here)

    def stage(peer, carry):
        which = lax.rem(peer - shift - own_pages * me + 2 * n_tok * own_pages, n_tok)
        outbox[peer] = pages[which]
        return carry

    lax.fori_loop(0, n_tok, stage, 0)
    scatter_start(outbox, inbox, page_sems, *tok)
    inbox[me] = outbox[me]

    wo_in.wait()
    project(0, state_ref)
    send_query(1, unpack(s_held[0].astype(f32)))()
    ready = sum_query(1)
    cut = split_at * DH
    qa_held[me] = ready[:, :cut]
    gather_start(qa_held, tok_sems.at[3, 1], *tok)
    qb_held[me] = ready[:, cut:]
    gather_start(qb_held, tok_sems.at[3, 2], *tok)
    for group, held in ((0, qa_held), (1, qb_held)):
        finish(held, tok_sems.at[3, 1 + group], *tok)

        def one_head(g, carry, group=group, held=held):
            q = head_of(held, g - spans[group][0])
            acc, top = soft_old(q)
            acc, top = soft(q, acc, top, fk[...], fv[...], None)
            put_head(1, group, g, acc, top)
            return carry

        lax.fori_loop(*spans[group], one_head, 0)
        send_group(1, group)
    finish(inbox, page_sems, *tok)
    inbox_out = pltpu.make_async_copy(inbox, inbox_hbm, local_sems.at[1])
    inbox_out.start()
    project(1, s_held.at[0])
    ended = jnp.transpose(jnp.concatenate(unpack(s_held[1].astype(f32)), axis=1))
    state_end[...] = ended[:cols].astype(bf16)
    state_out = pltpu.make_async_copy(state_end, state_out_hbm, local_sems.at[2])
    state_out.start()
    hid_out.wait()
    inbox_out.wait()
    state_out.wait()

    def drain(step, carry):
        for sub, way in lanes:
            sum_copy(step, sub, way).wait_send()
        return carry

    lax.fori_loop(0, n_head - 1, drain, 0)
    for way in (0, 1):
        for step in range(count[way]):
            for sub in range(subs2):
                share_copy(step, sub, way).wait_send()
    relay(2 * core, 1, 2).wait_send()
    relay(2 + 2 * core, 3, 3).wait_send()
    win_two.wait_send()
    win_four.wait_send()
    for half in halves:
        for name in ("a+", "a-", "f+", "f-"):
            first(half, name).wait_send()
            for i in (0, -1, 1, 2):
                second(half, i, name).wait_send()
    for k in order:
        kv_out(k).wait_send()
        kv_share(k).wait_send()
    pair_all.wait_send()


def whole(
    n_tok,
    n_head,
    page_home,
    cache_len,
    parents,
    queries,
    hidden,
    gain,
    beams_t,
    beam_gain,
    own_w,
    own_kv,
    kvw,
    cache,
    wo,
    wq,
    side=4,
    subs=4,
    subs2=2,
    block=512,
):
    tokens, width = hidden.shape
    cols, beams = beams_t.shape
    bf16, f32 = jnp.bfloat16, jnp.float32
    heads_here = width // DH
    split_at = (heads_here + 1) // 2
    wide_a, wide_b = split_at * DH, (heads_here - split_at) * DH
    rows = beams // n_tok
    reach = WINDOW // tokens + 1
    cache_rows = cache.shape[0] // 2
    state3 = (n_head, beams // n_head * cols // DH, DH)
    pieces = (2, subs, tokens // 2 // subs, width)
    pieces2 = (2, subs2, tokens // subs2, 2 * DH)
    box = (n_tok, 2 * PAGE, DH)
    hbm = pl.BlockSpec(memory_space=pltpu.HBM)
    vmem, dma = pltpu.VMEM, pltpu.SemaphoreType.DMA
    return pl.pallas_call(
        functools.partial(whole_kernel, n_tok, n_head, side, subs, subs2, block, split_at),
        out_shape=[
            jax.ShapeDtypeStruct(hidden.shape, bf16),
            jax.ShapeDtypeStruct(box, bf16),
            jax.ShapeDtypeStruct(beams_t.shape, bf16),
        ],
        in_specs=[hbm] * 14,
        out_specs=[hbm] * 3,
        scratch_shapes=[
            vmem(beams_t.shape, bf16),
            vmem(hidden.shape, bf16),
            pltpu.SMEM(page_home.shape, jnp.int32),
            pltpu.SMEM(cache_len.shape, jnp.int32),
            vmem((1, beams), jnp.int32),
            vmem(queries.shape, bf16),
            vmem(hidden.shape, bf16),
            vmem((1, width), bf16),
            vmem((2 * DH, beams), bf16),
            vmem(beam_gain.shape, bf16),
            vmem((n_tok, *own_w.shape), bf16),
            vmem((reach, *own_kv.shape), bf16),
            vmem((reach, tokens, DH), bf16),
            vmem((reach, tokens, DH), bf16),
            vmem((tokens, width), bf16),
            vmem(state3, bf16),
            vmem(cache.shape, bf16),
            vmem((n_head, tokens, width), f32),
            vmem((n_head - 1, *pieces), bf16),
            vmem((n_head - 1, *pieces), bf16),
            vmem((n_head, tokens, 2 * DH), f32),
            vmem((n_head // 2, *pieces2), bf16),
            vmem((n_head // 2, *pieces2), bf16),
            vmem((n_head, 8, tokens), f32),
            vmem(kvw.shape, bf16),
            vmem((n_head, width, 2 * DH), bf16),
            vmem((2 * width, DH), f32),
            vmem((cache_rows, DH), bf16),
            vmem((cache_rows, DH), bf16),
            vmem((LAYERS, 2 * DH, width), bf16),
            vmem(wq.shape, bf16),
            vmem((1, cache_rows), f32),
            vmem((heads_here, beams, 2 * DH), f32),
            vmem((heads_here, beams, DH), f32),
            vmem((tokens, DH), bf16),
            vmem((tokens, DH), bf16),
            vmem(box, bf16),
            vmem(box, bf16),
            vmem(box, bf16),
            vmem((beams, DH), f32),
            vmem((LAYERS, n_tok, rows, wide_a + DH), bf16),
            vmem((LAYERS, n_tok, rows, wide_b + DH), bf16),
            vmem((LAYERS, n_tok, rows, wide_a + DH), bf16),
            vmem((LAYERS, n_tok, rows, wide_b + DH), bf16),
            vmem((LAYERS, n_tok, rows, wide_a), bf16),
            vmem((LAYERS, n_tok, rows, wide_b), bf16),
            vmem((LAYERS, *state3), bf16),
            vmem((LAYERS, *state3), bf16),
            vmem((LAYERS, *state3), bf16),
            vmem((LAYERS, n_tok, rows, width + DH), bf16),
            vmem((LAYERS, n_tok, rows, width + DH), bf16),
            vmem((n_tok, rows, wide_a), bf16),
            vmem((n_tok, rows, wide_b), bf16),
            vmem((n_tok, rows, width), bf16),
            dma((6,)),
            dma((8,)),
            dma((40, 2)),
            dma((2,)),
            dma((4, 2)),
            dma((n_head - 1, 2)),
            dma((n_head - 1, 2)),
            dma((n_head - 1, 2, subs)),
            dma((n_head - 1, 2, subs)),
            dma((n_head // 2, 2, subs2)),
            dma((n_head // 2, 2, subs2)),
            dma((2,)),
            dma((2,)),
            dma((LAYERS + 2, 4, 2)),
            dma((LAYERS, 2, 2)),
        ],
        compiler_params=pltpu.CompilerParams(
            collective_id=1, has_side_effects=True, vmem_limit_bytes=67000000
        ),
        name="whole",
    )(
        page_home,
        cache_len,
        parents[None, :],
        queries,
        hidden,
        gain[None, :],
        beams_t,
        beam_gain,
        own_w,
        own_kv,
        kvw,
        cache,
        wo,
        wq,
    )


def place_kernel(
    n_tok,
    own_pages,
    home_ref,
    cache_hbm,
    inbox_hbm,
    hid_hbm,
    state_hbm,
    out_ref,
    hid_out,
    state_out,
    cache,
    inbox,
    hid,
    state,
    sems,
):
    me = lax.axis_index("tokens")
    rows = inbox.shape[1]
    pages_here = out_ref.shape[0] // rows
    size = cache.shape[0] // 4
    parts = [pl.ds(k * size, size) for k in range(4)]
    loads = [
        pltpu.make_async_copy(cache_hbm.at[at], cache.at[at], sems.at[0, k])
        for k, at in enumerate(parts)
    ]
    stores = [
        pltpu.make_async_copy(cache.at[at], out_ref.at[at], sems.at[1, k])
        for k, at in enumerate(parts)
    ]
    for load in loads:
        load.start()
    hid_in = pltpu.make_async_copy(hid_hbm, hid, sems.at[2, 0])
    inbox_in = pltpu.make_async_copy(inbox_hbm, inbox, sems.at[2, 1])
    hid_store = pltpu.make_async_copy(hid, hid_out, sems.at[2, 2])
    state_in = pltpu.make_async_copy(state_hbm, state, sems.at[3, 0])
    state_store = pltpu.make_async_copy(state, state_out, sems.at[3, 1])
    inbox_in.start()
    hid_in.start()
    state_in.start()
    for load, store in zip(loads, stores):
        load.wait()
        store.start()
    hid_in.wait()
    hid_store.start()
    state_in.wait()
    state_store.start()
    inbox_in.wait()
    for store in stores:
        store.wait()

    def each(act):
        def one(slot, carry):
            page = page_slot(home_ref, me, own_pages, pages_here, n_tok, slot)

            @pl.when(page >= 0)
            def _():
                at = pl.ds(pl.multiple_of(page * rows, rows), rows)
                act(pltpu.make_async_copy(inbox.at[slot], out_ref.at[at], sems.at[2, 3]))

            return carry

        lax.fori_loop(0, n_tok, one, 0)

    each(lambda copy: copy.start())
    each(lambda copy: copy.wait())
    hid_store.wait()
    state_store.wait()


def place_pages(n_tok, own_pages, page_home, cache, inbox, hidden, state):
    hbm = pl.BlockSpec(memory_space=pltpu.HBM)
    return pl.pallas_call(
        functools.partial(place_kernel, n_tok, own_pages),
        out_shape=[
            jax.ShapeDtypeStruct(cache.shape, cache.dtype),
            jax.ShapeDtypeStruct(hidden.shape, hidden.dtype),
            jax.ShapeDtypeStruct(state.shape, state.dtype),
        ],
        in_specs=[pl.BlockSpec(memory_space=pltpu.SMEM)] + [hbm] * 4,
        out_specs=[hbm] * 3,
        scratch_shapes=[
            pltpu.VMEM(cache.shape, cache.dtype),
            pltpu.VMEM(inbox.shape, inbox.dtype),
            pltpu.VMEM(hidden.shape, hidden.dtype),
            pltpu.VMEM(state.shape, state.dtype),
            pltpu.SemaphoreType.DMA((4, 4)),
        ],
        compiler_params=pltpu.CompilerParams(vmem_limit_bytes=67000000),
        name="place_pages",
    )(page_home, cache, inbox, hidden, state)


def shards(
    hidden_in,
    queries,
    keyvals,
    out_weight,
    kv_gain,
    kv_weight,
    cache,
    page_home,
    cache_len,
    beam_state,
    parents,
    beam_gain,
    query_weight,
    beam_out_weight,
):
    n_tok = lax.axis_size("tokens")
    n_head = lax.axis_size("heads")
    flat_cache = cache.reshape(-1, DH)
    hidden, inbox, beams_end = whole(
        n_tok,
        n_head,
        page_home,
        cache_len,
        parents,
        queries,
        hidden_in,
        kv_gain,
        beam_state.T,
        beam_gain,
        out_weight.T,
        keyvals.reshape(-1, DH),
        kv_weight.reshape(n_head, -1, DH),
        flat_cache,
        jnp.swapaxes(beam_out_weight, 1, 2),
        query_weight,
    )
    own_pages = hidden_in.shape[0] // PAGE
    new_cache, stretch_hidden, beams_end = place_pages(
        n_tok, own_pages, page_home, flat_cache, inbox, hidden, beams_end
    )
    return (stretch_hidden, new_cache.reshape(cache.shape), beams_end.T)


def solution(mesh):
    tokens = "tokens"
    placed = (
        P(tokens, "heads"),
        P(tokens, "heads"),
        P(tokens, None, "heads"),
        P("heads", tokens),
        P("heads"),
        P(None, None, "heads"),
        P(tokens, None, "heads"),
        P(),
        P(),
        P(None, tokens),
        P(),
        P(None, tokens),
        P(None, tokens, "heads"),
        P(None, "heads", tokens),
    )
    return jax.shard_map(
        shards,
        mesh=mesh,
        in_specs=placed,
        out_specs=(P(tokens, "heads"), P(tokens, None, "heads"), P(None, tokens)),
        check_vma=False,
    )
```

```python
import functools
import math

import jax
import jax.numpy as jnp
from jax import lax
from jax.experimental import pallas as pl
from jax.experimental.pallas import tpu as pltpu
from jax.sharding import PartitionSpec as P

D = 5120
DH = 128
WINDOW = 1024
PAGE = 16
LAYERS = 2
EPSILON = 1e-06
SCALE = DH ** (-0.5)
SCALE2 = SCALE * math.log2(math.e)
MESH = pl.DeviceIdType.MESH
VMEM_SPEC = pl.BlockSpec(memory_space=pltpu.VMEM)


def scatter_start(send, recv, sems, axis, count, me):
    def one(step, carry):
        peer = lax.rem(me + step, count)
        pltpu.make_async_remote_copy(
            src_ref=send.at[peer],
            dst_ref=recv.at[me],
            send_sem=sems.at[0],
            recv_sem=sems.at[1],
            device_id={axis: peer},
            device_id_type=MESH,
        ).start()
        return carry

    lax.fori_loop(1, count, one, 0)


def gather_start(held, sems, axis, count, me):
    def one(step, carry):
        peer = lax.rem(me + step, count)
        pltpu.make_async_remote_copy(
            src_ref=held.at[me],
            dst_ref=held.at[me],
            send_sem=sems.at[0],
            recv_sem=sems.at[1],
            device_id={axis: peer},
            device_id_type=MESH,
        ).start()
        return carry

    lax.fori_loop(1, count, one, 0)


def finish(held, sems, axis, count, me):
    everything = held.at[pl.ds(0, count - 1)]
    pltpu.make_async_remote_copy(
        src_ref=everything,
        dst_ref=everything,
        send_sem=sems.at[0],
        recv_sem=sems.at[1],
        device_id={axis: lax.rem(me + 1, count)},
        device_id_type=MESH,
    ).wait()


def greet(axis, count, me):
    barrier = pltpu.get_barrier_semaphore()

    def one(step, carry):
        pl.semaphore_signal(
            barrier, inc=1, device_id={axis: lax.rem(me + step, count)}, device_id_type=MESH
        )
        return carry

    lax.fori_loop(1, count, one, 0)


def page_slot(home_ref, me, own_pages, pages_here, n_tok, slot):
    shift = lax.div(home_ref[0], pages_here)
    which = lax.rem(me - shift - own_pages * slot + 2 * n_tok * own_pages, n_tok)
    page = home_ref[own_pages * slot + jnp.minimum(which, own_pages - 1)]
    return jnp.where(which < own_pages, lax.rem(page, pages_here), -1)


def whole_kernel(
    n_tok,
    n_head,
    side,
    subs,
    subs2,
    block,
    split_at,
    home_hbm,
    len_hbm,
    parents_hbm,
    query_hbm,
    hid_hbm,
    gain_hbm,
    beams_hbm,
    beam_gain_hbm,
    own_w,
    own_kv,
    kvw,
    cache,
    wo_hbm,
    wq_hbm,
    hid_out_hbm,
    inbox_hbm,
    state_out_hbm,
    state_end,
    hid_out_ref,
    home_ref,
    len_ref,
    parents_ref,
    query_ref,
    hid_ref,
    gain_ref,
    beams_ref,
    beam_gain_ref,
    whole_w,
    win,
    win_k,
    win_v,
    att,
    state_ref,
    cache_v,
    part,
    s_buf,
    r_buf,
    part2,
    s_buf2,
    r_buf2,
    squares,
    kvr,
    kvd,
    spread,
    keys,
    values,
    wo,
    wq,
    bias,
    acc_s,
    top_s,
    fk,
    fv,
    pages,
    outbox,
    inbox,
    lse_s,
    oa_send,
    ob_send,
    oa_recv,
    ob_recv,
    oa_held,
    ob_held,
    b_send,
    b_recv,
    s_held,
    q_send,
    q_recv,
    qa_held,
    qb_held,
    q0_held,
    local_sems,
    in_sems,
    w_sems,
    pair_sems,
    win_sems,
    kv_sems,
    kv_pair_sems,
    s_sems,
    r_sems,
    s_sems2,
    r_sems2,
    sq_sems,
    page_sems,
    tok_sems,
    head_sems,
):
    f32, bf16 = jnp.float32, jnp.bfloat16
    me = lax.axis_index("tokens")
    me_h = lax.axis_index("heads")
    tok = ("tokens", n_tok, me)
    head = ("heads", n_head, me_h)
    core = lax.rem(me, 2)
    y = lax.rem(me // 2, side)
    x = me // (2 * side)
    wide = n_tok // (2 * side)
    partner = me + 1 - 2 * core
    at = lambda i, j: (
        lax.rem(x + i + 2 * wide, wide) * side + lax.rem(y + j + 2 * side, side)
    ) * 2 + core
    cache_in = pltpu.make_async_copy(cache, cache_v, local_sems.at[3])
    wq_in = pltpu.make_async_copy(wq_hbm, wq, local_sems.at[0])
    wo_in = pltpu.make_async_copy(
        wo_hbm, wo.at[:, pl.ds(0, wo_hbm.shape[1])], local_sems.at[4]
    )
    small_in = [
        pltpu.make_async_copy(src, dst, in_sems.at[k])
        for k, (src, dst) in enumerate(
            [
                (parents_hbm, parents_ref),
                (beams_hbm, beams_ref.at[pl.ds(0, beams_hbm.shape[0])]),
                (beam_gain_hbm, beam_gain_ref),
                (home_hbm, home_ref),
                (len_hbm, len_ref),
                (query_hbm, query_ref),
                (hid_hbm, hid_ref),
                (gain_hbm, gain_ref),
            ]
        )
    ]
    for copy in small_in[:3]:
        copy.start()
    wq_in.start()
    for copy in small_in[3:]:
        copy.start()
    cache_in.start()
    wo_in.start()
    greet(*tok)
    greet(*head)

    tokens, width = hid_ref.shape
    beams = beams_hbm.shape[1]
    beams_ref[beams_hbm.shape[0] :] = jnp.zeros((beams_ref.shape[0] - beams_hbm.shape[0], beams), bf16)
    wo[:, wo_hbm.shape[1] :] = jnp.zeros((LAYERS, wo.shape[1] - wo_hbm.shape[1], width), bf16)
    source = lax.broadcasted_iota(jnp.int32, (beams, beams), 0)
    for copy in small_in[:3]:
        copy.wait()
    picked = jnp.transpose(jnp.where(source == parents_ref[...], 1.0, 0.0).astype(f32))
    picked = picked.astype(bf16)
    cols = wq.shape[1]
    extra = cols - DH
    strips = DH // extra

    def both_of(lhs, ref, lead):
        first = ref[lead, :DH] if lead is not None else ref[:DH]
        other = ref[lead, DH:] if lead is not None else ref[DH:]
        dims = (((1,), (1,)), ((), ()))
        return (
            lax.dot_general(lhs, first, dims, preferred_element_type=f32),
            lax.dot_general(lhs, other, dims, preferred_element_type=f32),
        )

    def pack(ref, main, rest):
        high = beams // n_head
        ref[:, :high, :] = main.reshape(n_head, high, DH).astype(bf16)
        strip = rest.reshape(n_head, strips, high // strips, DH)
        total = strip[:, 0]
        for k in range(1, strips):
            total = total + pltpu.roll(strip[:, k], k * extra, 2)
        ref[:, high:, :] = total.astype(bf16)

    def unpack(value):
        high = beams // n_head
        main = value[:, :high].reshape(beams, DH)
        strip = value[:, high:]
        inside = lax.broadcasted_iota(jnp.int32, strip.shape, 2) < extra
        parts = [
            jnp.where(inside, pltpu.roll(strip, (DH - k * extra) % DH, 2), 0.0)
            for k in range(strips)
        ]
        return main, jnp.stack(parts, axis=1).reshape(beams, DH)

    state = both_of(picked, beams_ref, None)
    pack(state_ref, *state)
    wq_in.wait()

    def send_query(layer, state):
        main, rest = state
        sq = jnp.sum(main * main + rest * rest, axis=1, keepdims=True)
        gain = beam_gain_ref[layer : layer + 1, :].astype(f32)
        share_q = jnp.dot(
            (main * gain[:, :DH]).astype(bf16), wq[layer, :DH], preferred_element_type=f32
        ) + jnp.dot(
            (rest[:, :extra] * gain[:, DH:]).astype(bf16), wq[layer, DH:], preferred_element_type=f32
        )
        rows = beams // n_tok
        q_send[layer, :, :, :width] = share_q.reshape(n_tok, rows, width).astype(bf16)
        q_send[layer, :, :, width:] = (
            jnp.broadcast_to(sq, (beams, DH)).reshape(n_tok, rows, DH).astype(bf16)
        )
        return lambda: scatter_start(q_send.at[layer], q_recv.at[layer], tok_sems.at[2 + layer, 0], *tok)

    def sum_query(layer):
        recv = q_recv.at[layer]
        recv[me] = q_send[layer, me]
        finish(recv, tok_sems.at[2 + layer, 0], *tok)
        total = jnp.sum(recv[...].astype(f32), axis=0)
        scale = lax.rsqrt(total[:, width : width + 1] / D + EPSILON)
        return (total[:, :width] * scale).astype(bf16)

    start_query = send_query(0, state)

    cache_rows = keys.shape[0]
    pages_here = cache_rows // PAGE
    own_pages = tokens // PAGE
    lane = lax.broadcasted_iota(jnp.int32, (1, cache_rows), 1)
    for copy in small_in[3:]:
        copy.wait()
    kept = (me * cache_rows + lane) < len_ref[0]
    page_of = lane // PAGE
    for slot in range(n_tok):
        landing = page_slot(home_ref, me, own_pages, pages_here, n_tok, slot)
        kept = kept & (page_of != landing)
    bias[...] = jnp.where(kept, 0.0, -1e30).astype(f32)

    pl.semaphore_wait(pltpu.get_barrier_semaphore(), n_tok + n_head - 2)

    def remote(src, dst, sems, target, axis="tokens"):
        return pltpu.make_async_remote_copy(
            src_ref=src,
            dst_ref=dst,
            send_sem=sems.at[0],
            recv_sem=sems.at[1],
            device_id={axis: target},
            device_id_type=MESH,
        )

    back = lambda b: lax.rem(me - b + n_tok, n_tok)
    ahead = lambda b: lax.rem(me + b, n_tok)
    win_two = remote(own_kv, win.at[2], win_sems.at[0], ahead(2))
    win_four = remote(own_kv, win.at[4], win_sems.at[1], ahead(4))
    win_two.start()
    win_four.start()

    depth = own_w.shape[0]
    cut_w = depth * 2 // 5
    spot = lambda half, i, j: at(i, j) if half == 0 else at(j, i)

    def rows_of(half, stage=None, part_at=None):
        begin, size = (0, cut_w) if half == 0 else (cut_w, depth - cut_w)
        if part_at is None:
            return pl.ds(begin, size)
        up = size // 2 if half == stage else 16
        return pl.ds(begin, up) if part_at == 0 else pl.ds(begin + up, size - up)

    slots = {}
    for half in (0, 1):
        for name in ("a+", "a-", "f+", "f-"):
            slots[half, name] = len(slots)
        for i in (0, -1, 1, 2):
            for name in ("a+", "a-", "f+", "f-"):
                slots[half, i, name] = len(slots)

    def first(half, name):
        way = 1 if name[1] == "+" else -1
        target = spot(half, way, 0)
        if name[0] == "a":
            where = rows_of(half)
            return remote(
                own_w.at[where], whole_w.at[me, where], w_sems.at[slots[half, name]], target
            )
        ref = whole_w.at[spot(half, -way, 0), rows_of(half, 0, 0 if way == 1 else 1)]
        return remote(ref, ref, w_sems.at[slots[half, name]], target)

    def first_in(half, name):
        way = 1 if name[1] == "+" else -1
        if name[0] == "a":
            ref = whole_w.at[spot(half, -way, 0), rows_of(half)]
        else:
            ref = whole_w.at[spot(half, -2 * way, 0), rows_of(half, 0, 0 if way == 1 else 1)]
        return remote(ref, ref, w_sems.at[slots[half, name]], spot(half, way, 0))

    def second(half, i, name):
        way = 1 if name[1] == "+" else -1
        target = spot(half, 0, way)
        if name[0] == "a":
            where = rows_of(half)
            dst = whole_w.at[spot(half, i, 0), where]
            src = own_w.at[where] if i == 0 else dst
        else:
            src = dst = whole_w.at[spot(half, i, -way), rows_of(half, 1, 0 if way == 1 else 1)]
        return remote(src, dst, w_sems.at[slots[half, i, name]], target)

    def second_in(half, i, name):
        way = 1 if name[1] == "+" else -1
        if name[0] == "a":
            ref = whole_w.at[spot(half, i, -way), rows_of(half)]
        else:
            ref = whole_w.at[spot(half, i, -2 * way), rows_of(half, 1, 0 if way == 1 else 1)]
        return remote(ref, ref, w_sems.at[slots[half, i, name]], spot(half, 0, way))

    def share(half, i, j):
        where = rows_of(half)
        dst = whole_w.at[spot(half, i, j), where]
        src = own_w.at[where] if (i, j) == (0, 0) else dst
        remote(src, dst, pair_sems, partner).start()

    halves = (0, 1)
    for half in halves:
        for name in ("a+", "a-"):
            first(half, name).start()
    for half in halves:
        for name in ("a+", "a-"):
            second(half, 0, name).start()
    for half in halves:
        share(half, 0, 0)

    kv_rows = kvw.shape[1] // 2
    kv_half = pl.ds(pl.multiple_of(core * kv_rows, kv_rows), kv_rows)

    def kv_out(k):
        target = lax.rem(me_h + k, n_head)
        return remote(
            kvw.at[target, kv_half], kvr.at[me_h, kv_half], kv_sems.at[k - 1], target, "heads"
        )

    def kv_in(k):
        ref = kvr.at[lax.rem(me_h - k + n_head, n_head), kv_half]
        return remote(ref, ref, kv_sems.at[k - 1], lax.rem(me_h + k, n_head), "heads")

    order = sorted(range(1, n_head), key=lambda k: min(k, n_head - k))
    for k in order:
        kv_out(k).start()

    own_copies = [
        pltpu.make_async_copy(own_w, whole_w.at[me], local_sems.at[5]),
        pltpu.make_async_copy(own_kv, win.at[0], local_sems.at[1]),
        pltpu.make_async_copy(kvw.at[me_h], kvr.at[me_h], local_sems.at[2]),
    ]
    for copy in own_copies:
        copy.start()

    own_copies[1].wait()
    cache_in.wait()
    size = cache_rows // 4
    parts = cache_v.shape[0] // size

    def split(k):
        spread[0:size, :] = cache_v[k * size : (k + 1) * size, :].astype(jnp.float32)
        at = slice(k * size // 2, (k + 1) * size // 2)
        keys[at, :] = spread[pl.ds(0, size // 2, stride=2), :].astype(jnp.bfloat16)
        values[at, :] = spread[pl.ds(1, size // 2, stride=2), :].astype(jnp.bfloat16)

    def split_window(b):
        spread[0 : 2 * tokens, :] = win[b].astype(f32)
        win_k[b] = spread[pl.ds(0, tokens, stride=2), :].astype(bf16)
        win_v[b] = spread[pl.ds(1, tokens, stride=2), :].astype(bf16)

    def attend_window(g):
        cols = slice(g * DH, (g + 1) * DH)
        q = query_ref[:, cols]
        count = q.shape[0]
        acc = jnp.zeros((count, 2 * DH), jnp.float32)
        top = jnp.full((count, 1), -1e30, jnp.float32)
        row = lax.broadcasted_iota(jnp.int32, (count, count), 0)
        col = lax.broadcasted_iota(jnp.int32, (count, count), 1)
        ones = jnp.ones((count, DH), jnp.bfloat16)
        reach = win.shape[0]
        for b in range(reach):
            s = lax.dot_general(
                q, win_k[b], (((1,), (1,)), ((), ())), preferred_element_type=jnp.float32
            )
            if b == 0:
                s = jnp.where(col <= row, s, -1e30)
            else:
                s = s + jnp.where(me >= b, jnp.float32(0.0), jnp.float32(-1e30))
            if b == reach - 1:
                s = jnp.where(col > row, s, -1e30)
            here = jnp.maximum(top, jnp.max(s, axis=1, keepdims=True))
            p = jnp.exp2((s - here) * SCALE2).astype(jnp.bfloat16)
            shrink = jnp.exp2((top - here) * SCALE2)
            both = jnp.concatenate([win_v[b], ones], axis=1)
            acc = acc * shrink + jnp.dot(p, both, preferred_element_type=jnp.float32)
            top = here
        att[:, cols] = (acc[:, :DH] / acc[:, DH:]).astype(jnp.bfloat16)

    early = [functools.partial(split, k) for k in range(parts)]
    late = [functools.partial(attend_window, g) for g in range(query_ref.shape[1] // DH)]

    def fill(work, amount=1):
        for _ in range(amount):
            if work:
                work.pop(0)()

    win_in = lambda b, k: remote(win.at[b], win.at[b], win_sems.at[k], partner)

    def relay(src, dst, k):
        return remote(win.at[src], win.at[dst], win_sems.at[k], partner)

    for name in ("a+", "a-"):
        way = 1 if name[1] == "+" else -1
        for half in halves:
            first_in(half, name).wait_recv()
            first(half, "f" + name[1]).start()
            for other in ("a+", "a-"):
                second(half, -way, other).start()
            share(half, -way, 0)
        fill(early)
    win_in(2, 0).wait_recv()
    relay(2 * core, 1, 2).start()
    for name in ("a+", "a-"):
        way = 1 if name[1] == "+" else -1
        for half in halves:
            second_in(half, 0, name).wait_recv()
            second(half, 0, "f" + name[1]).start()
            share(half, 0, -way)
        fill(early)
    for half in halves:
        first_in(half, "f+").wait_recv()
        first_in(half, "f-").wait_recv()
        for other in ("a+", "a-"):
            second(half, 2, other).start()
        share(half, 2, 0)
    win_in(4, 1).wait_recv()
    relay(2 + 2 * core, 3, 3).start()
    for i in (-1, 1):
        for name in ("a+", "a-"):
            way = 1 if name[1] == "+" else -1
            for half in halves:
                second_in(half, i, name).wait_recv()
                second(half, i, "f" + name[1]).start()
                share(half, i, -way)
            fill(early)
    fill(early, parts)
    win_in(1, 2).wait_recv()
    win_in(3, 3).wait_recv()
    for b in range(win.shape[0]):
        split_window(b)
    def kv_share(k):
        ref = kvr.at[lax.rem(me_h - k + n_head, n_head), kv_half]
        return remote(ref, ref, kv_pair_sems.at[k - 1], partner)

    def kv_share_in(k):
        other = pl.ds(pl.multiple_of((1 - core) * kv_rows, kv_rows), kv_rows)
        ref = kvr.at[lax.rem(me_h - k + n_head, n_head), other]
        return remote(ref, ref, kv_pair_sems.at[k - 1], partner)

    fill(late)
    for half in halves:
        second_in(half, 0, "f+").wait_recv()
        second_in(half, 0, "f-").wait_recv()
        share(half, 0, 2)
    for name in ("a+", "a-"):
        way = 1 if name[1] == "+" else -1
        for half in halves:
            second_in(half, 2, name).wait_recv()
            second(half, 2, "f" + name[1]).start()
            share(half, 2, -way)
        fill(late)
    for i in (-1, 1, 2):
        for half in halves:
            second_in(half, i, "f+").wait_recv()
            second_in(half, i, "f-").wait_recv()
            share(half, i, 2)
        if i != 2:
            fill(late)
    fill(late, len(late))
    half_of_all = whole_w.at[pl.ds(0, n_tok // 2)]
    pair_all = remote(half_of_all, half_of_all, pair_sems, partner)
    pair_all.wait_recv()
    own_copies[0].wait()

    heads_here = width // DH
    half_rows = tokens // 2
    middle = n_head // 2
    rows_sub = half_rows // subs
    rows_sub2 = tokens // subs2
    wrap = lambda value: lax.rem(value + 2 * n_head, n_head)
    lanes = [(sub, way) for sub in range(subs) for way in (0, 1)]
    sign = (1, -1)
    at_rows = lambda sub, way: slice(way * half_rows + sub * rows_sub, way * half_rows + (sub + 1) * rows_sub)

    def product(c):
        per = n_tok // n_head
        w = whole_w[pl.ds(c * per, per)].reshape(width, width)
        part[c] = lax.dot_general(
            att[...], w, (((1,), (1,)), ((), ())), preferred_element_type=f32
        )

    def sum_copy(step, sub, way):
        return pltpu.make_async_remote_copy(
            src_ref=s_buf.at[step, way, sub],
            dst_ref=r_buf.at[step, way, sub],
            send_sem=s_sems.at[step, way, sub],
            recv_sem=r_sems.at[step, way, sub],
            device_id={"heads": wrap(me_h + sign[way])},
            device_id_type=MESH,
        )

    def soft(q, acc, top, keys_b, values_b, bias_b):
        s = lax.dot_general(q, keys_b, (((1,), (1,)), ((), ())), preferred_element_type=f32)
        if bias_b is not None:
            s = s + bias_b
        here = jnp.maximum(top, jnp.max(s, axis=1, keepdims=True))
        p = jnp.exp2((s - here) * SCALE2).astype(bf16)
        shrink = jnp.exp2((top - here) * SCALE2)
        both = jnp.concatenate([values_b, jnp.ones_like(values_b)], axis=1)
        return acc * shrink + jnp.dot(p, both, preferred_element_type=f32), here

    def head_of(held, g):
        at = pl.multiple_of(g * DH, DH)
        return held[:, :, pl.ds(at, DH)].astype(f32).reshape(-1, DH).astype(bf16)

    def soft_old(q):
        acc = jnp.zeros((q.shape[0], 2 * DH), f32)
        top = jnp.full((q.shape[0], 1), -1e30, f32)
        for b in range(cache_rows // block):
            at = slice(b * block, (b + 1) * block)
            acc, top = soft(q, acc, top, keys[at, :], values[at, :], bias[:, at])
        return acc, top

    def spread_kv(c):
        count = width
        spread[0 : 2 * count, :] = kvr[c].astype(f32)
        kvd[c, :, :DH] = spread[pl.ds(0, count, stride=2), :].astype(bf16)
        kvd[c, :, DH:] = spread[pl.ds(1, count, stride=2), :].astype(bf16)

    start_query()
    product(wrap(me_h - 1))
    product(wrap(me_h + 1))

    begin_old = middle

    def old_half(g, k):
        q = head_of(q0_held, g)
        if k == 0:
            acc = jnp.zeros((beams, 2 * DH), f32)
            top = jnp.full((beams, 1), -1e30, f32)
        else:
            acc, top = acc_s[g], top_s[g][:, :1]
        per = cache_rows // block // 2
        for b in range(k * per, (k + 1) * per):
            where = slice(b * block, (b + 1) * block)
            acc, top = soft(q, acc, top, keys[where, :], values[where, :], bias[:, where])
        acc_s[g] = acc
        top_s[g] = jnp.broadcast_to(top, (beams, DH))

    def work(step, slot):
        if slot < 2:

            @pl.when(step < middle - 1)
            def _():
                if slot == 0:
                    product(wrap(me_h - 2 - step))
                else:
                    product(lax.select(step == middle - 2, me_h, wrap(me_h + 2 + step)))

            @pl.when(step >= n_head - 3)
            def _():
                spread_kv((step - (n_head - 3)) * 4 + slot * 2)
                spread_kv((step - (n_head - 3)) * 4 + slot * 2 + 1)

        else:

            @pl.when(step >= begin_old)
            def _():
                old_half(jnp.maximum(step - begin_old, 0), slot - 2)

    def reduce_step(step, carry):
        for sub in range(subs):
            for way in (0, 1):
                c = wrap(me_h - sign[way] * (1 + step))
                own = part[c, at_rows(sub, way), :]

                @pl.when(step == 0)
                def _():
                    s_buf[step, way, sub] = own.astype(bf16)

                @pl.when(step > 0)
                def _():
                    sum_copy(step - 1, sub, way).wait_recv()
                    s_buf[step, way, sub] = (
                        own + r_buf[step - 1, way, sub].astype(f32)
                    ).astype(bf16)

                sum_copy(step, sub, way).start()
            if sub == 0:

                @pl.when(step == n_head - 3)
                def _():
                    for k in order:
                        kv_share_in(k).wait_recv()
                    own_copies[2].wait()

            for slot in range(sub * 4 // subs, (sub + 1) * 4 // subs):
                work(step, slot)

        @pl.when(step == middle - 1)
        def _():
            for k in order:
                kv_in(k).wait_recv()
                kv_share(k).start()

        @pl.when(step == begin_old - 2)
        def _():
            q0_held[me] = sum_query(0)
            gather_start(q0_held, tok_sems.at[2, 1], *tok)

        @pl.when(step == begin_old - 1)
        def _():
            finish(q0_held, tok_sems.at[2, 1], *tok)

        return carry

    lax.fori_loop(0, n_head - 1, reduce_step, 0)
    left = [(g, k) for g in range(n_head - 1 - begin_old, heads_here) for k in (0, 1)]

    last = n_head - 2
    for sub, way in lanes:
        rows = at_rows(sub, way)
        sum_copy(last, sub, way).wait_recv()
        total = part[me_h, rows, :] + r_buf[last, way, sub].astype(f32)
        hid_out_ref[rows, :] = (hid_ref[rows, :].astype(f32) + total).astype(bf16)

    hid_out = pltpu.make_async_copy(hid_out_ref, hid_out_hbm, local_sems.at[0])
    hid_out.start()

    hidden = hid_out_ref[...].astype(f32)
    scaled = (hidden * gain_ref[...].astype(f32)).astype(bf16)

    def product2(c):
        part2[c] = jnp.dot(scaled, kvd[c], preferred_element_type=f32)

    count = (middle, n_head - 1 - middle)

    def chunk(step, way):
        return wrap(me_h + middle - step) if way == 0 else wrap(me_h - count[1] + step)

    def share_copy(step, sub, way):
        return pltpu.make_async_remote_copy(
            src_ref=s_buf2.at[step, way, sub],
            dst_ref=r_buf2.at[step, way, sub],
            send_sem=s_sems2.at[step, way, sub],
            recv_sem=r_sems2.at[step, way, sub],
            device_id={"heads": wrap(me_h + sign[way])},
            device_id_type=MESH,
        )

    product2(chunk(0, 0))
    product2(chunk(0, 1))
    for step in range(middle):
        for sub in range(subs2):
            rows = slice(sub * rows_sub2, (sub + 1) * rows_sub2)
            for way in (0, 1):
                if step >= count[way]:
                    continue
                value = part2[chunk(step, way), rows, :]
                if step:
                    share_copy(step - 1, sub, way).wait_recv()
                    value = value + r_buf2[step - 1, way, sub].astype(f32)
                s_buf2[step, way, sub] = value.astype(bf16)
                share_copy(step, sub, way).start()
        if step == 0:
            flat = (hidden * hidden).astype(bf16)
            ones = jnp.ones((8, width), bf16)
            squares[me_h] = lax.dot_general(
                ones, flat, (((1,), (1,)), ((), ())), preferred_element_type=f32
            )
            gather_start(squares, sq_sems, *head)
        for way in (0, 1):
            if step + 1 < count[way]:
                product2(chunk(step + 1, way))
        if step == middle - 1:
            product2(me_h)
        if left:
            old_half(*left.pop(0))
    while left:
        old_half(*left.pop(0))
    finish(squares, sq_sems, *head)
    mean = jnp.transpose(jnp.sum(squares[...], axis=0))[:, :1] / D
    factor = lax.rsqrt(mean + EPSILON)
    for sub in range(subs2):
        rows = slice(sub * rows_sub2, (sub + 1) * rows_sub2)
        total = part2[me_h, rows, :]
        for way in (0, 1):
            share_copy(count[way] - 1, sub, way).wait_recv()
            total = total + r_buf2[count[way] - 1, way, sub].astype(f32)
        fresh = total * factor[rows]
        fk[rows, :] = fresh[:, :DH].astype(bf16)
        fv[rows, :] = fresh[:, DH:].astype(bf16)

    lane8 = lax.broadcasted_iota(jnp.int32, (tokens, DH), 1)
    sends = (oa_send, ob_send)
    spans = ((0, split_at), (split_at, heads_here))

    def put_head(layer, group, g, acc, top):
        amount = acc[:, DH:]
        out = (acc[:, :DH] / amount).reshape(n_tok, -1, DH).astype(bf16)
        at = pl.multiple_of((g - spans[group][0]) * DH, DH)
        sends[group][layer, :, :, pl.ds(at, DH)] = out
        value = top * SCALE2 + jnp.log2(amount)
        mine = (lane8 % 8 == g) & (lane8 < 24)
        lse_s[...] = jnp.where(mine, value, lse_s[...])

    def send_group(layer, group):
        value = lse_s[...]
        high = value.astype(bf16).astype(f32)
        mid = (value - high).astype(bf16).astype(f32)
        low = value - high - mid
        packed = jnp.where(lane8 < 8, high, jnp.where(lane8 < 16, mid, low))
        wide = (spans[group][1] - spans[group][0]) * DH
        sends[group][layer, :, :, wide:] = packed.reshape(n_tok, -1, DH).astype(bf16)
        recv = (oa_recv, ob_recv)[group].at[layer]
        scatter_start(sends[group].at[layer], recv, tok_sems.at[layer, group], *tok)

    def mix_group(layer, group):
        recv = (oa_recv, ob_recv)[group].at[layer]
        held = (oa_held, ob_held)[group].at[layer]
        low, high = spans[group]
        wide = (high - low) * DH
        recv[me] = sends[group][layer, me]
        finish(recv, tok_sems.at[layer, group], *tok)
        packed = recv[:, :, wide:].astype(f32)
        lse = (
            packed[:, :, low:high]
            + packed[:, :, 8 + low : 8 + high]
            + packed[:, :, 16 + low : 16 + high]
        )
        weight = jnp.exp2(lse - jnp.max(lse, axis=0, keepdims=True))
        share = weight / jnp.sum(weight, axis=0, keepdims=True)
        for k in range(high - low):
            cols = slice(k * DH, (k + 1) * DH)
            mixed = jnp.sum(recv[:, :, cols].astype(f32) * share[:, :, k : k + 1], axis=0)
            held[me, :, cols] = mixed.astype(bf16)
        gather_start(held, tok_sems.at[layer, 2 + group], *tok)

    def branch_of(layer, group):
        held = (oa_held, ob_held)[group].at[layer]
        finish(held, tok_sems.at[layer, 2 + group], *tok)
        low, high = spans[group]
        wide = (high - low) * DH
        whole = held[...].astype(f32).reshape(-1, wide).astype(bf16)
        return both_of(whole, wo.at[:, :, pl.ds(low * DH, wide)], layer)

    def project(layer, before, beside=None):
        mix_group(layer, 0)
        mix_group(layer, 1)
        one, two = branch_of(layer, 0), branch_of(layer, 1)
        send, recv, held = b_send.at[layer], b_recv.at[layer], s_held.at[layer]
        pack(send, one[0] + two[0], one[1] + two[1])
        scatter_start(send, recv, head_sems.at[layer, 0], *head)
        if beside is not None:
            beside()
        recv[me_h] = send[me_h]
        finish(recv, head_sems.at[layer, 0], *head)
        total = jnp.sum(recv[...].astype(f32), axis=0)
        held[me_h] = (before[me_h].astype(f32) + total).astype(bf16)
        gather_start(held, head_sems.at[layer, 1], *head)
        finish(held, head_sems.at[layer, 1], *head)

    lse_s[...] = jnp.zeros(lse_s.shape, f32)
    for group in (0, 1):
        for g in range(*spans[group]):
            acc, top = soft(head_of(q0_held, g), acc_s[g], top_s[g][:, :1], fk[...], fv[...], None)
            put_head(0, group, g, acc, top)
        send_group(0, group)

    def send_pages():
        spread[pl.ds(0, tokens, stride=2), :] = fk[...].astype(f32)
        spread[pl.ds(1, tokens, stride=2), :] = fv[...].astype(f32)
        pages[0:own_pages] = spread[0 : 2 * tokens, :].reshape(own_pages, -1, DH).astype(bf16)
        pages[own_pages:] = jnp.zeros((n_tok - own_pages, *pages.shape[1:]), bf16)
        shift = lax.div(home_ref[0], pages_here)

        def stage(peer, carry):
            which = lax.rem(peer - shift - own_pages * me + 2 * n_tok * own_pages, n_tok)
            outbox[peer] = pages[which]
            return carry

        lax.fori_loop(0, n_tok, stage, 0)
        scatter_start(outbox, inbox, page_sems, *tok)
        inbox[me] = outbox[me]

    wo_in.wait()
    project(0, state_ref, send_pages)
    send_query(1, unpack(s_held[0].astype(f32)))()
    ready = sum_query(1)
    cut = split_at * DH
    qa_held[me] = ready[:, :cut]
    gather_start(qa_held, tok_sems.at[3, 1], *tok)
    qb_held[me] = ready[:, cut:]
    gather_start(qb_held, tok_sems.at[3, 2], *tok)
    for group, held in ((0, qa_held), (1, qb_held)):
        finish(held, tok_sems.at[3, 1 + group], *tok)

        def one_head(g, carry, group=group, held=held):
            q = head_of(held, g - spans[group][0])
            acc, top = soft_old(q)
            acc, top = soft(q, acc, top, fk[...], fv[...], None)
            put_head(1, group, g, acc, top)
            return carry

        lax.fori_loop(*spans[group], one_head, 0)
        send_group(1, group)
    finish(inbox, page_sems, *tok)
    inbox_out = pltpu.make_async_copy(inbox, inbox_hbm, local_sems.at[1])
    inbox_out.start()
    project(1, s_held.at[0])
    ended = jnp.transpose(jnp.concatenate(unpack(s_held[1].astype(f32)), axis=1))
    state_end[...] = ended[:cols].astype(bf16)
    state_out = pltpu.make_async_copy(state_end, state_out_hbm, local_sems.at[2])
    state_out.start()
    hid_out.wait()
    inbox_out.wait()
    state_out.wait()

    def drain(step, carry):
        for sub, way in lanes:
            sum_copy(step, sub, way).wait_send()
        return carry

    lax.fori_loop(0, n_head - 1, drain, 0)
    for way in (0, 1):
        for step in range(count[way]):
            for sub in range(subs2):
                share_copy(step, sub, way).wait_send()
    relay(2 * core, 1, 2).wait_send()
    relay(2 + 2 * core, 3, 3).wait_send()
    win_two.wait_send()
    win_four.wait_send()
    for half in halves:
        for name in ("a+", "a-", "f+", "f-"):
            first(half, name).wait_send()
            for i in (0, -1, 1, 2):
                second(half, i, name).wait_send()
    for k in order:
        kv_out(k).wait_send()
        kv_share(k).wait_send()
    pair_all.wait_send()


def whole(
    n_tok,
    n_head,
    page_home,
    cache_len,
    parents,
    queries,
    hidden,
    gain,
    beams_t,
    beam_gain,
    own_w,
    own_kv,
    kvw,
    cache,
    wo,
    wq,
    side=4,
    subs=4,
    subs2=2,
    block=512,
):
    tokens, width = hidden.shape
    cols, beams = beams_t.shape
    bf16, f32 = jnp.bfloat16, jnp.float32
    heads_here = width // DH
    split_at = (heads_here + 1) // 2
    wide_a, wide_b = split_at * DH, (heads_here - split_at) * DH
    rows = beams // n_tok
    reach = WINDOW // tokens + 1
    cache_rows = cache.shape[0] // 2
    state3 = (n_head, beams // n_head * cols // DH, DH)
    pieces = (2, subs, tokens // 2 // subs, width)
    pieces2 = (2, subs2, tokens // subs2, 2 * DH)
    box = (n_tok, 2 * PAGE, DH)
    hbm = pl.BlockSpec(memory_space=pltpu.HBM)
    vmem, dma = pltpu.VMEM, pltpu.SemaphoreType.DMA
    return pl.pallas_call(
        functools.partial(whole_kernel, n_tok, n_head, side, subs, subs2, block, split_at),
        out_shape=[
            jax.ShapeDtypeStruct(hidden.shape, bf16),
            jax.ShapeDtypeStruct(box, bf16),
            jax.ShapeDtypeStruct(beams_t.shape, bf16),
        ],
        in_specs=[hbm] * 14,
        out_specs=[hbm] * 3,
        scratch_shapes=[
            vmem(beams_t.shape, bf16),
            vmem(hidden.shape, bf16),
            pltpu.SMEM(page_home.shape, jnp.int32),
            pltpu.SMEM(cache_len.shape, jnp.int32),
            vmem((1, beams), jnp.int32),
            vmem(queries.shape, bf16),
            vmem(hidden.shape, bf16),
            vmem((1, width), bf16),
            vmem((2 * DH, beams), bf16),
            vmem(beam_gain.shape, bf16),
            vmem((n_tok, *own_w.shape), bf16),
            vmem((reach, *own_kv.shape), bf16),
            vmem((reach, tokens, DH), bf16),
            vmem((reach, tokens, DH), bf16),
            vmem((tokens, width), bf16),
            vmem(state3, bf16),
            vmem(cache.shape, bf16),
            vmem((n_head, tokens, width), f32),
            vmem((n_head - 1, *pieces), bf16),
            vmem((n_head - 1, *pieces), bf16),
            vmem((n_head, tokens, 2 * DH), f32),
            vmem((n_head // 2, *pieces2), bf16),
            vmem((n_head // 2, *pieces2), bf16),
            vmem((n_head, 8, tokens), f32),
            vmem(kvw.shape, bf16),
            vmem((n_head, width, 2 * DH), bf16),
            vmem((2 * width, DH), f32),
            vmem((cache_rows, DH), bf16),
            vmem((cache_rows, DH), bf16),
            vmem((LAYERS, 2 * DH, width), bf16),
            vmem(wq.shape, bf16),
            vmem((1, cache_rows), f32),
            vmem((heads_here, beams, 2 * DH), f32),
            vmem((heads_here, beams, DH), f32),
            vmem((tokens, DH), bf16),
            vmem((tokens, DH), bf16),
            vmem(box, bf16),
            vmem(box, bf16),
            vmem(box, bf16),
            vmem((beams, DH), f32),
            vmem((LAYERS, n_tok, rows, wide_a + DH), bf16),
            vmem((LAYERS, n_tok, rows, wide_b + DH), bf16),
            vmem((LAYERS, n_tok, rows, wide_a + DH), bf16),
            vmem((LAYERS, n_tok, rows, wide_b + DH), bf16),
            vmem((LAYERS, n_tok, rows, wide_a), bf16),
            vmem((LAYERS, n_tok, rows, wide_b), bf16),
            vmem((LAYERS, *state3), bf16),
            vmem((LAYERS, *state3), bf16),
            vmem((LAYERS, *state3), bf16),
            vmem((LAYERS, n_tok, rows, width + DH), bf16),
            vmem((LAYERS, n_tok, rows, width + DH), bf16),
            vmem((n_tok, rows, wide_a), bf16),
            vmem((n_tok, rows, wide_b), bf16),
            vmem((n_tok, rows, width), bf16),
            dma((6,)),
            dma((8,)),
            dma((40, 2)),
            dma((2,)),
            dma((4, 2)),
            dma((n_head - 1, 2)),
            dma((n_head - 1, 2)),
            dma((n_head - 1, 2, subs)),
            dma((n_head - 1, 2, subs)),
            dma((n_head // 2, 2, subs2)),
            dma((n_head // 2, 2, subs2)),
            dma((2,)),
            dma((2,)),
            dma((LAYERS + 2, 4, 2)),
            dma((LAYERS, 2, 2)),
        ],
        compiler_params=pltpu.CompilerParams(
            collective_id=1, has_side_effects=True, vmem_limit_bytes=67000000
        ),
        name="whole",
    )(
        page_home,
        cache_len,
        parents[None, :],
        queries,
        hidden,
        gain[None, :],
        beams_t,
        beam_gain,
        own_w,
        own_kv,
        kvw,
        cache,
        wo,
        wq,
    )


def place_kernel(
    n_tok,
    own_pages,
    home_ref,
    cache_hbm,
    inbox_hbm,
    hid_hbm,
    state_hbm,
    out_ref,
    hid_out,
    state_out,
    cache,
    inbox,
    hid,
    state,
    sems,
):
    me = lax.axis_index("tokens")
    rows = inbox.shape[1]
    pages_here = out_ref.shape[0] // rows
    size = cache.shape[0] // 4
    parts = [pl.ds(k * size, size) for k in range(4)]
    loads = [
        pltpu.make_async_copy(cache_hbm.at[at], cache.at[at], sems.at[0, k])
        for k, at in enumerate(parts)
    ]
    stores = [
        pltpu.make_async_copy(cache.at[at], out_ref.at[at], sems.at[1, k])
        for k, at in enumerate(parts)
    ]
    for load in loads:
        load.start()
    hid_in = pltpu.make_async_copy(hid_hbm, hid, sems.at[2, 0])
    inbox_in = pltpu.make_async_copy(inbox_hbm, inbox, sems.at[2, 1])
    hid_store = pltpu.make_async_copy(hid, hid_out, sems.at[2, 2])
    state_in = pltpu.make_async_copy(state_hbm, state, sems.at[3, 0])
    state_store = pltpu.make_async_copy(state, state_out, sems.at[3, 1])
    inbox_in.start()
    hid_in.start()
    state_in.start()
    for load, store in zip(loads, stores):
        load.wait()
        store.start()
    hid_in.wait()
    hid_store.start()
    state_in.wait()
    state_store.start()
    inbox_in.wait()
    for store in stores:
        store.wait()

    def each(act):
        def one(slot, carry):
            page = page_slot(home_ref, me, own_pages, pages_here, n_tok, slot)

            @pl.when(page >= 0)
            def _():
                at = pl.ds(pl.multiple_of(page * rows, rows), rows)
                act(pltpu.make_async_copy(inbox.at[slot], out_ref.at[at], sems.at[2, 3]))

            return carry

        lax.fori_loop(0, n_tok, one, 0)

    each(lambda copy: copy.start())
    each(lambda copy: copy.wait())
    hid_store.wait()
    state_store.wait()


def place_pages(n_tok, own_pages, page_home, cache, inbox, hidden, state):
    hbm = pl.BlockSpec(memory_space=pltpu.HBM)
    return pl.pallas_call(
        functools.partial(place_kernel, n_tok, own_pages),
        out_shape=[
            jax.ShapeDtypeStruct(cache.shape, cache.dtype),
            jax.ShapeDtypeStruct(hidden.shape, hidden.dtype),
            jax.ShapeDtypeStruct(state.shape, state.dtype),
        ],
        in_specs=[pl.BlockSpec(memory_space=pltpu.SMEM)] + [hbm] * 4,
        out_specs=[hbm] * 3,
        scratch_shapes=[
            pltpu.VMEM(cache.shape, cache.dtype),
            pltpu.VMEM(inbox.shape, inbox.dtype),
            pltpu.VMEM(hidden.shape, hidden.dtype),
            pltpu.VMEM(state.shape, state.dtype),
            pltpu.SemaphoreType.DMA((4, 4)),
        ],
        compiler_params=pltpu.CompilerParams(vmem_limit_bytes=67000000),
        name="place_pages",
    )(page_home, cache, inbox, hidden, state)


def shards(
    hidden_in,
    queries,
    keyvals,
    out_weight,
    kv_gain,
    kv_weight,
    cache,
    page_home,
    cache_len,
    beam_state,
    parents,
    beam_gain,
    query_weight,
    beam_out_weight,
):
    n_tok = lax.axis_size("tokens")
    n_head = lax.axis_size("heads")
    flat_cache = cache.reshape(-1, DH)
    hidden, inbox, beams_end = whole(
        n_tok,
        n_head,
        page_home,
        cache_len,
        parents,
        queries,
        hidden_in,
        kv_gain,
        beam_state.T,
        beam_gain,
        out_weight.T,
        keyvals.reshape(-1, DH),
        kv_weight.reshape(n_head, -1, DH),
        flat_cache,
        jnp.swapaxes(beam_out_weight, 1, 2),
        query_weight,
    )
    own_pages = hidden_in.shape[0] // PAGE
    new_cache, stretch_hidden, beams_end = place_pages(
        n_tok, own_pages, page_home, flat_cache, inbox, hidden, beams_end
    )
    return (stretch_hidden, new_cache.reshape(cache.shape), beams_end.T)


def solution(mesh):
    tokens = "tokens"
    placed = (
        P(tokens, "heads"),
        P(tokens, "heads"),
        P(tokens, None, "heads"),
        P("heads", tokens),
        P("heads"),
        P(None, None, "heads"),
        P(tokens, None, "heads"),
        P(),
        P(),
        P(None, tokens),
        P(),
        P(None, tokens),
        P(None, tokens, "heads"),
        P(None, "heads", tokens),
    )
    return jax.shard_map(
        shards,
        mesh=mesh,
        in_specs=placed,
        out_specs=(P(tokens, "heads"), P(tokens, None, "heads"), P(None, tokens)),
        check_vma=False,
    )
```
